32 devices in a mesh: seq: 4 (over y, x), tp: 8 (over z, core).
Axes of the slice: x: 2, y: 2, z: 4, core: 2. Of those that a mesh axis runs over, the one named last changes fastest.
Arguments:
- hidden: bfloat16 [4096, 4096], P(('seq', 'tp')), may hold values from -6 to 6
- norm_gain: float32 [4096], replicated, may hold values from 0.5 to 1.5
- inner_weight: bfloat16 [4096, 2, 2048], P(None, None, 'tp'), may hold values from -0.09375 to 0.09375
- group_weight: bfloat16 [4096, 1024], P(None, 'tp'), may hold values from -0.09375 to 0.09375
- step_weight: bfloat16 [4096, 32], P(None, 'tp'), may hold values from -0.09375 to 0.09375
- step_bias: float32 [32], P('tp'), may hold values from -2 to 1
- decay_rate: float32 [32], P('tp'), may hold values from 0.0001 to 0.1
- filter_inner: bfloat16 [4, 2048], P(None, 'tp'), may hold values from -3 to 3
- filter_group: bfloat16 [4, 1024], P(None, 'tp'), may hold values from -3 to 3
- skip_gain: float32 [32], P('tp'), may hold values from 0.5 to 1.5
- mixer_gain: float32 [2048], P('tp'), may hold values from 0.5 to 1.5
- output_weight: bfloat16 [2048, 4096], P('tp'), may hold values from -0.125 to 0.125
- segment_ids: int32 [4096], replicated, may hold values from 0 to 3, never falling along the last dimension, each value on 1 to 2048 neighbouring positions
Outputs:
- layer_out: bfloat16 [4096, 4096], P(('seq', 'tp'))
The draws below stay inside these ranges and needn't reach their ends.
Inputs may be any that keep to these rules, and one draw needn't show every extreme that they name: `segment_ids`: ids never fall along the pack; every id names at least one token, and one request has exactly 2048 tokens.
All inputs are finite; a program needn't handle non-finite values.
Results may differ from the reference program's by a relative error of at most 0.0051.
Values may be sent and summed in bfloat16 or wider, within the bound.
A program may use at most 128 MiB of HBM per device.

```python
import math
import jax
import jax.numpy as jnp
import numpy as np
from jax import lax

D = 4096
HEAD_DIM = 64
STATE = 128
CONV = 4
REQS = 4
HEADS = 32
GROUPS = 4
INNER = 2048
TOKENS = 4096
LONGEST = 2048


def level_of(rng, shape, cuts, smallest, largest):
    level = 1.0
    for dim, shards_of in cuts:
        draws = jax.random.uniform(jax.random.fold_in(jax.random.fold_in(rng, 6), dim), (shards_of,), jnp.float32, smallest / len(cuts), largest / len(cuts))
        level = level * jnp.repeat(jnp.exp(draws), shape[dim] // shards_of).reshape((-1,) + (1,) * (len(shape) - 1 - dim))
    return level


def length_profile(amount, total, limit, slope):
    loads = [(1 << 20) // math.isqrt(standing ** slope) + 1 for standing in range(2, amount + 1)]
    surplus, given = total - limit - (amount - 1), [1] * (amount - 1)
    while surplus > 0:
        movable = [i for i in range(amount - 1) if given[i] < limit]
        mass, remaining = sum([loads[i] for i in movable]), surplus
        for i in movable:
            more = min(limit - given[i], max(1, remaining * loads[i] // mass), surplus)
            given[i] = given[i] + more
            surplus = surplus - more
    return np.array([limit] + given)


def ragged_sizes(key, amount, total, bound, slope):
    if amount == 2:
        one = jax.random.randint(key, (), max(1, total - bound), min(bound, total - 1) + 1)
        return jnp.stack([one, total - one])
    lengths = jnp.asarray(length_profile(amount, total, bound, slope), jnp.int32)
    couples = (amount - 1) // 2
    donor, sink = lengths[1:1 + 2 * couples:2], lengths[2:2 + 2 * couples:2]
    room = jnp.minimum(donor - 1, bound - sink)
    shifted = jax.random.randint(jax.random.fold_in(key, 1), (couples,), 0, 1 << 20) % (room + 1)
    lengths = lengths.at[1:1 + 2 * couples:2].set(donor - shifted).at[2:2 + 2 * couples:2].set(sink + shifted)
    return lengths[jax.random.permutation(jax.random.fold_in(key, 2), amount)]


def bell_draw(key, extent, scale, most, shards=(), dtype=jnp.bfloat16):
    result = scale * jax.random.normal(key, extent, jnp.float32)
    if shards:
        result = result * level_of(key, extent, shards, -0.22, 0.18)
    return jnp.clip(result, -most, most).astype(dtype)


def setup_inputs(seed: int = 0) -> dict:
    arg_keys = jax.random.split(jax.random.key(seed), 14)
    hidden = bell_draw(arg_keys[0], (TOKENS, D), 1.0, 6.0, ((0, 32),))
    norm_gain = jnp.clip(1.0 + 0.1 * jax.random.normal(arg_keys[1], (D,), jnp.float32), 0.5, 1.5)
    inner_weight = bell_draw(arg_keys[2], (D, 2, INNER), D ** -0.5, 0.09375, ((2, 8),))
    group_weight = bell_draw(arg_keys[3], (D, GROUPS * 2 * STATE), D ** -0.5, 0.09375, ((1, 8),))
    step_weight = bell_draw(arg_keys[4], (D, HEADS), D ** -0.5, 0.09375, ((1, 8),))
    step_bias = jnp.clip(-2.0 + 3.0 * jax.random.uniform(arg_keys[5], (HEADS,), jnp.float32) ** level_of(arg_keys[5], (HEADS,), ((0, 8),), -0.2, 0.2), -2.0, 1.0)
    decay_rate = jnp.clip(jnp.exp(math.log(0.1) - 6.9077553 * jax.random.uniform(arg_keys[6], (HEADS,), jnp.float32) ** level_of(arg_keys[6], (HEADS,), ((0, 8),), -0.2, 0.2)), 0.0001, 0.1)
    filter_inner = bell_draw(arg_keys[7], (CONV, INNER), CONV ** -0.5, 3.0, ((1, 8),))
    filter_group = bell_draw(arg_keys[8], (CONV, GROUPS * 2 * STATE), CONV ** -0.5, 3.0, ((1, 8),))
    skip_gain = jnp.clip(0.5 + 1.0 * jax.random.uniform(arg_keys[9], (HEADS,), jnp.float32) ** level_of(arg_keys[9], (HEADS,), ((0, 8),), -0.2, 0.2), 0.5, 1.5)
    mixer_gain = jnp.clip(1.0 + 0.1 * jax.random.normal(arg_keys[10], (INNER,), jnp.float32), 0.5, 1.5)
    output_weight = bell_draw(arg_keys[11], (INNER, D), INNER ** -0.5, 0.125, ((0, 8),))
    segment_ids = jnp.searchsorted(jnp.cumsum(ragged_sizes(arg_keys[12], REQS, TOKENS, LONGEST, 2)), jnp.arange(TOKENS), side="right").astype(jnp.int32)
    return dict(hidden=hidden, norm_gain=norm_gain, inner_weight=inner_weight, group_weight=group_weight, step_weight=step_weight, step_bias=step_bias, decay_rate=decay_rate, filter_inner=filter_inner, filter_group=filter_group, skip_gain=skip_gain, mixer_gain=mixer_gain, output_weight=output_weight, segment_ids=segment_ids)


EPS = 1e-05

def reference(hidden, norm_gain, inner_weight, group_weight, step_weight, step_bias, decay_rate, filter_inner, filter_group, skip_gain, mixer_gain, output_weight, segment_ids):
    hidden_f = hidden.astype(jnp.float32)
    normed = (hidden_f * lax.rsqrt(lax.optimization_barrier(jnp.mean(hidden_f * hidden_f, axis=-1, keepdims=True)) + EPS) * norm_gain).astype(jnp.bfloat16)
    gate_in = jnp.dot(normed, inner_weight.reshape(D, 2 * INNER), preferred_element_type=jnp.float32)
    gate_z = gate_in[:, :INNER]
    maps_in = jnp.dot(normed, group_weight, preferred_element_type=jnp.float32)
    step_raw = jnp.dot(normed, step_weight, preferred_element_type=jnp.float32)
    conv_in = jnp.concatenate([gate_in[:, INNER:], maps_in], axis=1)
    filters = jnp.concatenate([filter_inner, filter_group], axis=1).astype(jnp.float32)
    padded = jnp.pad(conv_in, ((CONV - 1, 0), (0, 0)))
    seg_pad = jnp.concatenate([jnp.full((CONV - 1,), -1, jnp.int32), segment_ids.astype(jnp.int32)])
    total = jnp.zeros_like(conv_in)
    for offset in range(CONV):
        same = (seg_pad[offset:offset + TOKENS] == segment_ids).astype(jnp.float32)
        total = total + filters[offset] * padded[offset:offset + TOKENS] * same[:, None]
    active = jax.nn.silu(total)
    inner_x = active[:, :INNER].reshape(TOKENS, HEADS, HEAD_DIM)
    grouped_maps = active[:, INNER:].reshape(TOKENS, GROUPS, 2, STATE)
    input_map = grouped_maps[:, :, 0]
    output_map = grouped_maps[:, :, 1]
    step = jax.nn.softplus(step_raw + step_bias)
    log_decay = -step * decay_rate
    starts = jnp.concatenate([jnp.ones((1,), jnp.bool_), segment_ids[1:] != segment_ids[:-1]])
    per_group = HEADS // GROUPS

    def advance(state, inputs):
        token_x, token_b, token_c, token_step, token_log, token_start = inputs
        keep = jnp.where(token_start, 0.0, jnp.exp(token_log))
        wide_b = jnp.repeat(token_b, per_group, axis=0)
        wide_c = jnp.repeat(token_c, per_group, axis=0)
        state = keep[:, None, None] * state + (token_step[:, None] * token_x)[:, :, None] * wide_b[:, None, :]
        read = jnp.einsum('hpn,hn->hp', state, wide_c, precision=lax.Precision.HIGHEST)
        return (state, read)
    initial = jnp.zeros((HEADS, HEAD_DIM, STATE), jnp.float32)
    _, scanned = lax.scan(advance, initial, (inner_x, input_map, output_map, step, log_decay, starts))
    ssm_out = scanned + skip_gain[None, :, None] * inner_x
    gated = ssm_out.reshape(TOKENS, INNER) * jax.nn.silu(gate_z)
    by_group = gated.reshape(TOKENS, GROUPS, INNER // GROUPS)
    scaled = by_group * lax.rsqrt(lax.optimization_barrier(jnp.mean(by_group * by_group, axis=-1, keepdims=True)) + EPS)
    mixed = (scaled.reshape(TOKENS, INNER) * mixer_gain).astype(jnp.bfloat16)
    return (hidden_f + jnp.dot(mixed, output_weight, preferred_element_type=jnp.float32)).astype(jnp.bfloat16)
```

```python
import functools
import jax
import jax.numpy as jnp
from jax import lax
from jax.experimental import pallas as pl
from jax.experimental.pallas import tpu as pltpu
from jax.sharding import PartitionSpec as P

EPS = 1e-05
LANES = 128
STRETCH = 128
HIGH = lax.Precision.HIGHEST
MESH = pl.DeviceIdType.MESH


def silu(v):
    return v / (1.0 + jnp.exp(-v))


def widen(cols, heads, head_dim):
    rows = cols.shape[0]
    parts = [jnp.broadcast_to(cols[:, h : h + 1], (rows, head_dim)) for h in range(heads)]
    return jnp.concatenate(parts, axis=1)


def dot16(a, b, dims=((1,), (0,))):
    a, b = a.astype(jnp.bfloat16), b.astype(jnp.bfloat16)
    return lax.dot_general(a, b, (dims, ((), ())), preferred_element_type=jnp.float32)


def scan_stretch(
    count, heads, head_dim, inner, states, at,
    proj, aux, row_seg, taps, bias, rate, skip, y_out, c_out, w_out, edge, state, total,
):
    conv = inner + 2 * states
    cur = proj[at, :conv]
    both = jnp.concatenate([edge[...], cur], axis=0)
    edge[...] = cur[STRETCH - 8 :]
    size = STRETCH
    tap = taps[...]
    acc = tap[count - 1 : count] * cur
    for back in range(1, count):
        same = aux[at, back : back + 1]
        acc += tap[count - 1 - back : count - back] * both[8 - back : 8 - back + size] * same
    active = silu(acc)
    x = active[:, :inner]
    b_map = active[:, inner : inner + states]
    c_map = active[:, inner + states :]
    raw = proj[at, conv + inner :] + bias[...]
    step = jnp.maximum(raw, 0.0) + jnp.log1p(jnp.exp(-jnp.abs(raw)))
    log_decay = -step * rate[...]
    row_at = lax.broadcasted_iota(jnp.int32, (size, size), 0)
    col_at = lax.broadcasted_iota(jnp.int32, (size, size), 1)
    causal = row_at >= col_at
    cum = jnp.dot(
        causal.astype(jnp.float32), log_decay, precision=HIGH, preferred_element_type=jnp.float32
    )
    cum_rows = cum.T
    alive, in_last, alive_span = aux[at, 4:5], aux[at, 5:6], aux[at, 6:7]
    last = cum[size - 1 :]
    mask = causal & (aux[at, 0:1] == row_seg[0:1, at])
    xs = x * widen(step, heads, head_dim)
    xs16 = xs.astype(jnp.bfloat16)
    products = dot16(c_map, b_map, ((1,), (1,)))
    parts = []
    for h in range(heads):
        gap = cum[:, h : h + 1] - cum_rows[h : h + 1, :]
        mixing = products * jnp.exp(jnp.where(mask, gap, -1e30))
        parts.append(dot16(mixing, xs16[:, h * head_dim : (h + 1) * head_dim]))
    local = jnp.concatenate(parts, axis=1)
    entry = jnp.exp(cum) * alive
    carried = dot16(c_map, state[...]) * widen(entry, heads, head_dim)
    y_out[at, :] = local + carried + skip[...] * x
    c_out[at, :] = c_map.astype(jnp.bfloat16)
    w_span = jnp.exp(cum + total[...]) * alive_span
    w_out[at, :] = w_span
    end = jnp.exp(last - cum) * in_last
    fresh = dot16(b_map, xs * widen(end, heads, head_dim), ((0,), (0,)))
    state[...] = widen(entry[size - 1 :], heads, head_dim) * state[...] + fresh
    total[...] = total[...] + last


def servers_of(chips):
    return [2 * i + 1 - i % 2 for i in range(chips // 2)]


def mixer_kernel(
    n, spans, ns, heads, count,
    hidden, gain, inner, group, step, wout, aux, row_seg, taps_inner, taps_group, bias, rate, skip, mixer_gain,
    out,
    buf, mytail, tail, raw, gbuf, gtaps, taps, w, proj, edge, wq,
    y, c_maps, w_span, state, total, packed, decay, came, came_decay,
    sq, mixed, taken, results, landed,
    rsend, lsend, xsend, rrecv, lrecv, xrecv,
    tsend, trecv, gsend, grecv, wsend, wrecv, qsend, qrecv, local,
    ssend, srecv, esend, erecv, msend, mrecv, nsend, nrecv, osend, orecv,
):
    tp, seq = lax.axis_index("tp"), lax.axis_index("seq")
    c, k = tp // 2, tp % 2
    rows, width = hidden.shape
    dc = width // ns
    sib = {"tp": tp + 1 - 2 * k}
    has_left, has_right = c > 0, c < n - 1
    inner_dev = w.shape[1] - 3 * LANES
    half_cols = inner_dev // 2
    servers = servers_of(n)
    serving = functools.reduce(jnp.logical_or, [c == s for s in servers])
    bits = spans.bit_length() - 1
    half = wout.shape[1] // 2
    quarter = half // spans

    def copy(src, dst, send, recv, dev):
        return pltpu.make_async_remote_copy(
            src_ref=src, dst_ref=dst, send_sem=send, recv_sem=recv, device_id=dev, device_id_type=MESH
        )

    inner_in = pltpu.make_async_copy(inner, raw, local.at[0])
    group_in = pltpu.make_async_copy(group, gbuf.at[k], local.at[1])

    def half_cols_at(core, span):
        return pl.ds(pl.multiple_of(core * half + span * quarter, LANES), quarter)

    own_half = [
        pltpu.make_async_copy(wout.at[:, half_cols_at(k, e)], wq.at[tp, e], wsend.at[0, e])
        for e in range(spans)
    ]
    inner_in.start()
    group_in.start()

    @pl.when(serving)
    def _():
        for part in own_half:
            part.start()

    barrier = pltpu.get_barrier_semaphore()
    peers = 2 * n

    def greet(axis, size, me):
        def hello(i, carry):
            pl.semaphore_signal(
                barrier, inc=1, device_id={axis: lax.rem(me + i, size)}, device_id_type=MESH
            )
            return carry
        lax.fori_loop(1, size, hello, 0)

    greet("tp", peers, tp)
    greet("seq", spans, seq)

    h = hidden[...].astype(jnp.float32)
    scale = lax.rsqrt(jnp.mean(h * h, axis=1, keepdims=True) + EPS)
    for s in range(ns):
        part = slice(s * dc, (s + 1) * dc)
        normed = (hidden[:, part].astype(jnp.float32) * scale * gain[:, part]).astype(jnp.bfloat16)
        buf[c, k, s] = normed
        mytail[:, part] = normed[rows - 16 :]
    pl.semaphore_wait(barrier, peers - 1 + spans - 1)

    def to_right(j, s):
        return copy(buf.at[j, k, s], buf.at[j, k, s], rsend.at[j, s], rrecv.at[j, s], {"tp": lax.rem(tp + 2, peers)})

    def to_left(j, s):
        return copy(buf.at[j, k, s], buf.at[j, k, s], lsend.at[j, s], lrecv.at[j, s], {"tp": lax.rem(tp + peers - 2, peers)})

    def to_sib(j, s):
        return copy(buf.at[j, k, s], buf.at[j, k, s], xsend.at[j, s], xrecv.at[j, s], sib)

    def from_sib(j, s):
        return copy(buf.at[j, 1 - k, s], buf.at[j, 1 - k, s], xsend.at[j, s], xrecv.at[j, s], sib)

    def own(s, carry):
        @pl.when(has_right)
        def _():
            to_right(c, s).start()

        @pl.when(has_left)
        def _():
            to_left(c, s).start()

        to_sib(c, s).start()
        return carry

    def w_far(m, core):
        return copy(
            wout.at[:, half_cols_at(core, seq)], wq.at[tp, seq],
            wsend.at[1 + m, core], wrecv.at[tp], {"tp": 2 * servers[m] + core},
        )

    other = tp + 1 - 2 * k
    w_near = [
        copy(wout.at[:, half_cols_at(1 - k, e)], wq.at[tp, e], wsend.at[1 + len(servers), e], wrecv.at[tp], sib)
        for e in range(spans)
    ]
    near_in = copy(wq.at[other], wq.at[other], wsend.at[0, 0], wrecv.at[other], sib)

    def w_send(m, core):
        @pl.when(c != servers[m])
        def _():
            w_far(m, core).start()

    sends = [(m, core) for m in range(len(servers)) for core in range(2)]
    for m, core in sends:
        w_send(m, core)

    lax.fori_loop(0, ns, own, 0)

    last = peers - 1
    has_tail = seq > 0
    tail_next = copy(mytail, tail, tsend.at[0], trecv.at[0], {"seq": lax.rem(seq + 1, spans)})
    tail_left = copy(tail, tail, tsend.at[1], trecv.at[0], {"tp": lax.rem(tp + peers - 2, peers)})
    tail_sib = copy(tail, tail, tsend.at[2], trecv.at[0], sib)

    @pl.when((tp == last) & (seq < spans - 1))
    def _():
        tail_next.start()

    group_out = copy(group, gbuf.at[k], gsend.at[0], grecv.at[0], sib)
    group_out.start()
    gtaps[k] = taps_group[...]
    taps_out = copy(gtaps.at[k], gtaps.at[k], gsend.at[1], grecv.at[1], sib)
    taps_out.start()

    @pl.when(serving)
    def _():
        for part in w_near:
            part.start()

    def far_block(m):
        return lax.rem(2 * c + 2 + m, peers)

    def wq_part(j, span):
        return wq.at[j, span]

    def q_copy(j, origin, b):
        return copy(
            wq_part(j, origin), wq_part(j, origin), qsend.at[j, origin, b], qrecv.at[j, origin],
            {"seq": seq ^ (1 << b)},
        )

    def q_spread(m):
        j = far_block(m)
        copy(wq_part(j, seq), wq_part(j, seq), wsend.at[0, 0], wrecv.at[j], sib).wait_recv()
        for b in range(bits):
            q_copy(j, seq, b).start()

    def q_forwards(up):
        found = []
        for e in range(1, spans):
            top, low = e.bit_length() - 1, (e & -e).bit_length() - 1
            targets = [b for b in range(bits) if (b > top if up else b < low)]
            found.append((e, targets))
        return found

    def q_forward(m, relay=True):
        j = far_block(m)
        for up in (True, False):
            @pl.when(j % 2 == (0 if up else 1))
            def _():
                for e, targets in q_forwards(up):
                    if bool(targets) == relay:
                        origin = seq ^ e
                        part = wq_part(j, origin)
                        copy(part, part, wsend.at[0, 0], qrecv.at[j, origin], sib).wait_recv()
                        for b in targets:
                            q_copy(j, origin, b).start()

    def q_drain(m):
        j = far_block(m)
        for b in range(bits):
            q_copy(j, seq, b).wait_send()
        for up in (True, False):
            @pl.when(j % 2 == (0 if up else 1))
            def _():
                for e, targets in q_forwards(up):
                    for b in targets:
                        q_copy(j, seq ^ e, b).wait_send()

    inner_in.wait()
    lane_tiles = inner_dev // 2 // LANES
    size = 256
    depth = size // (2 * lane_tiles)
    row_at = lax.broadcasted_iota(jnp.int32, (size, size), 0)
    col_at = lax.broadcasted_iota(jnp.int32, (size, size), 1)
    kk, jj, tt = row_at % depth, row_at // (depth * lane_tiles), row_at // depth % lane_tiles
    perm = (col_at == kk * (2 * lane_tiles) + tt * 2 + jj).astype(jnp.float32).astype(jnp.bfloat16)
    gate_at = half_cols + 2 * LANES

    def sort(i, carry):
        block = raw[pl.ds(pl.multiple_of(i * size, size), size), :]
        out = jnp.dot(perm, block, preferred_element_type=jnp.float32).astype(jnp.bfloat16)
        at = pl.ds(pl.multiple_of(i * depth, depth), depth)
        for t in range(lane_tiles):
            w[at, gate_at + t * LANES : gate_at + (t + 1) * LANES] = out[t * depth : (t + 1) * depth]
            scan = out[(lane_tiles + t) * depth : (lane_tiles + t + 1) * depth]
            w[at, t * LANES : (t + 1) * LANES] = scan
        return carry

    lax.fori_loop(0, raw.shape[0] // size, sort, 0)
    eye = (row_at == col_at).astype(jnp.float32).astype(jnp.bfloat16)

    def turn(i, carry):
        at = pl.ds(pl.multiple_of(i * size, size), size)
        block = step[:, at]
        block = jnp.concatenate([block, jnp.zeros((LANES - block.shape[0], size), block.dtype)], axis=0)
        out = lax.dot_general(eye, block, (((1,), (1,)), ((), ())), preferred_element_type=jnp.float32)
        w[at, gate_at + half_cols :] = out.astype(jnp.bfloat16)
        return carry

    lax.fori_loop(0, width // size, turn, 0)
    group_in.wait()
    copy(gbuf.at[1 - k], gbuf.at[1 - k], gsend.at[0], grecv.at[0], sib).wait_recv()
    copy(gtaps.at[1 - k], gtaps.at[1 - k], gsend.at[1], grecv.at[1], sib).wait_recv()
    taps[:, :half_cols] = taps_inner[...]
    for m in range(2):
        w[:, half_cols + m * LANES : half_cols + (m + 1) * LANES] = gbuf[m]
        taps[:, half_cols + m * LANES : half_cols + (m + 1) * LANES] = gtaps[m]

    def arrivals(i):
        d, s = i // ns, i % ns

        @pl.when(c - d >= 0)
        def _():
            j = c - d
            copy(buf.at[j, k, s], buf.at[j, k, s], rsend.at[j, s], rrecv.at[j, s], sib).wait_recv()

            @pl.when(has_right)
            def _():
                to_right(j, s).start()

            to_sib(j, s).start()

        @pl.when(c + d < n)
        def _():
            j = c + d
            copy(buf.at[j, k, s], buf.at[j, k, s], lsend.at[j, s], lrecv.at[j, s], sib).wait_recv()

            @pl.when(has_left)
            def _():
                to_left(j, s).start()

            to_sib(j, s).start()

    def compute(i):
        d, s = i // ns, i % ns

        def side(which, carry):
            j = c - d + 2 * d * which

            @pl.when((j >= 0) & (j < n) & ((which == 0) | (d > 0)))
            def _():
                from_sib(j, s).wait_recv()
                x = buf[j, :, s].reshape(2 * rows, dc)
                at = pl.ds(pl.multiple_of(s * dc, dc), dc)
                out = jnp.dot(x, w[at, :], preferred_element_type=jnp.float32)
                place = pl.ds(pl.multiple_of(j * 2 * rows, 2 * rows), 2 * rows)

                @pl.when(s == 0)
                def _():
                    proj[place, :] = out

                @pl.when(s > 0)
                def _():
                    proj[place, :] += out

            return carry

        lax.fori_loop(0, 2, side, 0)

    far = peers - 2
    first_spread, first_forward = ns, ns + far

    def item(i, carry):
        @pl.when((i >= ns) & (i < n * ns))
        def _():
            arrivals(i)

        @pl.when((i == ns + 1) & has_tail & (k == 1))
        def _():
            copy(tail, tail, tsend.at[1], trecv.at[0], sib).wait_recv()

            @pl.when(has_left)
            def _():
                tail_left.start()

            tail_sib.start()

        compute(i - 1)

        @pl.when(serving & (i >= first_spread) & (i < first_spread + far))
        def _():
            q_spread(i - first_spread)

        @pl.when(serving & (i >= first_forward) & (i < first_forward + far))
        def _():
            q_forward(i - first_forward)

        return carry

    lax.fori_loop(1, n * ns + 1, item, 0)

    conv = half_cols + 2 * LANES

    @pl.when(has_tail)
    def _():
        @pl.when(k == 0)
        def _():
            copy(tail, tail, tsend.at[1], trecv.at[0], sib).wait_recv()

        edge[...] = jnp.dot(tail[...], w[:, :conv], preferred_element_type=jnp.float32)[8:]

    @pl.when(jnp.logical_not(has_tail))
    def _():
        edge[...] = jnp.zeros_like(edge)

    inner_own = half_cols
    head_dim = inner_own // heads
    states = LANES
    length = peers * rows
    state[...] = jnp.zeros_like(state)
    total[...] = jnp.zeros_like(total)

    def stretch(i, carry):
        at = pl.ds(pl.multiple_of(i * STRETCH, STRETCH), STRETCH)
        scan_stretch(
            count, heads, head_dim, inner_own, states, at,
            proj, aux, row_seg, taps, bias, rate, skip, y, c_maps, w_span, edge, state, total,
        )
        return carry

    lax.fori_loop(0, length // STRETCH, stretch, 0)

    packed[...] = state[...].astype(jnp.bfloat16)
    decay[...] = jnp.broadcast_to(
        widen(w_span[length - 8 :, :], heads, head_dim)[7:8], decay.shape
    )

    def state_to(e):
        dev = {"seq": lax.rem(seq + e, spans)}
        return (
            copy(packed, came.at[e], ssend.at[0, e], srecv.at[0, e], dev),
            copy(decay, came_decay.at[e], ssend.at[1, e], srecv.at[1, e], dev),
        )

    for e in range(1, spans):
        @pl.when(seq + e < spans)
        def _():
            for part in state_to(e):
                part.start()

    state[...] = jnp.zeros_like(state)
    for e in range(spans - 1, 0, -1):
        @pl.when(e <= seq)
        def _():
            for part in state_to(e):
                part.wait_recv()
            state[...] = came[e].astype(jnp.float32) + came_decay[e, 0:1] * state[...]

    block = 2 * rows
    pairs = n // 2

    def chip_at(i):
        m = lax.rem(i, pairs)
        first = i < pairs
        return jnp.where(first, 2 * m + m % 2, 2 * m + 1 - m % 2)

    def rows_of(chip):
        return pl.ds(pl.multiple_of(chip * block, block), block)

    def sq_copy(chip):
        return copy(sq.at[0, chip], sq.at[1, chip], esend.at[chip], erecv.at[chip], sib)

    def gate_block(i, carry):
        chip = chip_at(i)
        at = rows_of(chip)
        entering = dot16(c_maps[at, :], state[...]) * widen(w_span[at, :], heads, head_dim)
        gated = (y[at, :] + entering) * silu(proj[at, conv : conv + inner_own])
        y[at, :] = gated
        sums = jnp.sum(gated * gated, axis=1, keepdims=True)
        sq[0, chip] = jnp.broadcast_to(sums, (block, LANES))
        sq_copy(chip).start()
        return carry

    lax.fori_loop(0, n, gate_block, 0)

    def server_of(chip):
        m = chip // 2
        return 2 * m + 1 - m % 2

    def slot_of(chip):
        return jnp.where(chip == server_of(chip), 1, 0)

    def mixed_far(chip):
        return copy(
            mixed.at[chip], taken.at[slot_of(chip), tp], msend.at[chip], mrecv.at[slot_of(chip), c],
            {"tp": lax.rem(2 * server_of(chip) + k, peers)},
        )

    def mixed_near(slot, src):
        place = taken.at[slot, 2 * src + k]
        return copy(place, place, nsend.at[slot, src], nrecv.at[slot, src], sib)

    def mix_block(i, carry):
        chip = chip_at(i)
        at = rows_of(chip)
        sq_copy(chip).wait_recv()
        mean = (sq[0, chip] + sq[1, chip]) / (2 * inner_own)
        factor = lax.rsqrt(mean + EPS)
        wide = jnp.concatenate([factor] * (inner_own // LANES), axis=1)
        done = (y[at, :] * wide * mixer_gain[...]).astype(jnp.bfloat16)

        @pl.when(c != server_of(chip))
        def _():
            mixed[chip] = done
            mixed_far(chip).start()

        @pl.when(c == server_of(chip))
        def _():
            taken[slot_of(chip), tp] = done
            mixed_near(slot_of(chip), c).start()

        return carry

    lax.fori_loop(0, n, mix_block, 0)

    mate = jnp.where(c == 2 * (c // 2), c + 1, c - 1)

    def result_far(q, core):
        return copy(
            results.at[0, q, pl.ds(core * rows, rows)], landed.at[k, q], osend.at[q, core], orecv.at[k, q],
            {"tp": 2 * mate + core},
        )

    def result_near(q):
        return copy(
            results.at[1, q, pl.ds(pl.multiple_of((1 - k) * rows, rows), rows)], landed.at[k, q],
            osend.at[q, 2], orecv.at[k, q], sib,
        )

    @pl.when(serving)
    def _():
        def rest_spread(m, carry):
            q_spread(m)
            return carry

        def rest_forward(m, carry):
            q_forward(m)
            return carry

        lax.fori_loop(min(far, n * ns + 1 - first_spread), far, rest_spread, 0)
        lax.fori_loop(min(far, n * ns + 1 - first_forward), far, rest_forward, 0)
        for e in range(spans):
            own_half[e].wait()
        near_in.wait_recv()

        def far_done(m, carry):
            q_forward(m, False)
            return carry

        lax.fori_loop(0, far, far_done, 0)

        def collect(slot):
            def relay(m, carry):
                src = lax.rem(c + m, n)
                place = taken.at[slot, 2 * src + k]
                copy(place, place, nsend.at[slot, src], mrecv.at[slot, src], sib).wait_recv()
                mixed_near(slot, src).start()
                return carry

            lax.fori_loop(1, n, relay, 0)

            def from_near(src, carry):
                place = taken.at[slot, 2 * src + 1 - k]
                copy(place, place, nsend.at[slot, src], nrecv.at[slot, src], sib).wait_recv()
                return carry

            lax.fori_loop(0, n, from_near, 0)

        def multiply(slot, q):
            sums = jnp.zeros((block, wq.shape[3]), jnp.float32)
            for j in range(peers):
                sums += jnp.dot(taken[slot, j], wq[j, q], preferred_element_type=jnp.float32)
            return sums.astype(jnp.bfloat16)

        collect(0)

        def for_mate(q, carry):
            results[0, q] = multiply(0, q)
            for core in range(2):
                result_far(q, core).start()
            return carry

        lax.fori_loop(0, spans, for_mate, 0)
        collect(1)

        def for_own(q, carry):
            results[1, q] = multiply(1, q)
            result_near(q).start()
            landed[k, q] = results[1, q, pl.ds(pl.multiple_of(k * rows, rows), rows)]
            return carry

        lax.fori_loop(0, spans, for_own, 0)

    def finish(core, q):
        place = landed.at[core, q]
        arrival = copy(place, place, osend.at[q, 0], orecv.at[core, q], sib)

        @pl.when(jnp.logical_not(serving) | (k != core))
        def _():
            arrival.wait_recv()

        at = pl.ds(core * half + q * quarter, quarter)
        out[:, at] = (hidden[:, at].astype(jnp.float32) + landed[core, q].astype(jnp.float32)).astype(jnp.bfloat16)

    for q in range(spans):
        for core in range(2):
            finish(core, q)

    def drain(i, carry):
        j, s = i // ns, i % ns
        to_sib(j, s).wait_send()

        @pl.when(has_right & (j <= c))
        def _():
            to_right(j, s).wait_send()

        @pl.when(has_left & (j >= c))
        def _():
            to_left(j, s).wait_send()

        return carry

    lax.fori_loop(0, n * ns, drain, 0)
    group_out.wait_send()
    taps_out.wait_send()

    @pl.when((tp == last) & (seq < spans - 1))
    def _():
        tail_next.wait_send()

    @pl.when(has_tail & (k == 1))
    def _():
        @pl.when(has_left)
        def _():
            tail_left.wait_send()

        tail_sib.wait_send()

    for m, core in sends:
        @pl.when(c != servers[m])
        def _():
            w_far(m, core).wait_send()

    for e in range(1, spans):
        @pl.when(seq + e < spans)
        def _():
            for part in state_to(e):
                part.wait_send()

    def sums_left(chip, carry):
        sq_copy(chip).wait_send()

        @pl.when(c != server_of(chip))
        def _():
            mixed_far(chip).wait_send()

        return carry

    lax.fori_loop(0, n, sums_left, 0)

    @pl.when(serving)
    def _():
        for e in range(spans):
            w_near[e].wait_send()

        def far_left(m, carry):
            q_drain(m)
            return carry

        lax.fori_loop(0, far, far_left, 0)

        def near_left(src, carry):
            for slot in range(2):
                mixed_near(slot, src).wait_send()
            return carry

        lax.fori_loop(0, n, near_left, 0)

        def results_left(q, carry):
            for core in range(2):
                result_far(q, core).wait_send()
            result_near(q).wait_send()
            return carry

        lax.fori_loop(0, spans, results_left, 0)


def mixer(hidden, gain, inner, group, step, wout, aux, row_seg, taps_inner, taps_group, bias, rate, skip, mixer_gain, heads, count, n, spans, ns):
    rows, width = hidden.shape
    inner_dev = inner.shape[0] * inner.shape[1] // width
    own = inner_dev // 2
    cols = inner_dev + 3 * LANES
    half = wout.shape[1] // 2
    length = 2 * n * rows
    vmem = pl.BlockSpec(memory_space=pltpu.VMEM)
    anywhere = pl.BlockSpec(memory_space=pl.ANY)
    dma = pltpu.SemaphoreType.DMA
    bits = max(1, spans.bit_length() - 1)
    bf16, f32 = jnp.bfloat16, jnp.float32
    return pl.pallas_call(
        functools.partial(mixer_kernel, n, spans, ns, heads, count),
        out_shape=jax.ShapeDtypeStruct(hidden.shape, bf16),
        in_specs=[vmem, vmem, anywhere, anywhere, vmem, anywhere] + [vmem] * 8,
        out_specs=vmem,
        scratch_shapes=[
            pltpu.VMEM((n, 2, ns, rows, width // ns), bf16),
            pltpu.VMEM((16, width), bf16),
            pltpu.VMEM((16, width), bf16),
            pltpu.VMEM(inner.shape, bf16),
            pltpu.VMEM((2,) + group.shape, bf16),
            pltpu.VMEM((2, 8, LANES), f32),
            pltpu.VMEM((8, own + 2 * LANES), f32),
            pltpu.VMEM((width, cols), bf16),
            pltpu.VMEM((length, cols), f32),
            pltpu.VMEM((8, own + 2 * LANES), f32),
            pltpu.VMEM((2 * n, spans, wout.shape[0], half // spans), bf16),
            pltpu.VMEM((length, own), f32),
            pltpu.VMEM((length, LANES), bf16),
            pltpu.VMEM((length, LANES), f32),
            pltpu.VMEM((LANES, own), f32),
            pltpu.VMEM((1, LANES), f32),
            pltpu.VMEM((LANES, own), bf16),
            pltpu.VMEM((8, own), f32),
            pltpu.VMEM((spans, LANES, own), bf16),
            pltpu.VMEM((spans, 8, own), f32),
            pltpu.VMEM((2, n, 2 * rows, LANES), f32),
            pltpu.VMEM((n, 2 * rows, own), bf16),
            pltpu.VMEM((2, 2 * n, 2 * rows, own), bf16),
            pltpu.VMEM((2, spans, 2 * rows, half // spans), bf16),
            pltpu.VMEM((2, spans, rows, half // spans), bf16),
            dma((n, ns)), dma((n, ns)), dma((n, ns)), dma((n, ns)), dma((n, ns)), dma((n, ns)),
            dma((3,)), dma((1,)), dma((2,)), dma((2,)),
            dma((2 + n // 2, max(2, spans))), dma((2 * n,)), dma((2 * n, spans, bits)), dma((2 * n, spans)), dma((3,)),
            dma((2, spans)), dma((2, spans)), dma((n,)), dma((n,)),
            dma((n,)), dma((2, n)), dma((2, n)), dma((2, n)), dma((spans, 3)), dma((2, spans)),
        ],
        compiler_params=pltpu.CompilerParams(
            collective_id=0, has_side_effects=True, vmem_limit_bytes=60 << 20
        ),
        cost_estimate=pl.CostEstimate(
            flops=24_000_000_000, bytes_accessed=12_000_000, transcendentals=4_000_000
        ),
        name="mixer",
    )(hidden, gain, inner, group, step, wout, aux, row_seg, taps_inner, taps_group, bias, rate, skip, mixer_gain)


def by_row(weight):
    width, pair, cols = weight.shape
    tiles = cols // LANES
    return weight.reshape(width, pair, tiles, LANES).transpose(0, 2, 1, 3).reshape(-1, LANES)


def body(
    hidden,
    norm_gain,
    inner_weight,
    group_weight,
    step_weight,
    step_bias,
    decay_rate,
    filter_inner,
    filter_group,
    skip_gain,
    mixer_gain,
    output_weight,
    segment_ids,
):
    rows = hidden.shape[0]
    length = rows * lax.axis_size("tp")
    inner_dev = inner_weight.shape[2]
    heads_dev = step_weight.shape[1]
    head_dim = inner_dev // heads_dev
    taps = filter_inner.shape[0]
    first_row = lax.axis_index("seq") * length
    pad_heads = ((0, 0), (0, LANES - heads_dev))
    spans, chips = lax.axis_size("seq"), lax.axis_size("tp") // 2
    pad_taps = ((0, 8 - taps), (0, 0))
    taps_inner = jnp.pad(filter_inner.astype(jnp.float32), pad_taps)
    taps_group = jnp.pad(filter_group.astype(jnp.float32), pad_taps)
    seg_pad = jnp.concatenate([jnp.full((taps - 1,), -1, jnp.int32), segment_ids])
    seg_ext = lax.dynamic_slice_in_dim(seg_pad, first_row, length + taps - 1)
    seg = seg_ext[taps - 1 :]
    span_before = seg_ext[taps - 2]
    chunked = seg.reshape(-1, STRETCH)
    chunk_before = jnp.concatenate([span_before[None], chunked[:-1, -1]])
    columns = [seg]
    columns += [seg == seg_ext[taps - 1 - back : taps - 1 - back + length] for back in range(1, taps)]
    columns += [
        (chunked == chunk_before[:, None]).reshape(-1),
        (chunked == chunked[:, -1:]).reshape(-1),
        seg == span_before,
    ]
    columns += [jnp.zeros_like(seg)] * (8 - len(columns))
    row_form = jnp.stack([column.astype(jnp.float32) for column in columns])
    row_seg = row_form
    aux = row_form.T
    bias = jnp.pad(step_bias[None], pad_heads)
    rate = jnp.pad(decay_rate[None], pad_heads)
    skip = jnp.repeat(skip_gain, head_dim)[None]
    step = jnp.pad(step_weight.T, ((0, 16 - heads_dev), (0, 0)))
    return mixer(
        hidden, norm_gain[None], by_row(inner_weight), group_weight, step, output_weight,
        aux, row_seg, taps_inner, taps_group, bias, rate, skip, mixer_gain[None], heads_dev, taps, chips, spans, 4,
    )


def solution(mesh):
    in_specs = (
        P(("seq", "tp"), None),
        P(),
        P(None, None, "tp"),
        P(None, "tp"),
        P(None, "tp"),
        P("tp"),
        P("tp"),
        P(None, "tp"),
        P(None, "tp"),
        P("tp"),
        P("tp"),
        P("tp", None),
        P(),
    )
    out_specs = P(("seq", "tp"), None)
    return jax.shard_map(body, mesh=mesh, in_specs=in_specs, out_specs=out_specs, check_vma=False)
```

```python
import functools
import jax
import jax.numpy as jnp
from jax import lax
from jax.experimental import pallas as pl
from jax.experimental.pallas import tpu as pltpu
from jax.sharding import PartitionSpec as P

EPS = 1e-05
LANES = 128
STRETCH = 128
HIGH = lax.Precision.HIGHEST
MESH = pl.DeviceIdType.MESH


def silu(v):
    return v / (1.0 + jnp.exp(-v))


def widen(cols, heads, head_dim):
    rows = cols.shape[0]
    parts = [jnp.broadcast_to(cols[:, h : h + 1], (rows, head_dim)) for h in range(heads)]
    return jnp.concatenate(parts, axis=1)


def dot16(a, b, dims=((1,), (0,))):
    a, b = a.astype(jnp.bfloat16), b.astype(jnp.bfloat16)
    return lax.dot_general(a, b, (dims, ((), ())), preferred_element_type=jnp.float32)


def segment_marks(segments, first, i):
    shape = (8, STRETCH)

    def line(at):
        ids = segments[pl.ds(jnp.maximum(at, 0), 1), :].astype(jnp.float32)
        return jnp.broadcast_to(jnp.where(at >= 0, ids, -1.0), shape)

    now, past, span_past = line(first + i), line(first + i - 1), line(first - 1)
    lane = lax.broadcasted_iota(jnp.int32, shape, 1)
    row = lax.broadcasted_iota(jnp.int32, shape, 0)
    end = slice(STRETCH - 1, STRETCH)
    marks = now
    for back in range(1, 4):
        other = jnp.where(lane < back, pltpu.roll(past, back, 1), pltpu.roll(now, back, 1))
        marks = jnp.where(row == back, (now == other).astype(jnp.float32), marks)
    for at, other in ((4, past[:, end]), (5, now[:, end]), (6, span_past[:, end])):
        marks = jnp.where(row == at, (now == other).astype(jnp.float32), marks)
    return marks.T, now[0:1]


def head_line(values, heads, width, reach):
    lane = lax.broadcasted_iota(jnp.int32, (1, width), 1)
    line = jnp.zeros((1, width), jnp.float32)
    for h in range(heads):
        line = jnp.where((lane >= h * reach) & (lane < (h + 1) * reach), values[h], line)
    return line


def flat(ref):
    return jnp.concatenate([ref[i : i + 1, :] for i in range(ref.shape[0])], axis=1)


def scan_stretch(
    count, heads, head_dim, inner, states, at,
    proj, segments, first, i, taps, bias, rate, skip, y_out, c_out, w_out, edge, state, total,
):
    aux, row_seg = segment_marks(segments, first, i)
    conv = inner + 2 * states
    cur = proj[at, :conv]
    both = jnp.concatenate([edge[...], cur], axis=0)
    edge[...] = cur[STRETCH - 8 :]
    size = STRETCH
    tap = taps[...]
    acc = tap[count - 1 : count] * cur
    for back in range(1, count):
        same = aux[:, back : back + 1]
        acc += tap[count - 1 - back : count - back] * both[8 - back : 8 - back + size] * same
    active = silu(acc)
    x = active[:, :inner]
    b_map = active[:, inner : inner + states]
    c_map = active[:, inner + states :]
    raw = proj[at, conv + inner :] + bias
    step = jnp.maximum(raw, 0.0) + jnp.log1p(jnp.exp(-jnp.abs(raw)))
    log_decay = -step * rate
    row_at = lax.broadcasted_iota(jnp.int32, (size, size), 0)
    col_at = lax.broadcasted_iota(jnp.int32, (size, size), 1)
    causal = row_at >= col_at
    cum = jnp.dot(
        causal.astype(jnp.float32), log_decay, precision=HIGH, preferred_element_type=jnp.float32
    )
    cum_rows = cum.T
    alive, in_last, alive_span = aux[:, 4:5], aux[:, 5:6], aux[:, 6:7]
    last = cum[size - 1 :]
    mask = causal & (aux[:, 0:1] == row_seg)
    xs = x * widen(step, heads, head_dim)
    xs16 = xs.astype(jnp.bfloat16)
    products = dot16(c_map, b_map, ((1,), (1,)))
    parts = []
    for h in range(heads):
        gap = cum[:, h : h + 1] - cum_rows[h : h + 1, :]
        mixing = products * jnp.exp(jnp.where(mask, gap, -1e30))
        parts.append(dot16(mixing, xs16[:, h * head_dim : (h + 1) * head_dim]))
    local = jnp.concatenate(parts, axis=1)
    entry = jnp.exp(cum) * alive
    carried = dot16(c_map, state[...]) * widen(entry, heads, head_dim)
    y_out[at, :] = local + carried + skip * x
    c_out[at, :] = c_map.astype(jnp.bfloat16)
    w_span = jnp.exp(cum + total[...]) * alive_span
    w_out[at, :] = w_span
    end = jnp.exp(last - cum) * in_last
    fresh = dot16(b_map, xs * widen(end, heads, head_dim), ((0,), (0,)))
    state[...] = widen(entry[size - 1 :], heads, head_dim) * state[...] + fresh
    total[...] = total[...] + last


def servers_of(chips):
    return [2 * i + 1 - i % 2 for i in range(chips // 2)]


def mixer_kernel(
    n, spans, ns, heads, count,
    hidden, gain, inner, group, step, wout, segments, taps_inner, taps_group, bias, rate, skip, mixer_gain,
    out,
    buf, mytail, tail, raw, gbuf, gtaps, taps, w, proj, edge, wq,
    y, c_maps, w_span, state, total, packed, decay, came, came_decay,
    sq, mixed, taken, results, landed,
    rsend, lsend, xsend, rrecv, lrecv, xrecv,
    tsend, trecv, gsend, grecv, wsend, wrecv, qsend, qrecv, local,
    ssend, srecv, esend, erecv, msend, mrecv, nsend, nrecv, osend, orecv,
):
    tp, seq = lax.axis_index("tp"), lax.axis_index("seq")
    c, k = tp // 2, tp % 2
    rows, width = hidden.shape
    dc = width // ns
    sib = {"tp": tp + 1 - 2 * k}
    has_left, has_right = c > 0, c < n - 1
    inner_dev = w.shape[1] - 3 * LANES
    half_cols = inner_dev // 2
    servers = servers_of(n)
    mate = jnp.where(c == 2 * (c // 2), c + 1, c - 1)
    serving = functools.reduce(jnp.logical_or, [c == s for s in servers])
    bits = spans.bit_length() - 1
    half = wout.shape[1] // 2
    quarter = half // spans

    def copy(src, dst, send, recv, dev):
        return pltpu.make_async_remote_copy(
            src_ref=src, dst_ref=dst, send_sem=send, recv_sem=recv, device_id=dev, device_id_type=MESH
        )

    inner_in = pltpu.make_async_copy(inner, raw, local.at[0])
    group_in = pltpu.make_async_copy(group, gbuf.at[k], local.at[1])

    def half_cols_at(core, span):
        return pl.ds(pl.multiple_of(core * half + span * quarter, LANES), quarter)

    own_half = [
        pltpu.make_async_copy(wout.at[:, half_cols_at(k, e)], wq.at[tp, e], wsend.at[0, e])
        for e in range(spans)
    ]
    inner_in.start()
    group_in.start()

    @pl.when(serving)
    def _():
        for part in own_half:
            part.start()

    barrier = pltpu.get_barrier_semaphore()
    peers = 2 * n

    def greet(axis, size, me):
        def hello(i, carry):
            pl.semaphore_signal(
                barrier, inc=1, device_id={axis: lax.rem(me + i, size)}, device_id_type=MESH
            )
            return carry
        lax.fori_loop(1, size, hello, 0)

    greet("tp", peers, tp)
    greet("seq", spans, seq)

    h = hidden[...].astype(jnp.float32)
    scale = lax.rsqrt(jnp.mean(h * h, axis=1, keepdims=True) + EPS)
    gain_line = flat(gain)
    for s in range(ns):
        part = slice(s * dc, (s + 1) * dc)
        normed = (hidden[:, part].astype(jnp.float32) * scale * gain_line[:, part]).astype(jnp.bfloat16)
        buf[c, k, s] = normed
        mytail[:, part] = normed[rows - 16 :]
    pl.semaphore_wait(barrier, peers - 1 + spans - 1)

    def to_right(j, s):
        return copy(buf.at[j, k, s], buf.at[j, k, s], rsend.at[j, s], rrecv.at[j, s], {"tp": lax.rem(tp + 2, peers)})

    def to_left(j, s):
        return copy(buf.at[j, k, s], buf.at[j, k, s], lsend.at[j, s], lrecv.at[j, s], {"tp": lax.rem(tp + peers - 2, peers)})

    def to_sib(j, s):
        return copy(buf.at[j, k, s], buf.at[j, k, s], xsend.at[j, s], xrecv.at[j, s], sib)

    def from_sib(j, s):
        return copy(buf.at[j, 1 - k, s], buf.at[j, 1 - k, s], xsend.at[j, s], xrecv.at[j, s], sib)

    def own(s, carry):
        @pl.when(has_right)
        def _():
            to_right(c, s).start()

        @pl.when(has_left)
        def _():
            to_left(c, s).start()

        to_sib(c, s).start()
        return carry

    def w_far(m, core):
        return copy(
            wout.at[:, half_cols_at(core, seq)], wq.at[tp, seq],
            wsend.at[1 + m, core], wrecv.at[tp], {"tp": 2 * servers[m] + core},
        )

    other = tp + 1 - 2 * k
    w_near = [
        copy(wout.at[:, half_cols_at(1 - k, e)], wq.at[tp, e], wsend.at[1 + len(servers), e], wrecv.at[tp], sib)
        for e in range(spans)
    ]
    near_in = copy(wq.at[other], wq.at[other], wsend.at[0, 0], wrecv.at[other], sib)

    def w_send(m, core, close):
        @pl.when((c != servers[m]) & ((c // 2 == m) == close))
        def _():
            w_far(m, core).start()

    sends = [(m, core) for m in range(len(servers)) for core in range(2)]
    lax.fori_loop(0, ns, own, 0)

    last = peers - 1
    has_tail = seq > 0
    tail_next = copy(mytail, tail, tsend.at[0], trecv.at[0], {"seq": lax.rem(seq + 1, spans)})
    tail_left = copy(tail, tail, tsend.at[1], trecv.at[0], {"tp": lax.rem(tp + peers - 2, peers)})
    tail_sib = copy(tail, tail, tsend.at[2], trecv.at[0], sib)

    @pl.when((tp == last) & (seq < spans - 1))
    def _():
        tail_next.start()

    group_out = copy(group, gbuf.at[k], gsend.at[0], grecv.at[0], sib)
    group_out.start()
    gtaps[k] = jnp.zeros((8, LANES), jnp.float32)
    gtaps[k, :count] = taps_group[...].astype(jnp.float32)
    taps_out = copy(gtaps.at[k], gtaps.at[k], gsend.at[1], grecv.at[1], sib)
    taps_out.start()

    @pl.when(serving)
    def _():
        for part in w_near:
            part.start()

    def far_block(m):
        beyond = lax.rem(4 * (c // 2) + 2 + m, peers)
        return jnp.where(m < 2, 2 * mate + m, beyond)

    def wq_part(j, span):
        return wq.at[j, span]

    def q_copy(j, origin, b):
        return copy(
            wq_part(j, origin), wq_part(j, origin), qsend.at[j, origin, b], qrecv.at[j, origin],
            {"seq": seq ^ (1 << b)},
        )

    def q_spread(m):
        j = far_block(m)
        copy(wq_part(j, seq), wq_part(j, seq), wsend.at[0, 0], wrecv.at[j], sib).wait_recv()
        for b in range(bits):
            q_copy(j, seq, b).start()

    def q_forwards(up):
        found = []
        for e in range(1, spans):
            top, low = e.bit_length() - 1, (e & -e).bit_length() - 1
            targets = [b for b in range(bits) if (b > top if up else b < low)]
            found.append((e, targets))
        return found

    def q_forward(m):
        j = far_block(m)
        for up in (True, False):
            @pl.when(j % 2 == (0 if up else 1))
            def _():
                for e, targets in q_forwards(up):
                    if targets:
                        origin = seq ^ e
                        part = wq_part(j, origin)
                        copy(part, part, wsend.at[0, 0], qrecv.at[j, origin], sib).wait_recv()
                        for b in targets:
                            q_copy(j, origin, b).start()

    def q_drain(m):
        j = far_block(m)
        for b in range(bits):
            q_copy(j, seq, b).wait_send()
        for up in (True, False):
            @pl.when(j % 2 == (0 if up else 1))
            def _():
                for e, targets in q_forwards(up):
                    for b in targets:
                        q_copy(j, seq ^ e, b).wait_send()

    inner_in.wait()
    lane_tiles = inner_dev // 2 // LANES
    size = 256
    depth = size // (2 * lane_tiles)
    row_at = lax.broadcasted_iota(jnp.int32, (size, size), 0)
    col_at = lax.broadcasted_iota(jnp.int32, (size, size), 1)
    kk, jj, tt = row_at % depth, row_at // (depth * lane_tiles), row_at // depth % lane_tiles
    perm = (col_at == kk * (2 * lane_tiles) + tt * 2 + jj).astype(jnp.float32).astype(jnp.bfloat16)
    gate_at = half_cols + 2 * LANES

    def sort(i, carry):
        block = raw[pl.ds(pl.multiple_of(i * size, size), size), :]
        out = jnp.dot(perm, block, preferred_element_type=jnp.float32).astype(jnp.bfloat16)
        at = pl.ds(pl.multiple_of(i * depth, depth), depth)
        for t in range(lane_tiles):
            w[at, gate_at + t * LANES : gate_at + (t + 1) * LANES] = out[t * depth : (t + 1) * depth]
            scan = out[(lane_tiles + t) * depth : (lane_tiles + t + 1) * depth]
            w[at, t * LANES : (t + 1) * LANES] = scan
        return carry

    lax.fori_loop(0, raw.shape[0] // size, sort, 0)
    pick_at = [lax.broadcasted_iota(jnp.int32, (heads, LANES), d) for d in range(2)]
    pick = (pick_at[0] == pick_at[1]).astype(jnp.float32)

    def turn(i, carry):
        at = pl.ds(pl.multiple_of(i * size, size), size)
        out = dot16(step[:, at], pick, ((0,), (0,)))
        w[at, gate_at + half_cols :] = out.astype(jnp.bfloat16)
        return carry

    lax.fori_loop(0, width // size, turn, 0)
    group_in.wait()
    copy(gbuf.at[1 - k], gbuf.at[1 - k], gsend.at[0], grecv.at[0], sib).wait_recv()
    copy(gtaps.at[1 - k], gtaps.at[1 - k], gsend.at[1], grecv.at[1], sib).wait_recv()
    taps[:count, :half_cols] = taps_inner[...].astype(jnp.float32)
    for m in range(2):
        w[:, half_cols + m * LANES : half_cols + (m + 1) * LANES] = gbuf[m]
        taps[:, half_cols + m * LANES : half_cols + (m + 1) * LANES] = gtaps[m]

    def arrivals(i):
        d, s = i // ns, i % ns

        @pl.when(c - d >= 0)
        def _():
            j = c - d
            copy(buf.at[j, k, s], buf.at[j, k, s], rsend.at[j, s], rrecv.at[j, s], sib).wait_recv()

            @pl.when(has_right)
            def _():
                to_right(j, s).start()

            to_sib(j, s).start()

        @pl.when(c + d < n)
        def _():
            j = c + d
            copy(buf.at[j, k, s], buf.at[j, k, s], lsend.at[j, s], lrecv.at[j, s], sib).wait_recv()

            @pl.when(has_left)
            def _():
                to_left(j, s).start()

            to_sib(j, s).start()

    def compute(i):
        d, s = i // ns, i % ns

        def side(which, carry):
            j = c - d + 2 * d * which

            @pl.when((j >= 0) & (j < n) & ((which == 0) | (d > 0)))
            def _():
                from_sib(j, s).wait_recv()
                x = buf[j, :, s].reshape(2 * rows, dc)
                at = pl.ds(pl.multiple_of(s * dc, dc), dc)
                out = jnp.dot(x, w[at, :], preferred_element_type=jnp.float32)
                place = pl.ds(pl.multiple_of(j * 2 * rows, 2 * rows), 2 * rows)

                @pl.when(s == 0)
                def _():
                    proj[place, :] = out

                @pl.when(s > 0)
                def _():
                    proj[place, :] += out

            return carry

        lax.fori_loop(0, 2, side, 0)

    far = peers - 2
    first_spread, first_forward = 2 * ns - 1, 2 * ns + 2
    near = min(2, far)

    def item(i, carry):
        @pl.when((i >= ns) & (i < n * ns))
        def _():
            arrivals(i)

        @pl.when((i == ns + 1) & has_tail & (k == 1))
        def _():
            copy(tail, tail, tsend.at[1], trecv.at[0], sib).wait_recv()

            @pl.when(has_left)
            def _():
                tail_left.start()

            tail_sib.start()

        for close, when in ((True, ns), (False, 3 * ns - 1)):
            @pl.when(i == when)
            def _():
                for m, core in sends:
                    w_send(m, core, close)

        compute(i - 1)

        @pl.when(serving & (i >= first_spread) & (i < first_spread + near))
        def _():
            q_spread(i - first_spread)

        @pl.when(serving & (i >= first_forward) & (i < first_forward + near))
        def _():
            q_forward(i - first_forward)

        return carry

    lax.fori_loop(1, n * ns + 1, item, 0)

    @pl.when(serving)
    def _():
        def rest(m, carry):
            q_spread(m)

            @pl.when(m >= 4)
            def _():
                q_forward(m - 2)

            return carry

        lax.fori_loop(near, far, rest, 0)

    conv = half_cols + 2 * LANES

    @pl.when(has_tail)
    def _():
        @pl.when(k == 0)
        def _():
            copy(tail, tail, tsend.at[1], trecv.at[0], sib).wait_recv()

        edge[...] = jnp.dot(tail[...], w[:, :conv], preferred_element_type=jnp.float32)[8:]

    @pl.when(jnp.logical_not(has_tail))
    def _():
        edge[...] = jnp.zeros_like(edge)

    inner_own = half_cols
    head_dim = inner_own // heads
    states = LANES
    length = peers * rows
    bias_line = head_line(bias, heads, LANES, 1)
    rate_line = head_line(rate, heads, LANES, 1)
    skip_line = head_line(skip, heads, inner_own, head_dim)
    first = seq * (length // STRETCH)
    state[...] = jnp.zeros_like(state)
    total[...] = jnp.zeros_like(total)

    def stretch(i, carry):
        for m in range(max(near, far - 2), far):
            @pl.when(serving & (i == 3 * (m - far + 3) - 1))
            def _():
                q_forward(m)

        at = pl.ds(pl.multiple_of(i * STRETCH, STRETCH), STRETCH)
        scan_stretch(
            count, heads, head_dim, inner_own, states, at,
            proj, segments, first, i, taps, bias_line, rate_line, skip_line, y, c_maps, w_span, edge, state, total,
        )
        return carry

    lax.fori_loop(0, length // STRETCH, stretch, 0)

    packed[...] = state[...].astype(jnp.bfloat16)
    decay[...] = jnp.broadcast_to(
        widen(w_span[length - 8 :, :], heads, head_dim)[7:8], decay.shape
    )

    def state_to(e):
        dev = {"seq": lax.rem(seq + e, spans)}
        return (
            copy(packed, came.at[e], ssend.at[0, e], srecv.at[0, e], dev),
            copy(decay, came_decay.at[e], ssend.at[1, e], srecv.at[1, e], dev),
        )

    for e in range(1, spans):
        @pl.when(seq + e < spans)
        def _():
            for part in state_to(e):
                part.start()

    state[...] = jnp.zeros_like(state)
    for e in range(spans - 1, 0, -1):
        @pl.when(e <= seq)
        def _():
            for part in state_to(e):
                part.wait_recv()
            state[...] = came[e].astype(jnp.float32) + came_decay[e, 0:1] * state[...]

    block = 2 * rows
    pairs = n // 2

    def chip_at(i):
        m = lax.rem(i, pairs)
        first = i < pairs
        return jnp.where(first, 2 * m + m % 2, 2 * m + 1 - m % 2)

    def rows_of(chip):
        return pl.ds(pl.multiple_of(chip * block, block), block)

    def sq_copy(chip):
        return copy(sq.at[0, chip], sq.at[1, chip], esend.at[chip], erecv.at[chip], sib)

    def gate_block(i, carry):
        chip = chip_at(i)
        at = rows_of(chip)
        entering = dot16(c_maps[at, :], state[...]) * widen(w_span[at, :], heads, head_dim)
        gated = (y[at, :] + entering) * silu(proj[at, conv : conv + inner_own])
        y[at, :] = gated
        sums = jnp.sum(gated * gated, axis=1, keepdims=True)
        sq[0, chip] = jnp.broadcast_to(sums, (block, LANES))
        sq_copy(chip).start()
        return carry

    lax.fori_loop(0, n, gate_block, 0)

    def server_of(chip):
        m = chip // 2
        return 2 * m + 1 - m % 2

    def slot_of(chip):
        return jnp.where(chip == server_of(chip), 1, 0)

    def mixed_far(chip):
        return copy(
            mixed.at[chip], taken.at[slot_of(chip), tp], msend.at[chip], mrecv.at[slot_of(chip), c],
            {"tp": lax.rem(2 * server_of(chip) + k, peers)},
        )

    def mixed_near(slot, src):
        place = taken.at[slot, 2 * src + k]
        return copy(place, place, nsend.at[slot, src], nrecv.at[slot, src], sib)

    mix_line = flat(mixer_gain)

    def mix_block(i, carry):
        chip = chip_at(i)
        at = rows_of(chip)
        sq_copy(chip).wait_recv()
        mean = (sq[0, chip] + sq[1, chip]) / (2 * inner_own)
        factor = lax.rsqrt(mean + EPS)
        wide = jnp.concatenate([factor] * (inner_own // LANES), axis=1)
        done = (y[at, :] * wide * mix_line).astype(jnp.bfloat16)

        @pl.when(c != server_of(chip))
        def _():
            mixed[chip] = done
            mixed_far(chip).start()

        @pl.when(c == server_of(chip))
        def _():
            taken[slot_of(chip), tp] = done
            mixed_near(slot_of(chip), c).start()

        return carry

    lax.fori_loop(0, n, mix_block, 0)

    def result_far(q, core):
        return copy(
            results.at[0, q, pl.ds(core * rows, rows)], landed.at[k, q], osend.at[q, core], orecv.at[k, q],
            {"tp": 2 * mate + core},
        )

    def result_near(q):
        return copy(
            results.at[1, q, pl.ds(pl.multiple_of((1 - k) * rows, rows), rows)], landed.at[k, q],
            osend.at[q, 2], orecv.at[k, q], sib,
        )

    @pl.when(serving)
    def _():
        for e in range(spans):
            own_half[e].wait()
        near_in.wait_recv()

        def collect(slot):
            def relay(m, carry):
                src = lax.rem(c + m, n)
                place = taken.at[slot, 2 * src + k]
                copy(place, place, nsend.at[slot, src], mrecv.at[slot, src], sib).wait_recv()
                mixed_near(slot, src).start()
                return carry

            lax.fori_loop(1, n, relay, 0)

            def from_near(src, carry):
                place = taken.at[slot, 2 * src + 1 - k]
                copy(place, place, nsend.at[slot, src], nrecv.at[slot, src], sib).wait_recv()
                return carry

            lax.fori_loop(0, n, from_near, 0)

        def multiply(slot, q):
            sums = jnp.zeros((block, wq.shape[3]), jnp.float32)
            for j in range(peers):
                sums += jnp.dot(taken[slot, j], wq[j, q], preferred_element_type=jnp.float32)
            return sums.astype(jnp.bfloat16)

        collect(0)

        def for_mate(e, carry):
            q = seq ^ e

            def part_in(m, carry):
                j = far_block(m)
                ends = jnp.where(j % 2 == 0, 2 * e >= spans, e % 2 == 1)

                @pl.when((e > 0) & ends)
                def _():
                    part = wq_part(j, q)
                    copy(part, part, wsend.at[0, 0], qrecv.at[j, q], sib).wait_recv()

                return carry

            lax.fori_loop(0, far, part_in, 0)
            results[0, q] = multiply(0, q)
            for core in range(2):
                result_far(q, core).start()
            return carry

        lax.fori_loop(0, spans, for_mate, 0)
        collect(1)

        def for_own(q, carry):
            results[1, q] = multiply(1, q)
            result_near(q).start()
            landed[k, q] = results[1, q, pl.ds(pl.multiple_of(k * rows, rows), rows)]
            return carry

        lax.fori_loop(0, spans, for_own, 0)

    def finish(core, q):
        place = landed.at[core, q]
        arrival = copy(place, place, osend.at[q, 0], orecv.at[core, q], sib)

        @pl.when(jnp.logical_not(serving) | (k != core))
        def _():
            arrival.wait_recv()

        at = pl.ds(core * half + q * quarter, quarter)
        out[:, at] = (hidden[:, at].astype(jnp.float32) + landed[core, q].astype(jnp.float32)).astype(jnp.bfloat16)

    for q in range(spans):
        for core in range(2):
            finish(core, q)

    def drain(i, carry):
        j, s = i // ns, i % ns
        to_sib(j, s).wait_send()

        @pl.when(has_right & (j <= c))
        def _():
            to_right(j, s).wait_send()

        @pl.when(has_left & (j >= c))
        def _():
            to_left(j, s).wait_send()

        return carry

    lax.fori_loop(0, n * ns, drain, 0)
    group_out.wait_send()
    taps_out.wait_send()

    @pl.when((tp == last) & (seq < spans - 1))
    def _():
        tail_next.wait_send()

    @pl.when(has_tail & (k == 1))
    def _():
        @pl.when(has_left)
        def _():
            tail_left.wait_send()

        tail_sib.wait_send()

    for m, core in sends:
        @pl.when(c != servers[m])
        def _():
            w_far(m, core).wait_send()

    for e in range(1, spans):
        @pl.when(seq + e < spans)
        def _():
            for part in state_to(e):
                part.wait_send()

    def sums_left(chip, carry):
        sq_copy(chip).wait_send()

        @pl.when(c != server_of(chip))
        def _():
            mixed_far(chip).wait_send()

        return carry

    lax.fori_loop(0, n, sums_left, 0)

    @pl.when(serving)
    def _():
        for e in range(spans):
            w_near[e].wait_send()

        def far_left(m, carry):
            q_drain(m)
            return carry

        lax.fori_loop(0, far, far_left, 0)

        def near_left(src, carry):
            for slot in range(2):
                mixed_near(slot, src).wait_send()
            return carry

        lax.fori_loop(0, n, near_left, 0)

        def results_left(q, carry):
            for core in range(2):
                result_far(q, core).wait_send()
            result_near(q).wait_send()
            return carry

        lax.fori_loop(0, spans, results_left, 0)


def mixer(hidden, gain, inner, group, step, wout, segments, taps_inner, taps_group, bias, rate, skip, mixer_gain, heads, count, n, spans, ns):
    rows, width = hidden.shape
    inner_dev = inner.shape[0] * inner.shape[1] // width
    own = inner_dev // 2
    cols = inner_dev + 3 * LANES
    half = wout.shape[1] // 2
    length = 2 * n * rows
    vmem = pl.BlockSpec(memory_space=pltpu.VMEM)
    anywhere = pl.BlockSpec(memory_space=pl.ANY)
    scalars = pl.BlockSpec(memory_space=pltpu.SMEM)
    dma = pltpu.SemaphoreType.DMA
    bits = max(1, spans.bit_length() - 1)
    bf16, f32 = jnp.bfloat16, jnp.float32
    return pl.pallas_call(
        functools.partial(mixer_kernel, n, spans, ns, heads, count),
        out_shape=jax.ShapeDtypeStruct(hidden.shape, bf16),
        in_specs=[vmem, vmem, anywhere, anywhere, vmem, anywhere] + [vmem] * 3 + [scalars] * 3 + [vmem],
        out_specs=vmem,
        scratch_shapes=[
            pltpu.VMEM((n, 2, ns, rows, width // ns), bf16),
            pltpu.VMEM((16, width), bf16),
            pltpu.VMEM((16, width), bf16),
            pltpu.VMEM(inner.shape, bf16),
            pltpu.VMEM((2,) + group.shape, bf16),
            pltpu.VMEM((2, 8, LANES), f32),
            pltpu.VMEM((8, own + 2 * LANES), f32),
            pltpu.VMEM((width, cols), bf16),
            pltpu.VMEM((length, cols), f32),
            pltpu.VMEM((8, own + 2 * LANES), f32),
            pltpu.VMEM((2 * n, spans, wout.shape[0], half // spans), bf16),
            pltpu.VMEM((length, own), f32),
            pltpu.VMEM((length, LANES), bf16),
            pltpu.VMEM((length, LANES), f32),
            pltpu.VMEM((LANES, own), f32),
            pltpu.VMEM((1, LANES), f32),
            pltpu.VMEM((LANES, own), bf16),
            pltpu.VMEM((8, own), f32),
            pltpu.VMEM((spans, LANES, own), bf16),
            pltpu.VMEM((spans, 8, own), f32),
            pltpu.VMEM((2, n, 2 * rows, LANES), f32),
            pltpu.VMEM((n, 2 * rows, own), bf16),
            pltpu.VMEM((2, 2 * n, 2 * rows, own), bf16),
            pltpu.VMEM((2, spans, 2 * rows, half // spans), bf16),
            pltpu.VMEM((2, spans, rows, half // spans), bf16),
            dma((n, ns)), dma((n, ns)), dma((n, ns)), dma((n, ns)), dma((n, ns)), dma((n, ns)),
            dma((3,)), dma((1,)), dma((2,)), dma((2,)),
            dma((2 + n // 2, max(2, spans))), dma((2 * n,)), dma((2 * n, spans, bits)), dma((2 * n, spans)), dma((3,)),
            dma((2, spans)), dma((2, spans)), dma((n,)), dma((n,)),
            dma((n,)), dma((2, n)), dma((2, n)), dma((2, n)), dma((spans, 3)), dma((2, spans)),
        ],
        compiler_params=pltpu.CompilerParams(
            collective_id=0, has_side_effects=True, vmem_limit_bytes=60 << 20
        ),
        cost_estimate=pl.CostEstimate(
            flops=24_000_000_000, bytes_accessed=12_000_000, transcendentals=4_000_000
        ),
        name="mixer",
    )(hidden, gain, inner, group, step, wout, segments, taps_inner, taps_group, bias, rate, skip, mixer_gain)


def by_row(weight):
    width, pair, cols = weight.shape
    tiles = cols // LANES
    return weight.reshape(width, pair, tiles, LANES).transpose(0, 2, 1, 3).reshape(-1, LANES)


def body(
    hidden,
    norm_gain,
    inner_weight,
    group_weight,
    step_weight,
    step_bias,
    decay_rate,
    filter_inner,
    filter_group,
    skip_gain,
    mixer_gain,
    output_weight,
    segment_ids,
):
    spans, chips = lax.axis_size("seq"), lax.axis_size("tp") // 2
    return mixer(
        hidden, norm_gain.reshape(-1, LANES), by_row(inner_weight), group_weight, step_weight.T, output_weight,
        segment_ids.reshape(-1, STRETCH), filter_inner, filter_group, step_bias, decay_rate, skip_gain,
        mixer_gain.reshape(-1, LANES), step_weight.shape[1], filter_inner.shape[0], chips, spans, 4,
    )


def solution(mesh):
    in_specs = (
        P(("seq", "tp"), None),
        P(),
        P(None, None, "tp"),
        P(None, "tp"),
        P(None, "tp"),
        P("tp"),
        P("tp"),
        P(None, "tp"),
        P(None, "tp"),
        P("tp"),
        P("tp"),
        P("tp", None),
        P(),
    )
    out_specs = P(("seq", "tp"), None)
    return jax.shard_map(body, mesh=mesh, in_specs=in_specs, out_specs=out_specs, check_vma=False)
```

```python
import functools
import jax
import jax.numpy as jnp
from jax import lax
from jax.experimental import pallas as pl
from jax.experimental.pallas import tpu as pltpu
from jax.sharding import PartitionSpec as P

EPS = 1e-05
LANES = 128
STRETCH = 128
HIGH = lax.Precision.HIGHEST
MESH = pl.DeviceIdType.MESH


def silu(v):
    return v / (1.0 + jnp.exp(-v))


def widen(cols, heads, head_dim):
    rows = cols.shape[0]
    parts = [jnp.broadcast_to(cols[:, h : h + 1], (rows, head_dim)) for h in range(heads)]
    return jnp.concatenate(parts, axis=1)


def dot16(a, b, dims=((1,), (0,))):
    a, b = a.astype(jnp.bfloat16), b.astype(jnp.bfloat16)
    return lax.dot_general(a, b, (dims, ((), ())), preferred_element_type=jnp.float32)


def segment_marks(segments, first, i):
    shape = (8, STRETCH)

    def line(at):
        ids = segments[pl.ds(jnp.maximum(at, 0), 1), :].astype(jnp.float32)
        return jnp.broadcast_to(jnp.where(at >= 0, ids, -1.0), shape)

    now, past, span_past = line(first + i), line(first + i - 1), line(first - 1)
    lane = lax.broadcasted_iota(jnp.int32, shape, 1)
    row = lax.broadcasted_iota(jnp.int32, shape, 0)
    end = slice(STRETCH - 1, STRETCH)
    marks = now
    for back in range(1, 4):
        other = jnp.where(lane < back, pltpu.roll(past, back, 1), pltpu.roll(now, back, 1))
        marks = jnp.where(row == back, (now == other).astype(jnp.float32), marks)
    for at, other in ((4, past[:, end]), (5, now[:, end]), (6, span_past[:, end])):
        marks = jnp.where(row == at, (now == other).astype(jnp.float32), marks)
    return marks.T, now[0:1]


def head_line(values, heads, width, reach):
    lane = lax.broadcasted_iota(jnp.int32, (1, width), 1)
    line = jnp.zeros((1, width), jnp.float32)
    for h in range(heads):
        line = jnp.where((lane >= h * reach) & (lane < (h + 1) * reach), values[h], line)
    return line


def flat(ref):
    return jnp.concatenate([ref[i : i + 1, :] for i in range(ref.shape[0])], axis=1)


def scan_stretch(
    count, heads, head_dim, inner, states, at,
    proj, segments, first, i, taps, bias, rate, skip, y_out, c_out, w_out, edge, state, total,
):
    aux, row_seg = segment_marks(segments, first, i)
    conv = inner + 2 * states
    cur = proj[at, :conv]
    both = jnp.concatenate([edge[...], cur], axis=0)
    edge[...] = cur[STRETCH - 8 :]
    size = STRETCH
    tap = taps[...]
    acc = tap[count - 1 : count] * cur
    for back in range(1, count):
        same = aux[:, back : back + 1]
        acc += tap[count - 1 - back : count - back] * both[8 - back : 8 - back + size] * same
    active = silu(acc)
    x = active[:, :inner]
    b_map = active[:, inner : inner + states]
    c_map = active[:, inner + states :]
    raw = proj[at, conv + inner :] + bias
    step = jnp.maximum(raw, 0.0) + jnp.log1p(jnp.exp(-jnp.abs(raw)))
    log_decay = -step * rate
    row_at = lax.broadcasted_iota(jnp.int32, (size, size), 0)
    col_at = lax.broadcasted_iota(jnp.int32, (size, size), 1)
    causal = row_at >= col_at
    cum = jnp.dot(
        causal.astype(jnp.float32), log_decay, precision=HIGH, preferred_element_type=jnp.float32
    )
    cum_rows = cum.T
    alive, in_last, alive_span = aux[:, 4:5], aux[:, 5:6], aux[:, 6:7]
    last = cum[size - 1 :]
    mask = causal & (aux[:, 0:1] == row_seg)
    xs = x * widen(step, heads, head_dim)
    xs16 = xs.astype(jnp.bfloat16)
    products = dot16(c_map, b_map, ((1,), (1,)))
    parts = []
    for h in range(heads):
        gap = cum[:, h : h + 1] - cum_rows[h : h + 1, :]
        mixing = products * jnp.exp(jnp.where(mask, gap, -1e30))
        parts.append(dot16(mixing, xs16[:, h * head_dim : (h + 1) * head_dim]))
    local = jnp.concatenate(parts, axis=1)
    entry = jnp.exp(cum) * alive
    carried = dot16(c_map, state[...]) * widen(entry, heads, head_dim)
    y_out[at, :] = local + carried + skip * x
    c_out[at, :] = c_map.astype(jnp.bfloat16)
    w_span = jnp.exp(cum + total[...]) * alive_span
    w_out[at, :] = w_span
    end = jnp.exp(last - cum) * in_last
    fresh = dot16(b_map, xs * widen(end, heads, head_dim), ((0,), (0,)))
    state[...] = widen(entry[size - 1 :], heads, head_dim) * state[...] + fresh
    total[...] = total[...] + last


def servers_of(chips):
    return [2 * i + 1 - i % 2 for i in range(chips // 2)]


def mixer_kernel(
    n, spans, ns, heads, count,
    hidden, gain, inner, group, step, wout, segments, taps_inner, taps_group, bias, rate, skip, mixer_gain,
    out,
    buf, mytail, tail, raw, gbuf, gtaps, taps, w, proj, edge, wq,
    y, c_maps, w_span, state, total, packed, decay, came, came_decay,
    sq, mixed, taken, results, landed,
    rsend, lsend, xsend, rrecv, lrecv, xrecv,
    tsend, trecv, gsend, grecv, wsend, wrecv, qsend, qrecv, local,
    ssend, srecv, esend, erecv, msend, mrecv, nsend, nrecv, osend, orecv,
):
    tp, seq = lax.axis_index("tp"), lax.axis_index("seq")
    c, k = tp // 2, tp % 2
    rows, width = hidden.shape
    dc = width // ns
    sib = {"tp": tp + 1 - 2 * k}
    has_left, has_right = c > 0, c < n - 1
    inner_dev = w.shape[1] - 3 * LANES
    half_cols = inner_dev // 2
    servers = servers_of(n)
    mate = jnp.where(c == 2 * (c // 2), c + 1, c - 1)
    serving = functools.reduce(jnp.logical_or, [c == s for s in servers])
    bits = spans.bit_length() - 1
    half = wout.shape[1] // 2
    quarter = half // spans

    def copy(src, dst, send, recv, dev):
        return pltpu.make_async_remote_copy(
            src_ref=src, dst_ref=dst, send_sem=send, recv_sem=recv, device_id=dev, device_id_type=MESH
        )

    inner_in = pltpu.make_async_copy(inner, raw, local.at[0])
    group_in = pltpu.make_async_copy(group, gbuf.at[k], local.at[1])

    def half_cols_at(core, span):
        return pl.ds(pl.multiple_of(core * half + span * quarter, LANES), quarter)

    own_half = [
        pltpu.make_async_copy(wout.at[:, half_cols_at(k, e)], wq.at[tp, e], wsend.at[0, e])
        for e in range(spans)
    ]
    inner_in.start()
    group_in.start()

    @pl.when(serving)
    def _():
        for part in own_half:
            part.start()

    barrier = pltpu.get_barrier_semaphore()
    peers = 2 * n

    def greet(axis, size, me):
        def hello(i, carry):
            pl.semaphore_signal(
                barrier, inc=1, device_id={axis: lax.rem(me + i, size)}, device_id_type=MESH
            )
            return carry
        lax.fori_loop(1, size, hello, 0)

    greet("tp", peers, tp)
    greet("seq", spans, seq)

    h = hidden[...].astype(jnp.float32)
    scale = lax.rsqrt(jnp.mean(h * h, axis=1, keepdims=True) + EPS)
    gain_line = flat(gain)
    for s in range(ns):
        part = slice(s * dc, (s + 1) * dc)
        normed = (hidden[:, part].astype(jnp.float32) * scale * gain_line[:, part]).astype(jnp.bfloat16)
        buf[c, k, s] = normed
        mytail[:, part] = normed[rows - 16 :]
    pl.semaphore_wait(barrier, peers - 1 + spans - 1)

    def to_right(j, s):
        return copy(buf.at[j, k, s], buf.at[j, k, s], rsend.at[j, s], rrecv.at[j, s], {"tp": lax.rem(tp + 2, peers)})

    def to_left(j, s):
        return copy(buf.at[j, k, s], buf.at[j, k, s], lsend.at[j, s], lrecv.at[j, s], {"tp": lax.rem(tp + peers - 2, peers)})

    def to_sib(j, s):
        return copy(buf.at[j, k, s], buf.at[j, k, s], xsend.at[j, s], xrecv.at[j, s], sib)

    def from_sib(j, s):
        return copy(buf.at[j, 1 - k, s], buf.at[j, 1 - k, s], xsend.at[j, s], xrecv.at[j, s], sib)

    def own(s, carry):
        @pl.when(has_right)
        def _():
            to_right(c, s).start()

        @pl.when(has_left)
        def _():
            to_left(c, s).start()

        to_sib(c, s).start()
        return carry

    def w_far(m, core):
        return copy(
            wout.at[:, half_cols_at(core, seq)], wq.at[tp, seq],
            wsend.at[1 + m, core], wrecv.at[tp], {"tp": 2 * servers[m] + core},
        )

    other = tp + 1 - 2 * k
    w_near = [
        copy(wout.at[:, half_cols_at(1 - k, e)], wq.at[tp, e], wsend.at[1 + len(servers), e], wrecv.at[tp], sib)
        for e in range(spans)
    ]
    near_in = copy(wq.at[other], wq.at[other], wsend.at[0, 0], wrecv.at[other], sib)

    def w_send(m, core, close):
        @pl.when((c != servers[m]) & ((c // 2 == m) == close))
        def _():
            w_far(m, core).start()

    sends = [(m, core) for m in range(len(servers)) for core in range(2)]
    lax.fori_loop(0, ns, own, 0)

    last = peers - 1
    has_tail = seq > 0
    tail_next = copy(mytail, tail, tsend.at[0], trecv.at[0], {"seq": lax.rem(seq + 1, spans)})
    tail_left = copy(tail, tail, tsend.at[1], trecv.at[0], {"tp": lax.rem(tp + peers - 2, peers)})
    tail_sib = copy(tail, tail, tsend.at[2], trecv.at[0], sib)

    @pl.when((tp == last) & (seq < spans - 1))
    def _():
        tail_next.start()

    group_out = copy(group, gbuf.at[k], gsend.at[0], grecv.at[0], sib)
    group_out.start()
    gtaps[k] = jnp.zeros((8, LANES), jnp.float32)
    gtaps[k, :count] = taps_group[...].astype(jnp.float32)
    taps_out = copy(gtaps.at[k], gtaps.at[k], gsend.at[1], grecv.at[1], sib)
    taps_out.start()

    @pl.when(serving)
    def _():
        for part in w_near:
            part.start()

    def far_block(m):
        beyond = lax.rem(4 * (c // 2) + 2 + m, peers)
        return jnp.where(m < 2, 2 * mate + m, beyond)

    def wq_part(j, span):
        return wq.at[j, span]

    def q_copy(j, origin, b):
        return copy(
            wq_part(j, origin), wq_part(j, origin), qsend.at[j, origin, b], qrecv.at[j, origin],
            {"seq": seq ^ (1 << b)},
        )

    def q_spread(m):
        j = far_block(m)
        copy(wq_part(j, seq), wq_part(j, seq), wsend.at[0, 0], wrecv.at[j], sib).wait_recv()
        for b in range(bits):
            q_copy(j, seq, b).start()

    def q_forwards(up):
        found = []
        for e in range(1, spans):
            top, low = e.bit_length() - 1, (e & -e).bit_length() - 1
            targets = [b for b in range(bits) if (b > top if up else b < low)]
            found.append((e, targets))
        return found

    def q_forward(m):
        j = far_block(m)
        for up in (True, False):
            @pl.when(j % 2 == (0 if up else 1))
            def _():
                for e, targets in q_forwards(up):
                    if targets:
                        origin = seq ^ e
                        part = wq_part(j, origin)
                        copy(part, part, wsend.at[0, 0], qrecv.at[j, origin], sib).wait_recv()
                        for b in targets:
                            q_copy(j, origin, b).start()

    def q_drain(m):
        j = far_block(m)
        for b in range(bits):
            q_copy(j, seq, b).wait_send()
        for up in (True, False):
            @pl.when(j % 2 == (0 if up else 1))
            def _():
                for e, targets in q_forwards(up):
                    for b in targets:
                        q_copy(j, seq ^ e, b).wait_send()

    inner_in.wait()
    lane_tiles = inner_dev // 2 // LANES
    size = 256
    depth = size // (2 * lane_tiles)
    row_at = lax.broadcasted_iota(jnp.int32, (size, size), 0)
    col_at = lax.broadcasted_iota(jnp.int32, (size, size), 1)
    kk, jj, tt = row_at % depth, row_at // (depth * lane_tiles), row_at // depth % lane_tiles
    perm = (col_at == kk * (2 * lane_tiles) + tt * 2 + jj).astype(jnp.float32).astype(jnp.bfloat16)
    gate_at = half_cols + 2 * LANES

    def sort(i, carry):
        block = raw[pl.ds(pl.multiple_of(i * size, size), size), :]
        out = jnp.dot(perm, block, preferred_element_type=jnp.float32).astype(jnp.bfloat16)
        at = pl.ds(pl.multiple_of(i * depth, depth), depth)
        for t in range(lane_tiles):
            w[at, gate_at + t * LANES : gate_at + (t + 1) * LANES] = out[t * depth : (t + 1) * depth]
            scan = out[(lane_tiles + t) * depth : (lane_tiles + t + 1) * depth]
            w[at, t * LANES : (t + 1) * LANES] = scan
        return carry

    lax.fori_loop(0, raw.shape[0] // size, sort, 0)
    pick_at = [lax.broadcasted_iota(jnp.int32, (heads, LANES), d) for d in range(2)]
    pick = (pick_at[0] == pick_at[1]).astype(jnp.float32)

    def turn(i, carry):
        at = pl.ds(pl.multiple_of(i * size, size), size)
        out = dot16(step[:, at], pick, ((0,), (0,)))
        w[at, gate_at + half_cols :] = out.astype(jnp.bfloat16)
        return carry

    lax.fori_loop(0, width // size, turn, 0)
    group_in.wait()
    copy(gbuf.at[1 - k], gbuf.at[1 - k], gsend.at[0], grecv.at[0], sib).wait_recv()
    copy(gtaps.at[1 - k], gtaps.at[1 - k], gsend.at[1], grecv.at[1], sib).wait_recv()
    taps[:count, :half_cols] = taps_inner[...].astype(jnp.float32)
    for m in range(2):
        w[:, half_cols + m * LANES : half_cols + (m + 1) * LANES] = gbuf[m]
        taps[:, half_cols + m * LANES : half_cols + (m + 1) * LANES] = gtaps[m]

    def arrivals(i):
        d, s = i // ns, i % ns

        @pl.when(c - d >= 0)
        def _():
            j = c - d
            copy(buf.at[j, k, s], buf.at[j, k, s], rsend.at[j, s], rrecv.at[j, s], sib).wait_recv()

            @pl.when(has_right)
            def _():
                to_right(j, s).start()

            to_sib(j, s).start()

        @pl.when(c + d < n)
        def _():
            j = c + d
            copy(buf.at[j, k, s], buf.at[j, k, s], lsend.at[j, s], lrecv.at[j, s], sib).wait_recv()

            @pl.when(has_left)
            def _():
                to_left(j, s).start()

            to_sib(j, s).start()

    def compute(i):
        d, s = i // ns, i % ns

        def side(which, carry):
            j = c - d + 2 * d * which

            @pl.when((j >= 0) & (j < n) & ((which == 0) | (d > 0)))
            def _():
                from_sib(j, s).wait_recv()
                x = buf[j, :, s].reshape(2 * rows, dc)
                at = pl.ds(pl.multiple_of(s * dc, dc), dc)
                out = jnp.dot(x, w[at, :], preferred_element_type=jnp.float32)
                place = pl.ds(pl.multiple_of(j * 2 * rows, 2 * rows), 2 * rows)

                @pl.when(s == 0)
                def _():
                    proj[place, :] = out

                @pl.when(s > 0)
                def _():
                    proj[place, :] += out

            return carry

        lax.fori_loop(0, 2, side, 0)

    far = peers - 2
    first_spread, first_forward = 2 * ns - 1, 2 * ns + 2
    near = min(2, far)

    def item(i, carry):
        @pl.when((i >= ns) & (i < n * ns))
        def _():
            arrivals(i)

        @pl.when((i == ns + 1) & has_tail & (k == 1))
        def _():
            copy(tail, tail, tsend.at[1], trecv.at[0], sib).wait_recv()

            @pl.when(has_left)
            def _():
                tail_left.start()

            tail_sib.start()

        for close, when in ((True, ns), (False, 3 * ns)):
            @pl.when(i == when)
            def _():
                for m, core in sends:
                    w_send(m, core, close)

        compute(i - 1)

        @pl.when(serving & (i >= first_spread) & (i < first_spread + near))
        def _():
            q_spread(i - first_spread)

        @pl.when(serving & (i >= first_forward) & (i < first_forward + near))
        def _():
            q_forward(i - first_forward)

        return carry

    lax.fori_loop(1, n * ns + 1, item, 0)

    conv = half_cols + 2 * LANES

    @pl.when(has_tail)
    def _():
        @pl.when(k == 0)
        def _():
            copy(tail, tail, tsend.at[1], trecv.at[0], sib).wait_recv()

        edge[...] = jnp.dot(tail[...], w[:, :conv], preferred_element_type=jnp.float32)[8:]

    @pl.when(jnp.logical_not(has_tail))
    def _():
        edge[...] = jnp.zeros_like(edge)

    inner_own = half_cols
    head_dim = inner_own // heads
    states = LANES
    length = peers * rows
    bias_line = head_line(bias, heads, LANES, 1)
    rate_line = head_line(rate, heads, LANES, 1)
    skip_line = head_line(skip, heads, inner_own, head_dim)
    first = seq * (length // STRETCH)
    state[...] = jnp.zeros_like(state)
    total[...] = jnp.zeros_like(total)

    early, early_at = near, 4

    def stretch(i, carry):
        for m in range(near, early):
            @pl.when(serving & (i == early_at))
            def _():
                q_spread(m)

        at = pl.ds(pl.multiple_of(i * STRETCH, STRETCH), STRETCH)
        scan_stretch(
            count, heads, head_dim, inner_own, states, at,
            proj, segments, first, i, taps, bias_line, rate_line, skip_line, y, c_maps, w_span, edge, state, total,
        )
        return carry

    lax.fori_loop(0, length // STRETCH, stretch, 0)

    packed[...] = state[...].astype(jnp.bfloat16)
    decay[...] = jnp.broadcast_to(
        widen(w_span[length - 8 :, :], heads, head_dim)[7:8], decay.shape
    )

    def state_to(e):
        dev = {"seq": lax.rem(seq + e, spans)}
        return (
            copy(packed, came.at[e], ssend.at[0, e], srecv.at[0, e], dev),
            copy(decay, came_decay.at[e], ssend.at[1, e], srecv.at[1, e], dev),
        )

    for e in range(1, spans):
        @pl.when(seq + e < spans)
        def _():
            for part in state_to(e):
                part.start()

    def over(act):
        def one(m, carry):
            act(m)
            return carry
        return one

    @pl.when(serving)
    def _():
        lax.fori_loop(early, far, over(q_spread), 0)

    state[...] = jnp.zeros_like(state)
    for e in range(spans - 1, 0, -1):
        @pl.when(e <= seq)
        def _():
            for part in state_to(e):
                part.wait_recv()
            state[...] = came[e].astype(jnp.float32) + came_decay[e, 0:1] * state[...]

    block = 2 * rows
    pairs = n // 2

    def chip_at(i):
        m = lax.rem(i, pairs)
        first = i < pairs
        return jnp.where(first, 2 * m + m % 2, 2 * m + 1 - m % 2)

    def rows_of(chip):
        return pl.ds(pl.multiple_of(chip * block, block), block)

    def sq_copy(chip):
        return copy(sq.at[0, chip], sq.at[1, chip], esend.at[chip], erecv.at[chip], sib)

    def gate_block(i, carry):
        chip = chip_at(i)
        at = rows_of(chip)
        entering = dot16(c_maps[at, :], state[...]) * widen(w_span[at, :], heads, head_dim)
        gated = (y[at, :] + entering) * silu(proj[at, conv : conv + inner_own])
        y[at, :] = gated
        sums = jnp.sum(gated * gated, axis=1, keepdims=True)
        sq[0, chip] = jnp.broadcast_to(sums, (block, LANES))
        sq_copy(chip).start()
        return carry

    lax.fori_loop(0, n, gate_block, 0)

    def server_of(chip):
        m = chip // 2
        return 2 * m + 1 - m % 2

    def slot_of(chip):
        return jnp.where(chip == server_of(chip), 1, 0)

    def mixed_far(chip):
        return copy(
            mixed.at[chip], taken.at[slot_of(chip), tp], msend.at[chip], mrecv.at[slot_of(chip), c],
            {"tp": lax.rem(2 * server_of(chip) + k, peers)},
        )

    def mixed_near(slot, src):
        place = taken.at[slot, 2 * src + k]
        return copy(place, place, nsend.at[slot, src], nrecv.at[slot, src], sib)

    mix_line = flat(mixer_gain)

    def mix_block(i, carry):
        chip = chip_at(i)
        at = rows_of(chip)
        sq_copy(chip).wait_recv()
        mean = (sq[0, chip] + sq[1, chip]) / (2 * inner_own)
        factor = lax.rsqrt(mean + EPS)
        wide = jnp.concatenate([factor] * (inner_own // LANES), axis=1)
        done = (y[at, :] * wide * mix_line).astype(jnp.bfloat16)

        @pl.when(c != server_of(chip))
        def _():
            mixed[chip] = done
            mixed_far(chip).start()

        @pl.when(c == server_of(chip))
        def _():
            taken[slot_of(chip), tp] = done
            mixed_near(slot_of(chip), c).start()

        return carry

    lax.fori_loop(0, n, mix_block, 0)

    def result_far(q, core):
        return copy(
            results.at[0, q, pl.ds(core * rows, rows)], landed.at[k, q], osend.at[q, core], orecv.at[k, q],
            {"tp": 2 * mate + core},
        )

    def result_near(q):
        return copy(
            results.at[1, q, pl.ds(pl.multiple_of((1 - k) * rows, rows), rows)], landed.at[k, q],
            osend.at[q, 2], orecv.at[k, q], sib,
        )

    @pl.when(serving)
    def _():
        for e in range(spans):
            own_half[e].wait()
        near_in.wait_recv()
        lax.fori_loop(near, max(near, far - 2), over(q_forward), 0)

        def collect(slot):
            def relay(m, carry):
                src = lax.rem(c + m, n)
                place = taken.at[slot, 2 * src + k]
                copy(place, place, nsend.at[slot, src], mrecv.at[slot, src], sib).wait_recv()
                mixed_near(slot, src).start()
                return carry

            lax.fori_loop(1, n, relay, 0)

            def from_near(src, carry):
                place = taken.at[slot, 2 * src + 1 - k]
                copy(place, place, nsend.at[slot, src], nrecv.at[slot, src], sib).wait_recv()
                return carry

            lax.fori_loop(0, n, from_near, 0)

        def multiply(slot, q):
            sums = jnp.zeros((block, wq.shape[3]), jnp.float32)
            for j in range(peers):
                sums += jnp.dot(taken[slot, j], wq[j, q], preferred_element_type=jnp.float32)
            return sums.astype(jnp.bfloat16)

        collect(0)

        def for_mate(e, carry):
            q = seq ^ e

            @pl.when(e == 1)
            def _():
                lax.fori_loop(max(near, far - 2), far, over(q_forward), 0)

            def part_in(m, carry):
                j = far_block(m)
                ends = jnp.where(j % 2 == 0, 2 * e >= spans, e % 2 == 1)

                @pl.when((e > 0) & ends)
                def _():
                    part = wq_part(j, q)
                    copy(part, part, wsend.at[0, 0], qrecv.at[j, q], sib).wait_recv()

                return carry

            lax.fori_loop(0, far, part_in, 0)
            results[0, q] = multiply(0, q)
            for core in range(2):
                result_far(q, core).start()
            return carry

        lax.fori_loop(0, spans, for_mate, 0)
        collect(1)

        def for_own(q, carry):
            results[1, q] = multiply(1, q)
            result_near(q).start()
            landed[k, q] = results[1, q, pl.ds(pl.multiple_of(k * rows, rows), rows)]
            return carry

        lax.fori_loop(0, spans, for_own, 0)

    def finish(core, q):
        place = landed.at[core, q]
        arrival = copy(place, place, osend.at[q, 0], orecv.at[core, q], sib)

        @pl.when(jnp.logical_not(serving) | (k != core))
        def _():
            arrival.wait_recv()

        at = pl.ds(core * half + q * quarter, quarter)
        out[:, at] = (hidden[:, at].astype(jnp.float32) + landed[core, q].astype(jnp.float32)).astype(jnp.bfloat16)

    for q in range(spans):
        for core in range(2):
            finish(core, q)

    def drain(i, carry):
        j, s = i // ns, i % ns
        to_sib(j, s).wait_send()

        @pl.when(has_right & (j <= c))
        def _():
            to_right(j, s).wait_send()

        @pl.when(has_left & (j >= c))
        def _():
            to_left(j, s).wait_send()

        return carry

    lax.fori_loop(0, n * ns, drain, 0)
    group_out.wait_send()
    taps_out.wait_send()

    @pl.when((tp == last) & (seq < spans - 1))
    def _():
        tail_next.wait_send()

    @pl.when(has_tail & (k == 1))
    def _():
        @pl.when(has_left)
        def _():
            tail_left.wait_send()

        tail_sib.wait_send()

    for m, core in sends:
        @pl.when(c != servers[m])
        def _():
            w_far(m, core).wait_send()

    for e in range(1, spans):
        @pl.when(seq + e < spans)
        def _():
            for part in state_to(e):
                part.wait_send()

    def sums_left(chip, carry):
        sq_copy(chip).wait_send()

        @pl.when(c != server_of(chip))
        def _():
            mixed_far(chip).wait_send()

        return carry

    lax.fori_loop(0, n, sums_left, 0)

    @pl.when(serving)
    def _():
        for e in range(spans):
            w_near[e].wait_send()

        def far_left(m, carry):
            q_drain(m)
            return carry

        lax.fori_loop(0, far, far_left, 0)

        def near_left(src, carry):
            for slot in range(2):
                mixed_near(slot, src).wait_send()
            return carry

        lax.fori_loop(0, n, near_left, 0)

        def results_left(q, carry):
            for core in range(2):
                result_far(q, core).wait_send()
            result_near(q).wait_send()
            return carry

        lax.fori_loop(0, spans, results_left, 0)


def mixer(hidden, gain, inner, group, step, wout, segments, taps_inner, taps_group, bias, rate, skip, mixer_gain, heads, count, n, spans, ns):
    rows, width = hidden.shape
    inner_dev = inner.shape[0] * inner.shape[1] // width
    own = inner_dev // 2
    cols = inner_dev + 3 * LANES
    half = wout.shape[1] // 2
    length = 2 * n * rows
    vmem = pl.BlockSpec(memory_space=pltpu.VMEM)
    anywhere = pl.BlockSpec(memory_space=pl.ANY)
    scalars = pl.BlockSpec(memory_space=pltpu.SMEM)
    dma = pltpu.SemaphoreType.DMA
    bits = max(1, spans.bit_length() - 1)
    bf16, f32 = jnp.bfloat16, jnp.float32
    return pl.pallas_call(
        functools.partial(mixer_kernel, n, spans, ns, heads, count),
        out_shape=jax.ShapeDtypeStruct(hidden.shape, bf16),
        in_specs=[vmem, vmem, anywhere, anywhere, vmem, anywhere] + [vmem] * 3 + [scalars] * 3 + [vmem],
        out_specs=vmem,
        scratch_shapes=[
            pltpu.VMEM((n, 2, ns, rows, width // ns), bf16),
            pltpu.VMEM((16, width), bf16),
            pltpu.VMEM((16, width), bf16),
            pltpu.VMEM(inner.shape, bf16),
            pltpu.VMEM((2,) + group.shape, bf16),
            pltpu.VMEM((2, 8, LANES), f32),
            pltpu.VMEM((8, own + 2 * LANES), f32),
            pltpu.VMEM((width, cols), bf16),
            pltpu.VMEM((length, cols), f32),
            pltpu.VMEM((8, own + 2 * LANES), f32),
            pltpu.VMEM((2 * n, spans, wout.shape[0], half // spans), bf16),
            pltpu.VMEM((length, own), f32),
            pltpu.VMEM((length, LANES), bf16),
            pltpu.VMEM((length, LANES), f32),
            pltpu.VMEM((LANES, own), f32),
            pltpu.VMEM((1, LANES), f32),
            pltpu.VMEM((LANES, own), bf16),
            pltpu.VMEM((8, own), f32),
            pltpu.VMEM((spans, LANES, own), bf16),
            pltpu.VMEM((spans, 8, own), f32),
            pltpu.VMEM((2, n, 2 * rows, LANES), f32),
            pltpu.VMEM((n, 2 * rows, own), bf16),
            pltpu.VMEM((2, 2 * n, 2 * rows, own), bf16),
            pltpu.VMEM((2, spans, 2 * rows, half // spans), bf16),
            pltpu.VMEM((2, spans, rows, half // spans), bf16),
            dma((n, ns)), dma((n, ns)), dma((n, ns)), dma((n, ns)), dma((n, ns)), dma((n, ns)),
            dma((3,)), dma((1,)), dma((2,)), dma((2,)),
            dma((2 + n // 2, max(2, spans))), dma((2 * n,)), dma((2 * n, spans, bits)), dma((2 * n, spans)), dma((3,)),
            dma((2, spans)), dma((2, spans)), dma((n,)), dma((n,)),
            dma((n,)), dma((2, n)), dma((2, n)), dma((2, n)), dma((spans, 3)), dma((2, spans)),
        ],
        compiler_params=pltpu.CompilerParams(
            collective_id=0, has_side_effects=True, vmem_limit_bytes=60 << 20
        ),
        cost_estimate=pl.CostEstimate(
            flops=24_000_000_000, bytes_accessed=12_000_000, transcendentals=4_000_000
        ),
        name="mixer",
    )(hidden, gain, inner, group, step, wout, segments, taps_inner, taps_group, bias, rate, skip, mixer_gain)


def by_row(weight):
    width, pair, cols = weight.shape
    tiles = cols // LANES
    return weight.reshape(width, pair, tiles, LANES).transpose(0, 2, 1, 3).reshape(-1, LANES)


def body(
    hidden,
    norm_gain,
    inner_weight,
    group_weight,
    step_weight,
    step_bias,
    decay_rate,
    filter_inner,
    filter_group,
    skip_gain,
    mixer_gain,
    output_weight,
    segment_ids,
):
    spans, chips = lax.axis_size("seq"), lax.axis_size("tp") // 2
    return mixer(
        hidden, norm_gain.reshape(-1, LANES), by_row(inner_weight), group_weight, step_weight.T, output_weight,
        segment_ids.reshape(-1, STRETCH), filter_inner, filter_group, step_bias, decay_rate, skip_gain,
        mixer_gain.reshape(-1, LANES), step_weight.shape[1], filter_inner.shape[0], chips, spans, 4,
    )


def solution(mesh):
    in_specs = (
        P(("seq", "tp"), None),
        P(),
        P(None, None, "tp"),
        P(None, "tp"),
        P(None, "tp"),
        P("tp"),
        P("tp"),
        P(None, "tp"),
        P(None, "tp"),
        P("tp"),
        P("tp"),
        P("tp", None),
        P(),
    )
    out_specs = P(("seq", "tp"), None)
    return jax.shard_map(body, mesh=mesh, in_specs=in_specs, out_specs=out_specs, check_vma=False)
```

```python
import functools
import jax
import jax.numpy as jnp
from jax import lax
from jax.experimental import pallas as pl
from jax.experimental.pallas import tpu as pltpu
from jax.sharding import PartitionSpec as P

EPS = 1e-05
LANES = 128
STRETCH = 128
HIGH = lax.Precision.HIGHEST
MESH = pl.DeviceIdType.MESH


def silu(v):
    return v / (1.0 + jnp.exp(-v))


def widen(cols, heads, head_dim):
    rows = cols.shape[0]
    parts = [jnp.broadcast_to(cols[:, h : h + 1], (rows, head_dim)) for h in range(heads)]
    return jnp.concatenate(parts, axis=1)


def dot16(a, b, dims=((1,), (0,))):
    a, b = a.astype(jnp.bfloat16), b.astype(jnp.bfloat16)
    return lax.dot_general(a, b, (dims, ((), ())), preferred_element_type=jnp.float32)


def segment_marks(segments, first, i):
    shape = (8, STRETCH)

    def line(at):
        ids = segments[pl.ds(jnp.maximum(at, 0), 1), :].astype(jnp.float32)
        return jnp.broadcast_to(jnp.where(at >= 0, ids, -1.0), shape)

    now, past = line(first + i), line(first + i - 1)
    lane = lax.broadcasted_iota(jnp.int32, shape, 1)
    row = lax.broadcasted_iota(jnp.int32, shape, 0)
    end = slice(STRETCH - 1, STRETCH)
    marks = now
    for back in range(1, 4):
        other = jnp.where(lane < back, pltpu.roll(past, back, 1), pltpu.roll(now, back, 1))
        marks = jnp.where(row == back, (now == other).astype(jnp.float32), marks)
    for at, other in ((4, past[:, end]), (5, now[:, end])):
        marks = jnp.where(row == at, (now == other).astype(jnp.float32), marks)
    return marks.T, now[0:1]


def head_line(values, heads, width, reach):
    lane = lax.broadcasted_iota(jnp.int32, (1, width), 1)
    line = jnp.zeros((1, width), jnp.float32)
    for h in range(heads):
        line = jnp.where((lane >= h * reach) & (lane < (h + 1) * reach), values[h], line)
    return line


def flat(ref):
    return jnp.concatenate([ref[i : i + 1, :] for i in range(ref.shape[0])], axis=1)


def scan_stretch(
    count, heads, head_dim, inner, states, at,
    proj, segments, first, i, taps, bias, rate, skip, y_out, c_out, entry_out, edge, fresh_out, decay_out,
):
    aux, row_seg = segment_marks(segments, first, i)
    conv = inner + 2 * states
    cur = proj[at, :conv]
    past = proj[pl.ds(pl.multiple_of(jnp.maximum(i * STRETCH - 8, 0), 8), 8), :conv]
    both = jnp.concatenate([jnp.where(i == 0, edge[...], past), cur], axis=0)
    size = STRETCH
    tap = taps[...]
    acc = tap[count - 1 : count] * cur
    for back in range(1, count):
        same = aux[:, back : back + 1]
        acc += tap[count - 1 - back : count - back] * both[8 - back : 8 - back + size] * same
    active = silu(acc)
    x = active[:, :inner]
    b_map = active[:, inner : inner + states]
    c_map = active[:, inner + states :]
    raw = proj[at, conv + inner :] + bias
    step = jnp.maximum(raw, 0.0) + jnp.log1p(jnp.exp(-jnp.abs(raw)))
    log_decay = -step * rate
    row_at = lax.broadcasted_iota(jnp.int32, (size, size), 0)
    col_at = lax.broadcasted_iota(jnp.int32, (size, size), 1)
    causal = row_at >= col_at
    cum = jnp.dot(
        causal.astype(jnp.float32), log_decay, precision=HIGH, preferred_element_type=jnp.float32
    )
    cum_rows = cum.T
    alive, in_last = aux[:, 4:5], aux[:, 5:6]
    last = cum[size - 1 :]
    mask = causal & (aux[:, 0:1] == row_seg)
    xs = x * widen(step, heads, head_dim)
    xs16 = xs.astype(jnp.bfloat16)
    products = dot16(c_map, b_map, ((1,), (1,)))
    parts = []
    for h in range(heads):
        gap = cum[:, h : h + 1] - cum_rows[h : h + 1, :]
        mixing = products * jnp.exp(jnp.where(mask, gap, -1e30))
        parts.append(dot16(mixing, xs16[:, h * head_dim : (h + 1) * head_dim]))
    local = jnp.concatenate(parts, axis=1)
    entry = jnp.exp(cum) * alive
    y_out[at, :] = local + skip * x
    c_out[at, :] = c_map.astype(jnp.bfloat16)
    entry_out[at, :] = entry
    end = jnp.exp(last - cum) * in_last
    fresh_out[i] = dot16(b_map, xs * widen(end, heads, head_dim), ((0,), (0,)))
    decay_out[i] = jnp.broadcast_to(widen(entry[size - 8 :], heads, head_dim)[7:8], (8, inner))


def servers_of(chips):
    return [2 * i + 1 - i % 2 for i in range(chips // 2)]


def mixer_kernel(
    n, spans, ns, heads, count,
    hidden, gain, inner, group, step, wout, segments, taps_inner, taps_group, bias, rate, skip, mixer_gain,
    out,
    buf, mytail, tail, raw, gbuf, gtaps, taps, w, proj, edge, wq,
    y, c_maps, entries, state, fresh, decays, entering, packed, decay, came, came_decay,
    sq, mixed, taken, results, landed,
    rsend, lsend, xsend, rrecv, lrecv, xrecv,
    tsend, trecv, gsend, grecv, wsend, wrecv, qsend, qrecv, local,
    ssend, srecv, esend, erecv, msend, mrecv, nsend, nrecv, osend, orecv,
):
    tp, seq = lax.axis_index("tp"), lax.axis_index("seq")
    c, k = tp // 2, tp % 2
    rows, width = hidden.shape
    dc = width // ns
    sib = {"tp": tp + 1 - 2 * k}
    has_left, has_right = c > 0, c < n - 1
    inner_dev = w.shape[1] - 3 * LANES
    half_cols = inner_dev // 2
    servers = servers_of(n)
    mate = jnp.where(c == 2 * (c // 2), c + 1, c - 1)
    serving = functools.reduce(jnp.logical_or, [c == s for s in servers])
    bits = spans.bit_length() - 1
    half = wout.shape[1] // 2
    quarter = half // spans

    def copy(src, dst, send, recv, dev):
        return pltpu.make_async_remote_copy(
            src_ref=src, dst_ref=dst, send_sem=send, recv_sem=recv, device_id=dev, device_id_type=MESH
        )

    inner_in = pltpu.make_async_copy(inner, raw, local.at[0])
    group_in = pltpu.make_async_copy(group, gbuf.at[k], local.at[1])

    def half_cols_at(core, span):
        return pl.ds(pl.multiple_of(core * half + span * quarter, LANES), quarter)

    own_half = [
        pltpu.make_async_copy(wout.at[:, half_cols_at(k, e)], wq.at[tp, e], wsend.at[0, e])
        for e in range(spans)
    ]
    inner_in.start()
    group_in.start()

    @pl.when(serving)
    def _():
        for part in own_half:
            part.start()

    barrier = pltpu.get_barrier_semaphore()
    peers = 2 * n

    def greet(axis, size, me):
        def hello(i, carry):
            pl.semaphore_signal(
                barrier, inc=1, device_id={axis: lax.rem(me + i, size)}, device_id_type=MESH
            )
            return carry
        lax.fori_loop(1, size, hello, 0)

    greet("tp", peers, tp)
    greet("seq", spans, seq)

    h = hidden[...].astype(jnp.float32)
    scale = lax.rsqrt(jnp.mean(h * h, axis=1, keepdims=True) + EPS)
    gain_line = flat(gain)
    for s in range(ns):
        part = slice(s * dc, (s + 1) * dc)
        normed = (hidden[:, part].astype(jnp.float32) * scale * gain_line[:, part]).astype(jnp.bfloat16)
        buf[c, k, s] = normed
        mytail[:, part] = normed[rows - 16 :]
    pl.semaphore_wait(barrier, peers - 1 + spans - 1)

    def to_right(j, s):
        return copy(buf.at[j, k, s], buf.at[j, k, s], rsend.at[j, s], rrecv.at[j, s], {"tp": lax.rem(tp + 2, peers)})

    def to_left(j, s):
        return copy(buf.at[j, k, s], buf.at[j, k, s], lsend.at[j, s], lrecv.at[j, s], {"tp": lax.rem(tp + peers - 2, peers)})

    def to_sib(j, s):
        return copy(buf.at[j, k, s], buf.at[j, k, s], xsend.at[j, s], xrecv.at[j, s], sib)

    def from_sib(j, s):
        return copy(buf.at[j, 1 - k, s], buf.at[j, 1 - k, s], xsend.at[j, s], xrecv.at[j, s], sib)

    def own(s, carry):
        @pl.when(has_right)
        def _():
            to_right(c, s).start()

        @pl.when(has_left)
        def _():
            to_left(c, s).start()

        to_sib(c, s).start()
        return carry

    def w_far(m, core):
        return copy(
            wout.at[:, half_cols_at(core, seq)], wq.at[tp, seq],
            wsend.at[1 + m, core], wrecv.at[tp], {"tp": 2 * servers[m] + core},
        )

    other = tp + 1 - 2 * k
    w_near = [
        copy(wout.at[:, half_cols_at(1 - k, e)], wq.at[tp, e], wsend.at[1 + len(servers), e], wrecv.at[tp], sib)
        for e in range(spans)
    ]
    near_in = copy(wq.at[other], wq.at[other], wsend.at[0, 0], wrecv.at[other], sib)

    def w_send(m, core, close):
        @pl.when((c != servers[m]) & ((c // 2 == m) == close))
        def _():
            w_far(m, core).start()

    sends = [(m, core) for m in range(len(servers)) for core in range(2)]
    lax.fori_loop(0, ns, own, 0)

    last = peers - 1
    has_tail = seq > 0
    tail_next = copy(mytail, tail, tsend.at[0], trecv.at[0], {"seq": lax.rem(seq + 1, spans)})
    tail_left = copy(tail, tail, tsend.at[1], trecv.at[0], {"tp": lax.rem(tp + peers - 2, peers)})
    tail_sib = copy(tail, tail, tsend.at[2], trecv.at[0], sib)

    @pl.when((tp == last) & (seq < spans - 1))
    def _():
        tail_next.start()

    group_out = copy(group, gbuf.at[k], gsend.at[0], grecv.at[0], sib)
    group_out.start()
    gtaps[k] = jnp.zeros((8, LANES), jnp.float32)
    gtaps[k, :count] = taps_group[...].astype(jnp.float32)
    taps_out = copy(gtaps.at[k], gtaps.at[k], gsend.at[1], grecv.at[1], sib)
    taps_out.start()

    @pl.when(serving)
    def _():
        for part in w_near:
            part.start()

    def far_block(m):
        beyond = lax.rem(4 * (c // 2) + 2 + m, peers)
        return jnp.where(m < 2, 2 * mate + m, beyond)

    def wq_part(j, span):
        return wq.at[j, span]

    def q_copy(j, origin, b):
        return copy(
            wq_part(j, origin), wq_part(j, origin), qsend.at[j, origin, b], qrecv.at[j, origin],
            {"seq": seq ^ (1 << b)},
        )

    def q_spread(m):
        j = far_block(m)
        copy(wq_part(j, seq), wq_part(j, seq), wsend.at[0, 0], wrecv.at[j], sib).wait_recv()
        for b in range(bits):
            q_copy(j, seq, b).start()

    def q_forwards(up):
        found = []
        for e in range(1, spans):
            top, low = e.bit_length() - 1, (e & -e).bit_length() - 1
            targets = [b for b in range(bits) if (b > top if up else b < low)]
            found.append((e, targets))
        return found

    def q_forward(m):
        j = far_block(m)
        for up in (True, False):
            @pl.when(j % 2 == (0 if up else 1))
            def _():
                for e, targets in q_forwards(up):
                    if targets:
                        origin = seq ^ e
                        part = wq_part(j, origin)
                        copy(part, part, wsend.at[0, 0], qrecv.at[j, origin], sib).wait_recv()
                        for b in targets:
                            q_copy(j, origin, b).start()

    def q_drain(m):
        j = far_block(m)
        for b in range(bits):
            q_copy(j, seq, b).wait_send()
        for up in (True, False):
            @pl.when(j % 2 == (0 if up else 1))
            def _():
                for e, targets in q_forwards(up):
                    for b in targets:
                        q_copy(j, seq ^ e, b).wait_send()

    inner_in.wait()
    lane_tiles = inner_dev // 2 // LANES
    size = 256
    depth = size // (2 * lane_tiles)
    row_at = lax.broadcasted_iota(jnp.int32, (size, size), 0)
    col_at = lax.broadcasted_iota(jnp.int32, (size, size), 1)
    kk, jj, tt = row_at % depth, row_at // (depth * lane_tiles), row_at // depth % lane_tiles
    perm = (col_at == kk * (2 * lane_tiles) + tt * 2 + jj).astype(jnp.float32).astype(jnp.bfloat16)
    gate_at = half_cols + 2 * LANES

    def sort(i, carry):
        block = raw[pl.ds(pl.multiple_of(i * size, size), size), :]
        out = jnp.dot(perm, block, preferred_element_type=jnp.float32).astype(jnp.bfloat16)
        at = pl.ds(pl.multiple_of(i * depth, depth), depth)
        for t in range(lane_tiles):
            w[at, gate_at + t * LANES : gate_at + (t + 1) * LANES] = out[t * depth : (t + 1) * depth]
            scan = out[(lane_tiles + t) * depth : (lane_tiles + t + 1) * depth]
            w[at, t * LANES : (t + 1) * LANES] = scan
        return carry

    lax.fori_loop(0, raw.shape[0] // size, sort, 0)
    pick_at = [lax.broadcasted_iota(jnp.int32, (heads, LANES), d) for d in range(2)]
    pick = (pick_at[0] == pick_at[1]).astype(jnp.float32)

    def turn(i, carry):
        at = pl.ds(pl.multiple_of(i * size, size), size)
        out = dot16(step[:, at], pick, ((0,), (0,)))
        w[at, gate_at + half_cols :] = out.astype(jnp.bfloat16)
        return carry

    lax.fori_loop(0, width // size, turn, 0)
    group_in.wait()
    copy(gbuf.at[1 - k], gbuf.at[1 - k], gsend.at[0], grecv.at[0], sib).wait_recv()
    copy(gtaps.at[1 - k], gtaps.at[1 - k], gsend.at[1], grecv.at[1], sib).wait_recv()
    taps[:count, :half_cols] = taps_inner[...].astype(jnp.float32)
    for m in range(2):
        w[:, half_cols + m * LANES : half_cols + (m + 1) * LANES] = gbuf[m]
        taps[:, half_cols + m * LANES : half_cols + (m + 1) * LANES] = gtaps[m]

    def arrivals(i):
        d, s = i // ns, i % ns

        @pl.when(c - d >= 0)
        def _():
            j = c - d
            copy(buf.at[j, k, s], buf.at[j, k, s], rsend.at[j, s], rrecv.at[j, s], sib).wait_recv()

            @pl.when(has_right)
            def _():
                to_right(j, s).start()

            to_sib(j, s).start()

        @pl.when(c + d < n)
        def _():
            j = c + d
            copy(buf.at[j, k, s], buf.at[j, k, s], lsend.at[j, s], lrecv.at[j, s], sib).wait_recv()

            @pl.when(has_left)
            def _():
                to_left(j, s).start()

            to_sib(j, s).start()

    def compute(i):
        d, s = i // ns, i % ns

        def side(which, carry):
            j = c - d + 2 * d * which

            @pl.when((j >= 0) & (j < n) & ((which == 0) | (d > 0)))
            def _():
                from_sib(j, s).wait_recv()
                x = buf[j, :, s].reshape(2 * rows, dc)
                at = pl.ds(pl.multiple_of(s * dc, dc), dc)
                out = jnp.dot(x, w[at, :], preferred_element_type=jnp.float32)
                place = pl.ds(pl.multiple_of(j * 2 * rows, 2 * rows), 2 * rows)

                @pl.when(s == 0)
                def _():
                    proj[place, :] = out

                @pl.when(s > 0)
                def _():
                    proj[place, :] += out

            return carry

        lax.fori_loop(0, 2, side, 0)

    far = peers - 2
    first_spread, first_forward = 2 * ns - 1, 2 * ns + 2
    near = min(2, far)

    conv = half_cols + 2 * LANES
    inner_own = half_cols
    head_dim = inner_own // heads
    length = peers * rows
    per_chip = 2 * rows // STRETCH
    bias_line = head_line(bias, heads, LANES, 1)
    rate_line = head_line(rate, heads, LANES, 1)
    skip_line = head_line(skip, heads, inner_own, head_dim)
    first = seq * (length // STRETCH)

    def take_tail():
        @pl.when(has_tail)
        def _():
            @pl.when(k == 0)
            def _():
                copy(tail, tail, tsend.at[1], trecv.at[0], sib).wait_recv()

            edge[...] = jnp.dot(tail[...], w[:, :conv], preferred_element_type=jnp.float32)[8:]

        @pl.when(jnp.logical_not(has_tail))
        def _():
            edge[...] = jnp.zeros_like(edge)

    def scan_slot(d, u):
        far_side = d > 0
        lowest = (c - d == 0) & far_side | (c == 0) & (d == 1)
        chip = jnp.where(u == 0, c - d, jnp.where(u == 1, c - d + 1, jnp.where(u < 4, c + d, 0)))
        part = jnp.where((u == 0) | (u == 3), 1, 0)
        ready = jnp.where(u == 0, c - d >= 0, jnp.where(u == 1, far_side & (c - d >= 0), jnp.where(u < 4, far_side & (c + d < n), lowest)))

        @pl.when(ready & (part < per_chip))
        def _():
            @pl.when(u == 4)
            def _():
                take_tail()

            i = chip * per_chip + part
            at = pl.ds(pl.multiple_of(i * STRETCH, STRETCH), STRETCH)
            scan_stretch(
                count, heads, head_dim, inner_own, LANES, at,
                proj, segments, first, i, taps, bias_line, rate_line, skip_line, y, c_maps, entries, edge, fresh, decays,
            )

    def scans(i):
        d, u = i // ns - 1, i % ns

        def one(slot, carry):
            scan_slot(d, slot)
            return carry

        @pl.when((d >= 0) & (u < 4))
        def _():
            lax.fori_loop(u, jnp.where(u == 3, 5, u + 1), one, 0)

    def item(i, carry):
        @pl.when((i >= ns) & (i < n * ns))
        def _():
            arrivals(i)

        @pl.when((i == ns + 1) & has_tail & (k == 1))
        def _():
            copy(tail, tail, tsend.at[1], trecv.at[0], sib).wait_recv()

            @pl.when(has_left)
            def _():
                tail_left.start()

            tail_sib.start()

        for close, when in ((True, ns), (False, 3 * ns)):
            @pl.when(i == when)
            def _():
                for m, core in sends:
                    w_send(m, core, close)

        @pl.when(i <= n * ns)
        def _():
            compute(i - 1)

        scans(i)

        @pl.when(serving & (i >= first_spread) & (i < first_spread + near))
        def _():
            q_spread(i - first_spread)

        @pl.when(serving & (i >= first_forward) & (i < first_forward + near))
        def _():
            q_forward(i - first_forward)

        return carry

    lax.fori_loop(1, n * ns + 4, item, 0)

    packed_sum = jnp.zeros(state.shape, jnp.float32)
    whole = jnp.ones((8, inner_own), jnp.float32)
    for i in range(length // STRETCH):
        packed_sum = decays[i, 0:1] * packed_sum + fresh[i]
        whole = whole * decays[i]

    packed[...] = packed_sum.astype(jnp.bfloat16)
    decay[...] = whole

    def state_to(e):
        dev = {"seq": lax.rem(seq + e, spans)}
        return (
            copy(packed, came.at[e], ssend.at[0, e], srecv.at[0, e], dev),
            copy(decay, came_decay.at[e], ssend.at[1, e], srecv.at[1, e], dev),
        )

    for e in range(1, spans):
        @pl.when(seq + e < spans)
        def _():
            for part in state_to(e):
                part.start()

    def over(act):
        def one(m, carry):
            act(m)
            return carry
        return one

    @pl.when(serving)
    def _():
        lax.fori_loop(near, far, over(q_spread), 0)

    state[...] = jnp.zeros_like(state)
    for e in range(spans - 1, 0, -1):
        @pl.when(e <= seq)
        def _():
            for part in state_to(e):
                part.wait_recv()
            state[...] = came[e].astype(jnp.float32) + came_decay[e, 0:1] * state[...]

    def enter(i, carry):
        entering[i] = state[...].astype(jnp.bfloat16)
        state[...] = decays[i, 0:1] * state[...] + fresh[i]
        return carry

    lax.fori_loop(0, length // STRETCH, enter, 0)

    block = 2 * rows
    pairs = n // 2

    def chip_at(i):
        m = lax.rem(i, pairs)
        first = i < pairs
        return jnp.where(first, 2 * m + m % 2, 2 * m + 1 - m % 2)

    def rows_of(chip):
        return pl.ds(pl.multiple_of(chip * block, block), block)

    def sq_copy(chip):
        return copy(sq.at[0, chip], sq.at[1, chip], esend.at[chip], erecv.at[chip], sib)

    def gate_block(i, carry):
        chip = chip_at(i)
        at = rows_of(chip)
        maps = c_maps[at, :]
        carried = [
            dot16(maps[u * STRETCH : (u + 1) * STRETCH], entering[chip * per_chip + u])
            for u in range(per_chip)
        ]
        carried = jnp.concatenate(carried, axis=0) * widen(entries[at, :], heads, head_dim)
        gated = (y[at, :] + carried) * silu(proj[at, conv : conv + inner_own])
        y[at, :] = gated
        sums = jnp.sum(gated * gated, axis=1, keepdims=True)
        sq[0, chip] = jnp.broadcast_to(sums, (block, LANES))
        sq_copy(chip).start()
        return carry

    lax.fori_loop(0, n, gate_block, 0)

    def server_of(chip):
        m = chip // 2
        return 2 * m + 1 - m % 2

    def slot_of(chip):
        return jnp.where(chip == server_of(chip), 1, 0)

    def mixed_far(chip):
        return copy(
            mixed.at[chip], taken.at[slot_of(chip), tp], msend.at[chip], mrecv.at[slot_of(chip), c],
            {"tp": lax.rem(2 * server_of(chip) + k, peers)},
        )

    def mixed_near(slot, src):
        place = taken.at[slot, 2 * src + k]
        return copy(place, place, nsend.at[slot, src], nrecv.at[slot, src], sib)

    mix_line = flat(mixer_gain)

    def mix_block(i, carry):
        chip = chip_at(i)
        at = rows_of(chip)
        sq_copy(chip).wait_recv()
        mean = (sq[0, chip] + sq[1, chip]) / (2 * inner_own)
        factor = lax.rsqrt(mean + EPS)
        wide = jnp.concatenate([factor] * (inner_own // LANES), axis=1)
        done = (y[at, :] * wide * mix_line).astype(jnp.bfloat16)

        @pl.when(c != server_of(chip))
        def _():
            mixed[chip] = done
            mixed_far(chip).start()

        @pl.when(c == server_of(chip))
        def _():
            taken[slot_of(chip), tp] = done
            mixed_near(slot_of(chip), c).start()

        return carry

    lax.fori_loop(0, n, mix_block, 0)

    def result_far(q, core):
        return copy(
            results.at[0, q, pl.ds(core * rows, rows)], landed.at[k, q], osend.at[q, core], orecv.at[k, q],
            {"tp": 2 * mate + core},
        )

    def result_near(q):
        return copy(
            results.at[1, q, pl.ds(pl.multiple_of((1 - k) * rows, rows), rows)], landed.at[k, q],
            osend.at[q, 2], orecv.at[k, q], sib,
        )

    @pl.when(serving)
    def _():
        for e in range(spans):
            own_half[e].wait()
        near_in.wait_recv()
        lax.fori_loop(near, max(near, far - 2), over(q_forward), 0)

        def collect(slot):
            def relay(m, carry):
                src = lax.rem(c + m, n)
                place = taken.at[slot, 2 * src + k]
                copy(place, place, nsend.at[slot, src], mrecv.at[slot, src], sib).wait_recv()
                mixed_near(slot, src).start()
                return carry

            lax.fori_loop(1, n, relay, 0)

            def from_near(src, carry):
                place = taken.at[slot, 2 * src + 1 - k]
                copy(place, place, nsend.at[slot, src], nrecv.at[slot, src], sib).wait_recv()
                return carry

            lax.fori_loop(0, n, from_near, 0)

        def multiply(slot, q):
            sums = jnp.zeros((block, wq.shape[3]), jnp.float32)
            for j in range(peers):
                sums += jnp.dot(taken[slot, j], wq[j, q], preferred_element_type=jnp.float32)
            return sums.astype(jnp.bfloat16)

        collect(0)

        def for_mate(e, carry):
            q = seq ^ e

            @pl.when(e == 1)
            def _():
                lax.fori_loop(max(near, far - 2), far, over(q_forward), 0)

            def part_in(m, carry):
                j = far_block(m)
                ends = jnp.where(j % 2 == 0, 2 * e >= spans, e % 2 == 1)

                @pl.when((e > 0) & ends)
                def _():
                    part = wq_part(j, q)
                    copy(part, part, wsend.at[0, 0], qrecv.at[j, q], sib).wait_recv()

                return carry

            lax.fori_loop(0, far, part_in, 0)
            results[0, q] = multiply(0, q)
            for core in range(2):
                result_far(q, core).start()
            return carry

        lax.fori_loop(0, spans, for_mate, 0)
        collect(1)

        def for_own(q, carry):
            results[1, q] = multiply(1, q)
            result_near(q).start()
            landed[k, q] = results[1, q, pl.ds(pl.multiple_of(k * rows, rows), rows)]
            return carry

        lax.fori_loop(0, spans, for_own, 0)

    def finish(core, q):
        place = landed.at[core, q]
        arrival = copy(place, place, osend.at[q, 0], orecv.at[core, q], sib)

        @pl.when(jnp.logical_not(serving) | (k != core))
        def _():
            arrival.wait_recv()

        at = pl.ds(core * half + q * quarter, quarter)
        out[:, at] = (hidden[:, at].astype(jnp.float32) + landed[core, q].astype(jnp.float32)).astype(jnp.bfloat16)

    for q in range(spans):
        for core in range(2):
            finish(core, q)

    def drain(i, carry):
        j, s = i // ns, i % ns
        to_sib(j, s).wait_send()

        @pl.when(has_right & (j <= c))
        def _():
            to_right(j, s).wait_send()

        @pl.when(has_left & (j >= c))
        def _():
            to_left(j, s).wait_send()

        return carry

    lax.fori_loop(0, n * ns, drain, 0)
    group_out.wait_send()
    taps_out.wait_send()

    @pl.when((tp == last) & (seq < spans - 1))
    def _():
        tail_next.wait_send()

    @pl.when(has_tail & (k == 1))
    def _():
        @pl.when(has_left)
        def _():
            tail_left.wait_send()

        tail_sib.wait_send()

    for m, core in sends:
        @pl.when(c != servers[m])
        def _():
            w_far(m, core).wait_send()

    for e in range(1, spans):
        @pl.when(seq + e < spans)
        def _():
            for part in state_to(e):
                part.wait_send()

    def sums_left(chip, carry):
        sq_copy(chip).wait_send()

        @pl.when(c != server_of(chip))
        def _():
            mixed_far(chip).wait_send()

        return carry

    lax.fori_loop(0, n, sums_left, 0)

    @pl.when(serving)
    def _():
        for e in range(spans):
            w_near[e].wait_send()

        def far_left(m, carry):
            q_drain(m)
            return carry

        lax.fori_loop(0, far, far_left, 0)

        def near_left(src, carry):
            for slot in range(2):
                mixed_near(slot, src).wait_send()
            return carry

        lax.fori_loop(0, n, near_left, 0)

        def results_left(q, carry):
            for core in range(2):
                result_far(q, core).wait_send()
            result_near(q).wait_send()
            return carry

        lax.fori_loop(0, spans, results_left, 0)


def mixer(hidden, gain, inner, group, step, wout, segments, taps_inner, taps_group, bias, rate, skip, mixer_gain, heads, count, n, spans, ns):
    rows, width = hidden.shape
    inner_dev = inner.shape[0] * inner.shape[1] // width
    own = inner_dev // 2
    cols = inner_dev + 3 * LANES
    half = wout.shape[1] // 2
    length = 2 * n * rows
    vmem = pl.BlockSpec(memory_space=pltpu.VMEM)
    anywhere = pl.BlockSpec(memory_space=pl.ANY)
    scalars = pl.BlockSpec(memory_space=pltpu.SMEM)
    dma = pltpu.SemaphoreType.DMA
    bits = max(1, spans.bit_length() - 1)
    bf16, f32 = jnp.bfloat16, jnp.float32
    return pl.pallas_call(
        functools.partial(mixer_kernel, n, spans, ns, heads, count),
        out_shape=jax.ShapeDtypeStruct(hidden.shape, bf16),
        in_specs=[vmem, vmem, anywhere, anywhere, vmem, anywhere] + [vmem] * 3 + [scalars] * 3 + [vmem],
        out_specs=vmem,
        scratch_shapes=[
            pltpu.VMEM((n, 2, ns, rows, width // ns), bf16),
            pltpu.VMEM((16, width), bf16),
            pltpu.VMEM((16, width), bf16),
            pltpu.VMEM(inner.shape, bf16),
            pltpu.VMEM((2,) + group.shape, bf16),
            pltpu.VMEM((2, 8, LANES), f32),
            pltpu.VMEM((8, own + 2 * LANES), f32),
            pltpu.VMEM((width, cols), bf16),
            pltpu.VMEM((length, cols), f32),
            pltpu.VMEM((8, own + 2 * LANES), f32),
            pltpu.VMEM((2 * n, spans, wout.shape[0], half // spans), bf16),
            pltpu.VMEM((length, own), f32),
            pltpu.VMEM((length, LANES), bf16),
            pltpu.VMEM((length, LANES), f32),
            pltpu.VMEM((LANES, own), f32),
            pltpu.VMEM((length // STRETCH, LANES, own), f32),
            pltpu.VMEM((length // STRETCH, 8, own), f32),
            pltpu.VMEM((length // STRETCH, LANES, own), bf16),
            pltpu.VMEM((LANES, own), bf16),
            pltpu.VMEM((8, own), f32),
            pltpu.VMEM((spans, LANES, own), bf16),
            pltpu.VMEM((spans, 8, own), f32),
            pltpu.VMEM((2, n, 2 * rows, LANES), f32),
            pltpu.VMEM((n, 2 * rows, own), bf16),
            pltpu.VMEM((2, 2 * n, 2 * rows, own), bf16),
            pltpu.VMEM((2, spans, 2 * rows, half // spans), bf16),
            pltpu.VMEM((2, spans, rows, half // spans), bf16),
            dma((n, ns)), dma((n, ns)), dma((n, ns)), dma((n, ns)), dma((n, ns)), dma((n, ns)),
            dma((3,)), dma((1,)), dma((2,)), dma((2,)),
            dma((2 + n // 2, max(2, spans))), dma((2 * n,)), dma((2 * n, spans, bits)), dma((2 * n, spans)), dma((3,)),
            dma((2, spans)), dma((2, spans)), dma((n,)), dma((n,)),
            dma((n,)), dma((2, n)), dma((2, n)), dma((2, n)), dma((spans, 3)), dma((2, spans)),
        ],
        compiler_params=pltpu.CompilerParams(
            collective_id=0, has_side_effects=True, vmem_limit_bytes=60 << 20
        ),
        cost_estimate=pl.CostEstimate(
            flops=24_000_000_000, bytes_accessed=12_000_000, transcendentals=4_000_000
        ),
        name="mixer",
    )(hidden, gain, inner, group, step, wout, segments, taps_inner, taps_group, bias, rate, skip, mixer_gain)


def by_row(weight):
    width, pair, cols = weight.shape
    tiles = cols // LANES
    return weight.reshape(width, pair, tiles, LANES).transpose(0, 2, 1, 3).reshape(-1, LANES)


def body(
    hidden,
    norm_gain,
    inner_weight,
    group_weight,
    step_weight,
    step_bias,
    decay_rate,
    filter_inner,
    filter_group,
    skip_gain,
    mixer_gain,
    output_weight,
    segment_ids,
):
    spans, chips = lax.axis_size("seq"), lax.axis_size("tp") // 2
    return mixer(
        hidden, norm_gain.reshape(-1, LANES), by_row(inner_weight), group_weight, step_weight.T, output_weight,
        segment_ids.reshape(-1, STRETCH), filter_inner, filter_group, step_bias, decay_rate, skip_gain,
        mixer_gain.reshape(-1, LANES), step_weight.shape[1], filter_inner.shape[0], chips, spans, 4,
    )


def solution(mesh):
    in_specs = (
        P(("seq", "tp"), None),
        P(),
        P(None, None, "tp"),
        P(None, "tp"),
        P(None, "tp"),
        P("tp"),
        P("tp"),
        P(None, "tp"),
        P(None, "tp"),
        P("tp"),
        P("tp"),
        P("tp", None),
        P(),
    )
    out_specs = P(("seq", "tp"), None)
    return jax.shard_map(body, mesh=mesh, in_specs=in_specs, out_specs=out_specs, check_vma=False)
```

```python
import functools
import jax
import jax.numpy as jnp
from jax import lax
from jax.experimental import pallas as pl
from jax.experimental.pallas import tpu as pltpu
from jax.sharding import PartitionSpec as P

EPS = 1e-05
LANES = 128
STRETCH = 128
HIGH = lax.Precision.HIGHEST
MESH = pl.DeviceIdType.MESH


def silu(v):
    return v / (1.0 + jnp.exp(-v))


def widen(cols, heads, head_dim):
    rows = cols.shape[0]
    parts = [jnp.broadcast_to(cols[:, h : h + 1], (rows, head_dim)) for h in range(heads)]
    return jnp.concatenate(parts, axis=1)


def dot16(a, b, dims=((1,), (0,))):
    a, b = a.astype(jnp.bfloat16), b.astype(jnp.bfloat16)
    return lax.dot_general(a, b, (dims, ((), ())), preferred_element_type=jnp.float32)


def segment_marks(segments, first, i):
    shape = (8, STRETCH)

    def line(at):
        ids = segments[pl.ds(jnp.maximum(at, 0), 1), :].astype(jnp.float32)
        return jnp.broadcast_to(jnp.where(at >= 0, ids, -1.0), shape)

    now, past = line(first + i), line(first + i - 1)
    lane = lax.broadcasted_iota(jnp.int32, shape, 1)
    row = lax.broadcasted_iota(jnp.int32, shape, 0)
    end = slice(STRETCH - 1, STRETCH)
    marks = now
    for back in range(1, 4):
        other = jnp.where(lane < back, pltpu.roll(past, back, 1), pltpu.roll(now, back, 1))
        marks = jnp.where(row == back, (now == other).astype(jnp.float32), marks)
    for at, other in ((4, past[:, end]), (5, now[:, end])):
        marks = jnp.where(row == at, (now == other).astype(jnp.float32), marks)
    return marks.T, now[0:1]


def head_line(values, heads, width, reach):
    lane = lax.broadcasted_iota(jnp.int32, (1, width), 1)
    line = jnp.zeros((1, width), jnp.float32)
    for h in range(heads):
        line = jnp.where((lane >= h * reach) & (lane < (h + 1) * reach), values[h], line)
    return line


def flat(ref):
    return jnp.concatenate([ref[i : i + 1, :] for i in range(ref.shape[0])], axis=1)


def scan_stretch(
    count, heads, head_dim, inner, states, at,
    proj, segments, first, i, taps, bias, rate, skip, y_out, c_out, entry_out, edge, fresh_out, decay_out,
):
    aux, row_seg = segment_marks(segments, first, i)
    conv = inner + 2 * states
    cur = proj[at, :conv]
    past = proj[pl.ds(pl.multiple_of(jnp.maximum(i * STRETCH - 8, 0), 8), 8), :conv]
    both = jnp.concatenate([jnp.where(i == 0, edge[...], past), cur], axis=0)
    size = STRETCH
    tap = taps[...]
    acc = tap[count - 1 : count] * cur
    for back in range(1, count):
        same = aux[:, back : back + 1]
        acc += tap[count - 1 - back : count - back] * both[8 - back : 8 - back + size] * same
    active = silu(acc)
    x = active[:, :inner]
    b_map = active[:, inner : inner + states]
    c_map = active[:, inner + states :]
    raw = proj[at, conv + inner :] + bias
    step = jnp.maximum(raw, 0.0) + jnp.log1p(jnp.exp(-jnp.abs(raw)))
    log_decay = -step * rate
    row_at = lax.broadcasted_iota(jnp.int32, (size, size), 0)
    col_at = lax.broadcasted_iota(jnp.int32, (size, size), 1)
    causal = row_at >= col_at
    cum = jnp.dot(
        causal.astype(jnp.float32), log_decay, precision=HIGH, preferred_element_type=jnp.float32
    )
    cum_rows = cum.T
    alive, in_last = aux[:, 4:5], aux[:, 5:6]
    last = cum[size - 1 :]
    mask = causal & (aux[:, 0:1] == row_seg)
    xs = x * widen(step, heads, head_dim)
    xs16 = xs.astype(jnp.bfloat16)
    products = dot16(c_map, b_map, ((1,), (1,)))
    parts = []
    for h in range(heads):
        gap = cum[:, h : h + 1] - cum_rows[h : h + 1, :]
        mixing = products * jnp.exp(jnp.where(mask, gap, -1e30))
        parts.append(dot16(mixing, xs16[:, h * head_dim : (h + 1) * head_dim]))
    local = jnp.concatenate(parts, axis=1)
    entry = jnp.exp(cum) * alive
    y_out[at, :] = local + skip * x
    c_out[at, :] = c_map.astype(jnp.bfloat16)
    entry_out[at, :] = entry
    end = jnp.exp(last - cum) * in_last
    fresh_out[i] = dot16(b_map, xs * widen(end, heads, head_dim), ((0,), (0,)))
    decay_out[i] = jnp.broadcast_to(widen(entry[size - 8 :], heads, head_dim)[7:8], (8, inner))


def servers_of(chips):
    return [2 * i + 1 - i % 2 for i in range(chips // 2)]


def mixer_kernel(
    n, spans, ns, heads, count,
    hidden, gain, inner, group, step, wout, segments, taps_inner, taps_group, bias, rate, skip, mixer_gain,
    out,
    buf, mytail, tail, raw, gbuf, gtaps, taps, w, proj, edge, wq,
    y, c_maps, entries, state, fresh, decays, entering, packed, decay, came, came_decay,
    sq, mixed, taken, results, landed,
    rsend, lsend, xsend, rrecv, lrecv, xrecv,
    tsend, trecv, gsend, grecv, wsend, wrecv, qsend, qrecv, local,
    ssend, srecv, esend, erecv, msend, mrecv, nsend, nrecv, osend, orecv,
):
    tp, seq = lax.axis_index("tp"), lax.axis_index("seq")
    c, k = tp // 2, tp % 2
    rows, width = hidden.shape
    dc = width // ns
    sib = {"tp": tp + 1 - 2 * k}
    has_left, has_right = c > 0, c < n - 1
    inner_dev = w.shape[1] - 3 * LANES
    half_cols = inner_dev // 2
    servers = servers_of(n)
    mate = jnp.where(c == 2 * (c // 2), c + 1, c - 1)
    serving = functools.reduce(jnp.logical_or, [c == s for s in servers])
    bits = spans.bit_length() - 1
    half = wout.shape[1] // 2
    quarter = half // spans

    def copy(src, dst, send, recv, dev):
        return pltpu.make_async_remote_copy(
            src_ref=src, dst_ref=dst, send_sem=send, recv_sem=recv, device_id=dev, device_id_type=MESH
        )

    inner_in = pltpu.make_async_copy(inner, raw, local.at[0])
    group_in = pltpu.make_async_copy(group, gbuf.at[k], local.at[1])

    def half_cols_at(core, span):
        return pl.ds(pl.multiple_of(core * half + span * quarter, LANES), quarter)

    own_half = [
        pltpu.make_async_copy(wout.at[:, half_cols_at(k, e)], wq.at[tp, e], wsend.at[0, e])
        for e in range(spans)
    ]
    inner_in.start()
    group_in.start()

    @pl.when(serving)
    def _():
        for part in own_half:
            part.start()

    barrier = pltpu.get_barrier_semaphore()
    peers = 2 * n

    def greet(axis, size, me):
        def hello(i, carry):
            pl.semaphore_signal(
                barrier, inc=1, device_id={axis: lax.rem(me + i, size)}, device_id_type=MESH
            )
            return carry
        lax.fori_loop(1, size, hello, 0)

    greet("tp", peers, tp)
    greet("seq", spans, seq)

    def to_right(j, s):
        return copy(buf.at[j, k, s], buf.at[j, k, s], rsend.at[j, s], rrecv.at[j, s], {"tp": lax.rem(tp + 2, peers)})

    def to_left(j, s):
        return copy(buf.at[j, k, s], buf.at[j, k, s], lsend.at[j, s], lrecv.at[j, s], {"tp": lax.rem(tp + peers - 2, peers)})

    def to_sib(j, s):
        return copy(buf.at[j, k, s], buf.at[j, k, s], xsend.at[j, s], xrecv.at[j, s], sib)

    def from_sib(j, s):
        return copy(buf.at[j, 1 - k, s], buf.at[j, 1 - k, s], xsend.at[j, s], xrecv.at[j, s], sib)

    def own(s):
        @pl.when(has_right)
        def _():
            to_right(c, s).start()

        @pl.when(has_left)
        def _():
            to_left(c, s).start()

        to_sib(c, s).start()

    h = hidden[...].astype(jnp.float32)
    scale = lax.rsqrt(jnp.mean(h * h, axis=1, keepdims=True) + EPS)
    gain_line = flat(gain)
    for s in range(ns):
        part = slice(s * dc, (s + 1) * dc)
        normed = (hidden[:, part].astype(jnp.float32) * scale * gain_line[:, part]).astype(jnp.bfloat16)
        buf[c, k, s] = normed
        mytail[:, part] = normed[rows - 16 :]
        if s == 0:
            pl.semaphore_wait(barrier, peers - 1 + spans - 1)
        own(s)

    def w_far(m, core):
        return copy(
            wout.at[:, half_cols_at(core, seq)], wq.at[tp, seq],
            wsend.at[1 + m, core], wrecv.at[tp], {"tp": 2 * servers[m] + core},
        )

    other = tp + 1 - 2 * k
    w_near = [
        copy(wout.at[:, half_cols_at(1 - k, e)], wq.at[tp, e], wsend.at[1 + len(servers), e], wrecv.at[tp], sib)
        for e in range(spans)
    ]
    near_in = copy(wq.at[other], wq.at[other], wsend.at[0, 0], wrecv.at[other], sib)

    def w_send(m, core, close):
        @pl.when((c != servers[m]) & ((c // 2 == m) == close))
        def _():
            w_far(m, core).start()

    sends = [(m, core) for m in range(len(servers)) for core in range(2)]

    last = peers - 1
    has_tail = seq > 0
    tail_next = copy(mytail, tail, tsend.at[0], trecv.at[0], {"seq": lax.rem(seq + 1, spans)})
    tail_left = copy(tail, tail, tsend.at[1], trecv.at[0], {"tp": lax.rem(tp + peers - 2, peers)})
    tail_sib = copy(tail, tail, tsend.at[2], trecv.at[0], sib)

    @pl.when((tp == last) & (seq < spans - 1))
    def _():
        tail_next.start()

    group_out = copy(group, gbuf.at[k], gsend.at[0], grecv.at[0], sib)
    group_out.start()
    gtaps[k] = jnp.zeros((8, LANES), jnp.float32)
    gtaps[k, :count] = taps_group[...].astype(jnp.float32)
    taps_out = copy(gtaps.at[k], gtaps.at[k], gsend.at[1], grecv.at[1], sib)
    taps_out.start()

    @pl.when(serving)
    def _():
        for part in w_near:
            part.start()

    def far_block(m):
        beyond = lax.rem(4 * (c // 2) + 2 + m, peers)
        return jnp.where(m < 2, 2 * mate + m, beyond)

    def wq_part(j, span):
        return wq.at[j, span]

    def q_copy(j, origin, b):
        return copy(
            wq_part(j, origin), wq_part(j, origin), qsend.at[j, origin, b], qrecv.at[j, origin],
            {"seq": seq ^ (1 << b)},
        )

    def q_spread(m):
        j = far_block(m)
        copy(wq_part(j, seq), wq_part(j, seq), wsend.at[0, 0], wrecv.at[j], sib).wait_recv()
        for b in range(bits):
            q_copy(j, seq, b).start()

    def q_forwards(up):
        found = []
        for e in range(1, spans):
            top, low = e.bit_length() - 1, (e & -e).bit_length() - 1
            targets = [b for b in range(bits) if (b > top if up else b < low)]
            found.append((e, targets))
        return found

    def q_forward(m):
        j = far_block(m)
        for up in (True, False):
            @pl.when(j % 2 == (0 if up else 1))
            def _():
                for e, targets in q_forwards(up):
                    if targets:
                        origin = seq ^ e
                        part = wq_part(j, origin)
                        copy(part, part, wsend.at[0, 0], qrecv.at[j, origin], sib).wait_recv()
                        for b in targets:
                            q_copy(j, origin, b).start()

    def q_drain(m):
        j = far_block(m)
        for b in range(bits):
            q_copy(j, seq, b).wait_send()
        for up in (True, False):
            @pl.when(j % 2 == (0 if up else 1))
            def _():
                for e, targets in q_forwards(up):
                    for b in targets:
                        q_copy(j, seq ^ e, b).wait_send()

    inner_in.wait()
    lane_tiles = inner_dev // 2 // LANES
    size = 256
    depth = size // (2 * lane_tiles)
    row_at = lax.broadcasted_iota(jnp.int32, (size, size), 0)
    col_at = lax.broadcasted_iota(jnp.int32, (size, size), 1)
    kk, jj, tt = row_at % depth, row_at // (depth * lane_tiles), row_at // depth % lane_tiles
    perm = (col_at == kk * (2 * lane_tiles) + tt * 2 + jj).astype(jnp.float32).astype(jnp.bfloat16)
    gate_at = half_cols + 2 * LANES

    def sort(i, carry):
        block = raw[pl.ds(pl.multiple_of(i * size, size), size), :]
        out = jnp.dot(perm, block, preferred_element_type=jnp.float32).astype(jnp.bfloat16)
        at = pl.ds(pl.multiple_of(i * depth, depth), depth)
        for t in range(lane_tiles):
            w[at, gate_at + t * LANES : gate_at + (t + 1) * LANES] = out[t * depth : (t + 1) * depth]
            scan = out[(lane_tiles + t) * depth : (lane_tiles + t + 1) * depth]
            w[at, t * LANES : (t + 1) * LANES] = scan
        return carry

    lax.fori_loop(0, raw.shape[0] // size, sort, 0)
    pick_at = [lax.broadcasted_iota(jnp.int32, (heads, LANES), d) for d in range(2)]
    pick = (pick_at[0] == pick_at[1]).astype(jnp.float32)

    def turn(i, carry):
        at = pl.ds(pl.multiple_of(i * size, size), size)
        out = dot16(step[:, at], pick, ((0,), (0,)))
        w[at, gate_at + half_cols :] = out.astype(jnp.bfloat16)
        return carry

    lax.fori_loop(0, width // size, turn, 0)
    group_in.wait()
    copy(gbuf.at[1 - k], gbuf.at[1 - k], gsend.at[0], grecv.at[0], sib).wait_recv()
    copy(gtaps.at[1 - k], gtaps.at[1 - k], gsend.at[1], grecv.at[1], sib).wait_recv()
    taps[:count, :half_cols] = taps_inner[...].astype(jnp.float32)
    for m in range(2):
        w[:, half_cols + m * LANES : half_cols + (m + 1) * LANES] = gbuf[m]
        taps[:, half_cols + m * LANES : half_cols + (m + 1) * LANES] = gtaps[m]

    def arrivals(i):
        d, s = i // ns, i % ns

        @pl.when(c - d >= 0)
        def _():
            j = c - d
            copy(buf.at[j, k, s], buf.at[j, k, s], rsend.at[j, s], rrecv.at[j, s], sib).wait_recv()

            @pl.when(has_right)
            def _():
                to_right(j, s).start()

            to_sib(j, s).start()

        @pl.when(c + d < n)
        def _():
            j = c + d
            copy(buf.at[j, k, s], buf.at[j, k, s], lsend.at[j, s], lrecv.at[j, s], sib).wait_recv()

            @pl.when(has_left)
            def _():
                to_left(j, s).start()

            to_sib(j, s).start()

    def compute(i):
        d, s = i // ns, i % ns

        def side(which, carry):
            j = c - d + 2 * d * which

            @pl.when((j >= 0) & (j < n) & ((which == 0) | (d > 0)))
            def _():
                from_sib(j, s).wait_recv()
                x = buf[j, :, s].reshape(2 * rows, dc)
                at = pl.ds(pl.multiple_of(s * dc, dc), dc)
                out = jnp.dot(x, w[at, :], preferred_element_type=jnp.float32)
                place = pl.ds(pl.multiple_of(j * 2 * rows, 2 * rows), 2 * rows)

                @pl.when(s == 0)
                def _():
                    proj[place, :] = out

                @pl.when(s > 0)
                def _():
                    proj[place, :] += out

            return carry

        lax.fori_loop(0, 2, side, 0)

    far = peers - 2
    first_spread, first_forward = 2 * ns - 1, 2 * ns + 2
    near = min(2, far)

    conv = half_cols + 2 * LANES
    inner_own = half_cols
    head_dim = inner_own // heads
    length = peers * rows
    per_chip = 2 * rows // STRETCH
    bias_line = head_line(bias, heads, LANES, 1)
    rate_line = head_line(rate, heads, LANES, 1)
    skip_line = head_line(skip, heads, inner_own, head_dim)
    first = seq * (length // STRETCH)

    def take_tail():
        @pl.when(has_tail)
        def _():
            @pl.when(k == 0)
            def _():
                copy(tail, tail, tsend.at[1], trecv.at[0], sib).wait_recv()

            edge[...] = jnp.dot(tail[...], w[:, :conv], preferred_element_type=jnp.float32)[8:]

        @pl.when(jnp.logical_not(has_tail))
        def _():
            edge[...] = jnp.zeros_like(edge)

    def scan_slot(d, u):
        far_side = d > 0
        lowest = (c - d == 0) & far_side | (c == 0) & (d == 1)
        chip = jnp.where(u == 0, c - d, jnp.where(u == 1, c - d + 1, jnp.where(u < 4, c + d, 0)))
        part = jnp.where((u == 0) | (u == 3), 1, 0)
        ready = jnp.where(u == 0, c - d >= 0, jnp.where(u == 1, far_side & (c - d >= 0), jnp.where(u < 4, far_side & (c + d < n), lowest)))

        @pl.when(ready & (part < per_chip))
        def _():
            @pl.when(u == 4)
            def _():
                take_tail()

            i = chip * per_chip + part
            at = pl.ds(pl.multiple_of(i * STRETCH, STRETCH), STRETCH)
            scan_stretch(
                count, heads, head_dim, inner_own, LANES, at,
                proj, segments, first, i, taps, bias_line, rate_line, skip_line, y, c_maps, entries, edge, fresh, decays,
            )

    def scans(i):
        d, u = i // ns - 1, i % ns

        def one(slot, carry):
            scan_slot(d, slot)
            return carry

        @pl.when((d >= 0) & (u < 4))
        def _():
            lax.fori_loop(u, jnp.where(u == 3, 5, u + 1), one, 0)

    def item(i, carry):
        @pl.when((i >= ns) & (i < n * ns))
        def _():
            arrivals(i)

        @pl.when((i == ns + 1) & has_tail & (k == 1))
        def _():
            copy(tail, tail, tsend.at[1], trecv.at[0], sib).wait_recv()

            @pl.when(has_left)
            def _():
                tail_left.start()

            tail_sib.start()

        for close, when in ((True, ns), (False, 3 * ns - 1)):
            @pl.when(i == when)
            def _():
                for m, core in sends:
                    w_send(m, core, close)

        @pl.when(i <= n * ns)
        def _():
            compute(i - 1)

        scans(i)

        @pl.when(serving & (i >= first_spread) & (i < first_spread + near))
        def _():
            q_spread(i - first_spread)

        @pl.when(serving & (i >= first_forward) & (i < first_forward + near))
        def _():
            q_forward(i - first_forward)

        return carry

    lax.fori_loop(1, n * ns + 4, item, 0)

    packed_sum = jnp.zeros(state.shape, jnp.float32)
    whole = jnp.ones((8, inner_own), jnp.float32)
    for i in range(length // STRETCH):
        packed_sum = decays[i, 0:1] * packed_sum + fresh[i]
        whole = whole * decays[i]

    packed[...] = packed_sum.astype(jnp.bfloat16)
    decay[...] = whole

    def state_to(e):
        dev = {"seq": lax.rem(seq + e, spans)}
        return (
            copy(packed, came.at[e], ssend.at[0, e], srecv.at[0, e], dev),
            copy(decay, came_decay.at[e], ssend.at[1, e], srecv.at[1, e], dev),
        )

    for e in range(1, spans):
        @pl.when(seq + e < spans)
        def _():
            for part in state_to(e):
                part.start()

    def over(act):
        def one(m, carry):
            act(m)
            return carry
        return one

    @pl.when(serving)
    def _():
        lax.fori_loop(near, far, over(q_spread), 0)

    state[...] = jnp.zeros_like(state)
    for e in range(spans - 1, 0, -1):
        @pl.when(e <= seq)
        def _():
            for part in state_to(e):
                part.wait_recv()
            state[...] = came[e].astype(jnp.float32) + came_decay[e, 0:1] * state[...]

    def enter(i, carry):
        entering[i] = state[...].astype(jnp.bfloat16)
        state[...] = decays[i, 0:1] * state[...] + fresh[i]
        return carry

    lax.fori_loop(0, length // STRETCH, enter, 0)

    block = 2 * rows
    pairs = n // 2

    def chip_at(i):
        m = lax.rem(i, pairs)
        first = i < pairs
        return jnp.where(first, 2 * m + m % 2, 2 * m + 1 - m % 2)

    def rows_of(chip):
        return pl.ds(pl.multiple_of(chip * block, block), block)

    def sq_copy(chip):
        return copy(sq.at[0, chip], sq.at[1, chip], esend.at[chip], erecv.at[chip], sib)

    def gate_block(i, carry):
        chip = chip_at(i)
        at = rows_of(chip)
        maps = c_maps[at, :]
        carried = [
            dot16(maps[u * STRETCH : (u + 1) * STRETCH], entering[chip * per_chip + u])
            for u in range(per_chip)
        ]
        carried = jnp.concatenate(carried, axis=0) * widen(entries[at, :], heads, head_dim)
        gated = (y[at, :] + carried) * silu(proj[at, conv : conv + inner_own])
        y[at, :] = gated
        sums = jnp.sum(gated * gated, axis=1, keepdims=True)
        sq[0, chip] = jnp.broadcast_to(sums, (block, LANES))
        sq_copy(chip).start()
        return carry

    lax.fori_loop(0, n, gate_block, 0)

    def server_of(chip):
        m = chip // 2
        return 2 * m + 1 - m % 2

    def slot_of(chip):
        return jnp.where(chip == server_of(chip), 1, 0)

    def mixed_far(chip):
        return copy(
            mixed.at[chip], taken.at[slot_of(chip), tp], msend.at[chip], mrecv.at[slot_of(chip), c],
            {"tp": lax.rem(2 * server_of(chip) + k, peers)},
        )

    def mixed_near(slot, src):
        place = taken.at[slot, 2 * src + k]
        return copy(place, place, nsend.at[slot, src], nrecv.at[slot, src], sib)

    mix_line = flat(mixer_gain)

    def mix_block(i, carry):
        chip = chip_at(i)
        at = rows_of(chip)
        sq_copy(chip).wait_recv()
        mean = (sq[0, chip] + sq[1, chip]) / (2 * inner_own)
        factor = lax.rsqrt(mean + EPS)
        wide = jnp.concatenate([factor] * (inner_own // LANES), axis=1)
        done = (y[at, :] * wide * mix_line).astype(jnp.bfloat16)

        @pl.when(c != server_of(chip))
        def _():
            mixed[chip] = done

            @pl.when(i < pairs)
            def _():
                mixed_far(chip).start()

        @pl.when(c == server_of(chip))
        def _():
            taken[slot_of(chip), tp] = done
            mixed_near(slot_of(chip), c).start()

        return carry

    lax.fori_loop(0, n, mix_block, 0)

    def mates_left(i, carry):
        @pl.when(c != server_of(chip_at(i)))
        def _():
            mixed_far(chip_at(i)).wait_send()

        return carry

    lax.fori_loop(0, pairs, mates_left, 0)

    def servers_next(i, carry):
        @pl.when(c != chip_at(i))
        def _():
            mixed_far(chip_at(i)).start()

        return carry

    lax.fori_loop(pairs, n, servers_next, 0)

    def result_far(q, core):
        return copy(
            results.at[0, q, pl.ds(core * rows, rows)], landed.at[k, q], osend.at[q, core], orecv.at[k, q],
            {"tp": 2 * mate + core},
        )

    def result_near(q):
        return copy(
            results.at[1, q, pl.ds(pl.multiple_of((1 - k) * rows, rows), rows)], landed.at[k, q],
            osend.at[q, 2], orecv.at[k, q], sib,
        )

    @pl.when(serving)
    def _():
        for e in range(spans):
            own_half[e].wait()
        near_in.wait_recv()
        lax.fori_loop(near, max(near, far - 2), over(q_forward), 0)

        def collect(slot):
            def relay(m, carry):
                src = lax.rem(c + m, n)
                place = taken.at[slot, 2 * src + k]
                copy(place, place, nsend.at[slot, src], mrecv.at[slot, src], sib).wait_recv()
                mixed_near(slot, src).start()
                return carry

            lax.fori_loop(1, n, relay, 0)

            def from_near(src, carry):
                place = taken.at[slot, 2 * src + 1 - k]
                copy(place, place, nsend.at[slot, src], nrecv.at[slot, src], sib).wait_recv()
                return carry

            lax.fori_loop(0, n, from_near, 0)

        def multiply(slot, q):
            sums = jnp.zeros((block, wq.shape[3]), jnp.float32)
            for j in range(peers):
                sums += jnp.dot(taken[slot, j], wq[j, q], preferred_element_type=jnp.float32)
            return sums.astype(jnp.bfloat16)

        collect(0)

        def for_mate(e, carry):
            q = seq ^ e

            @pl.when(e == 1)
            def _():
                lax.fori_loop(max(near, far - 2), far, over(q_forward), 0)

            def part_in(m, carry):
                j = far_block(m)
                ends = jnp.where(j % 2 == 0, 2 * e >= spans, e % 2 == 1)

                @pl.when((e > 0) & ends)
                def _():
                    part = wq_part(j, q)
                    copy(part, part, wsend.at[0, 0], qrecv.at[j, q], sib).wait_recv()

                return carry

            lax.fori_loop(0, far, part_in, 0)
            results[0, q] = multiply(0, q)
            for core in range(2):
                result_far(q, core).start()
            return carry

        lax.fori_loop(0, spans, for_mate, 0)
        collect(1)

        def for_own(q, carry):
            results[1, q] = multiply(1, q)
            result_near(q).start()
            landed[k, q] = results[1, q, pl.ds(pl.multiple_of(k * rows, rows), rows)]
            return carry

        lax.fori_loop(0, spans, for_own, 0)

    def finish(core, q):
        place = landed.at[core, q]
        arrival = copy(place, place, osend.at[q, 0], orecv.at[core, q], sib)

        @pl.when(jnp.logical_not(serving) | (k != core))
        def _():
            arrival.wait_recv()

        at = pl.ds(core * half + q * quarter, quarter)
        out[:, at] = (hidden[:, at].astype(jnp.float32) + landed[core, q].astype(jnp.float32)).astype(jnp.bfloat16)

    for q in range(spans):
        for core in range(2):
            finish(core, q)

    def drain(i, carry):
        j, s = i // ns, i % ns
        to_sib(j, s).wait_send()

        @pl.when(has_right & (j <= c))
        def _():
            to_right(j, s).wait_send()

        @pl.when(has_left & (j >= c))
        def _():
            to_left(j, s).wait_send()

        return carry

    lax.fori_loop(0, n * ns, drain, 0)
    group_out.wait_send()
    taps_out.wait_send()

    @pl.when((tp == last) & (seq < spans - 1))
    def _():
        tail_next.wait_send()

    @pl.when(has_tail & (k == 1))
    def _():
        @pl.when(has_left)
        def _():
            tail_left.wait_send()

        tail_sib.wait_send()

    for m, core in sends:
        @pl.when(c != servers[m])
        def _():
            w_far(m, core).wait_send()

    for e in range(1, spans):
        @pl.when(seq + e < spans)
        def _():
            for part in state_to(e):
                part.wait_send()

    def sums_left(chip, carry):
        sq_copy(chip).wait_send()

        @pl.when((c != chip) & (chip == server_of(chip)))
        def _():
            mixed_far(chip).wait_send()

        return carry

    lax.fori_loop(0, n, sums_left, 0)

    @pl.when(serving)
    def _():
        for e in range(spans):
            w_near[e].wait_send()

        def far_left(m, carry):
            q_drain(m)
            return carry

        lax.fori_loop(0, far, far_left, 0)

        def near_left(src, carry):
            for slot in range(2):
                mixed_near(slot, src).wait_send()
            return carry

        lax.fori_loop(0, n, near_left, 0)

        def results_left(q, carry):
            for core in range(2):
                result_far(q, core).wait_send()
            result_near(q).wait_send()
            return carry

        lax.fori_loop(0, spans, results_left, 0)


def mixer(hidden, gain, inner, group, step, wout, segments, taps_inner, taps_group, bias, rate, skip, mixer_gain, heads, count, n, spans, ns):
    rows, width = hidden.shape
    inner_dev = inner.shape[0] * inner.shape[1] // width
    own = inner_dev // 2
    cols = inner_dev + 3 * LANES
    half = wout.shape[1] // 2
    length = 2 * n * rows
    vmem = pl.BlockSpec(memory_space=pltpu.VMEM)
    anywhere = pl.BlockSpec(memory_space=pl.ANY)
    scalars = pl.BlockSpec(memory_space=pltpu.SMEM)
    dma = pltpu.SemaphoreType.DMA
    bits = max(1, spans.bit_length() - 1)
    bf16, f32 = jnp.bfloat16, jnp.float32
    return pl.pallas_call(
        functools.partial(mixer_kernel, n, spans, ns, heads, count),
        out_shape=jax.ShapeDtypeStruct(hidden.shape, bf16),
        in_specs=[vmem, vmem, anywhere, anywhere, vmem, anywhere] + [vmem] * 3 + [scalars] * 3 + [vmem],
        out_specs=vmem,
        scratch_shapes=[
            pltpu.VMEM((n, 2, ns, rows, width // ns), bf16),
            pltpu.VMEM((16, width), bf16),
            pltpu.VMEM((16, width), bf16),
            pltpu.VMEM(inner.shape, bf16),
            pltpu.VMEM((2,) + group.shape, bf16),
            pltpu.VMEM((2, 8, LANES), f32),
            pltpu.VMEM((8, own + 2 * LANES), f32),
            pltpu.VMEM((width, cols), bf16),
            pltpu.VMEM((length, cols), f32),
            pltpu.VMEM((8, own + 2 * LANES), f32),
            pltpu.VMEM((2 * n, spans, wout.shape[0], half // spans), bf16),
            pltpu.VMEM((length, own), f32),
            pltpu.VMEM((length, LANES), bf16),
            pltpu.VMEM((length, LANES), f32),
            pltpu.VMEM((LANES, own), f32),
            pltpu.VMEM((length // STRETCH, LANES, own), f32),
            pltpu.VMEM((length // STRETCH, 8, own), f32),
            pltpu.VMEM((length // STRETCH, LANES, own), bf16),
            pltpu.VMEM((LANES, own), bf16),
            pltpu.VMEM((8, own), f32),
            pltpu.VMEM((spans, LANES, own), bf16),
            pltpu.VMEM((spans, 8, own), f32),
            pltpu.VMEM((2, n, 2 * rows, LANES), f32),
            pltpu.VMEM((n, 2 * rows, own), bf16),
            pltpu.VMEM((2, 2 * n, 2 * rows, own), bf16),
            pltpu.VMEM((2, spans, 2 * rows, half // spans), bf16),
            pltpu.VMEM((2, spans, rows, half // spans), bf16),
            dma((n, ns)), dma((n, ns)), dma((n, ns)), dma((n, ns)), dma((n, ns)), dma((n, ns)),
            dma((3,)), dma((1,)), dma((2,)), dma((2,)),
            dma((2 + n // 2, max(2, spans))), dma((2 * n,)), dma((2 * n, spans, bits)), dma((2 * n, spans)), dma((3,)),
            dma((2, spans)), dma((2, spans)), dma((n,)), dma((n,)),
            dma((n,)), dma((2, n)), dma((2, n)), dma((2, n)), dma((spans, 3)), dma((2, spans)),
        ],
        compiler_params=pltpu.CompilerParams(
            collective_id=0, has_side_effects=True, vmem_limit_bytes=60 << 20
        ),
        cost_estimate=pl.CostEstimate(
            flops=24_000_000_000, bytes_accessed=12_000_000, transcendentals=4_000_000
        ),
        name="mixer",
    )(hidden, gain, inner, group, step, wout, segments, taps_inner, taps_group, bias, rate, skip, mixer_gain)


def by_row(weight):
    width, pair, cols = weight.shape
    tiles = cols // LANES
    return weight.reshape(width, pair, tiles, LANES).transpose(0, 2, 1, 3).reshape(-1, LANES)


def body(
    hidden,
    norm_gain,
    inner_weight,
    group_weight,
    step_weight,
    step_bias,
    decay_rate,
    filter_inner,
    filter_group,
    skip_gain,
    mixer_gain,
    output_weight,
    segment_ids,
):
    spans, chips = lax.axis_size("seq"), lax.axis_size("tp") // 2
    return mixer(
        hidden, norm_gain.reshape(-1, LANES), by_row(inner_weight), group_weight, step_weight.T, output_weight,
        segment_ids.reshape(-1, STRETCH), filter_inner, filter_group, step_bias, decay_rate, skip_gain,
        mixer_gain.reshape(-1, LANES), step_weight.shape[1], filter_inner.shape[0], chips, spans, 4,
    )


def solution(mesh):
    in_specs = (
        P(("seq", "tp"), None),
        P(),
        P(None, None, "tp"),
        P(None, "tp"),
        P(None, "tp"),
        P("tp"),
        P("tp"),
        P(None, "tp"),
        P(None, "tp"),
        P("tp"),
        P("tp"),
        P("tp", None),
        P(),
    )
    out_specs = P(("seq", "tp"), None)
    return jax.shard_map(body, mesh=mesh, in_specs=in_specs, out_specs=out_specs, check_vma=False)
```

```python
import functools
import jax
import jax.numpy as jnp
from jax import lax
from jax.experimental import pallas as pl
from jax.experimental.pallas import tpu as pltpu
from jax.sharding import PartitionSpec as P

EPS = 1e-05
LANES = 128
STRETCH = 128
HIGH = lax.Precision.HIGHEST
MESH = pl.DeviceIdType.MESH


def silu(v):
    return v / (1.0 + jnp.exp(-v))


def widen(cols, heads, head_dim):
    rows = cols.shape[0]
    parts = [jnp.broadcast_to(cols[:, h : h + 1], (rows, head_dim)) for h in range(heads)]
    return jnp.concatenate(parts, axis=1)


def dot16(a, b, dims=((1,), (0,))):
    a, b = a.astype(jnp.bfloat16), b.astype(jnp.bfloat16)
    return lax.dot_general(a, b, (dims, ((), ())), preferred_element_type=jnp.float32)


def segment_marks(segments, first, i):
    shape = (8, STRETCH)

    def line(at):
        ids = segments[pl.ds(jnp.maximum(at, 0), 1), :].astype(jnp.float32)
        return jnp.broadcast_to(jnp.where(at >= 0, ids, -1.0), shape)

    now, past = line(first + i), line(first + i - 1)
    lane = lax.broadcasted_iota(jnp.int32, shape, 1)
    row = lax.broadcasted_iota(jnp.int32, shape, 0)
    end = slice(STRETCH - 1, STRETCH)
    marks = now
    for back in range(1, 4):
        other = jnp.where(lane < back, pltpu.roll(past, back, 1), pltpu.roll(now, back, 1))
        marks = jnp.where(row == back, (now == other).astype(jnp.float32), marks)
    for at, other in ((4, past[:, end]), (5, now[:, end])):
        marks = jnp.where(row == at, (now == other).astype(jnp.float32), marks)
    return marks.T, now[0:1]


def head_line(values, heads, width, reach):
    lane = lax.broadcasted_iota(jnp.int32, (1, width), 1)
    line = jnp.zeros((1, width), jnp.float32)
    for h in range(heads):
        line = jnp.where((lane >= h * reach) & (lane < (h + 1) * reach), values[h], line)
    return line


def flat(ref):
    return jnp.concatenate([ref[i : i + 1, :] for i in range(ref.shape[0])], axis=1)


def scan_stretch(
    count, heads, head_dim, inner, states, at,
    proj, segments, first, i, taps, bias, rate, skip, y_out, c_out, entry_out, edge, fresh_out, decay_out,
):
    aux, row_seg = segment_marks(segments, first, i)
    conv = inner + 2 * states
    cur = proj[at, :conv]
    past = proj[pl.ds(pl.multiple_of(jnp.maximum(i * STRETCH - 8, 0), 8), 8), :conv]
    both = jnp.concatenate([jnp.where(i == 0, edge[...], past), cur], axis=0)
    size = STRETCH
    tap = taps[...]
    acc = tap[count - 1 : count] * cur
    for back in range(1, count):
        same = aux[:, back : back + 1]
        acc += tap[count - 1 - back : count - back] * both[8 - back : 8 - back + size] * same
    active = silu(acc)
    x = active[:, :inner]
    b_map = active[:, inner : inner + states]
    c_map = active[:, inner + states :]
    raw = proj[at, conv + inner :] + bias
    step = jnp.maximum(raw, 0.0) + jnp.log1p(jnp.exp(-jnp.abs(raw)))
    log_decay = -step * rate
    row_at = lax.broadcasted_iota(jnp.int32, (size, size), 0)
    col_at = lax.broadcasted_iota(jnp.int32, (size, size), 1)
    causal = row_at >= col_at
    cum = jnp.dot(
        causal.astype(jnp.float32), log_decay, precision=HIGH, preferred_element_type=jnp.float32
    )
    cum_rows = cum.T
    alive, in_last = aux[:, 4:5], aux[:, 5:6]
    last = cum[size - 1 :]
    mask = causal & (aux[:, 0:1] == row_seg)
    xs = x * widen(step, heads, head_dim)
    xs16 = xs.astype(jnp.bfloat16)
    products = dot16(c_map, b_map, ((1,), (1,)))
    parts = []
    for h in range(heads):
        gap = cum[:, h : h + 1] - cum_rows[h : h + 1, :]
        mixing = products * jnp.exp(jnp.where(mask, gap, -1e30))
        parts.append(dot16(mixing, xs16[:, h * head_dim : (h + 1) * head_dim]))
    local = jnp.concatenate(parts, axis=1)
    entry = jnp.exp(cum) * alive
    y_out[at, :] = local + skip * x
    c_out[at, :] = c_map.astype(jnp.bfloat16)
    entry_out[at, :] = entry
    end = jnp.exp(last - cum) * in_last
    fresh_out[i] = dot16(b_map, xs * widen(end, heads, head_dim), ((0,), (0,)))
    decay_out[i] = jnp.broadcast_to(widen(entry[size - 8 :], heads, head_dim)[7:8], (8, inner))


def servers_of(chips):
    return [2 * i + 1 - i % 2 for i in range(chips // 2)]


def mixer_kernel(
    n, spans, ns, heads, count,
    hidden, gain, inner, group, step, wout, segments, taps_inner, taps_group, bias, rate, skip, mixer_gain,
    out,
    buf, mytail, tail, raw, gbuf, gtaps, taps, w, proj, edge, wq,
    y, c_maps, entries, state, fresh, decays, entering, packed, decay, came, came_decay,
    sq, mixed, taken, results,
    rsend, lsend, xsend, rrecv, lrecv, xrecv,
    tsend, trecv, gsend, grecv, wsend, wrecv, qsend, qrecv, local,
    ssend, srecv, esend, erecv, msend, mrecv, nsend, nrecv, osend, orecv,
):
    tp, seq = lax.axis_index("tp"), lax.axis_index("seq")
    c, k = tp // 2, tp % 2
    rows, width = hidden.shape
    dc = width // ns
    sib = {"tp": tp + 1 - 2 * k}
    has_left, has_right = c > 0, c < n - 1
    inner_dev = w.shape[1] - 3 * LANES
    half_cols = inner_dev // 2
    servers = servers_of(n)
    mate = jnp.where(c == 2 * (c // 2), c + 1, c - 1)
    serving = functools.reduce(jnp.logical_or, [c == s for s in servers])
    bits = spans.bit_length() - 1
    half = wout.shape[1] // 2
    quarter = half // spans

    def copy(src, dst, send, recv, dev):
        return pltpu.make_async_remote_copy(
            src_ref=src, dst_ref=dst, send_sem=send, recv_sem=recv, device_id=dev, device_id_type=MESH
        )

    inner_in = pltpu.make_async_copy(inner, raw, local.at[0])
    group_in = pltpu.make_async_copy(group, gbuf.at[k], local.at[1])

    def half_cols_at(core, span):
        return pl.ds(pl.multiple_of(core * half + span * quarter, LANES), quarter)

    own_half = [
        pltpu.make_async_copy(wout.at[:, half_cols_at(k, e)], wq.at[tp, e], wsend.at[0, e])
        for e in range(spans)
    ]
    inner_in.start()
    group_in.start()

    @pl.when(serving)
    def _():
        for part in own_half:
            part.start()

    barrier = pltpu.get_barrier_semaphore()
    peers = 2 * n

    def greet(axis, size, me):
        def hello(i, carry):
            pl.semaphore_signal(
                barrier, inc=1, device_id={axis: lax.rem(me + i, size)}, device_id_type=MESH
            )
            return carry
        lax.fori_loop(1, size, hello, 0)

    greet("tp", peers, tp)
    greet("seq", spans, seq)

    def to_right(j, s):
        return copy(buf.at[j, k, s], buf.at[j, k, s], rsend.at[j, s], rrecv.at[j, s], {"tp": lax.rem(tp + 2, peers)})

    def to_left(j, s):
        return copy(buf.at[j, k, s], buf.at[j, k, s], lsend.at[j, s], lrecv.at[j, s], {"tp": lax.rem(tp + peers - 2, peers)})

    def to_sib(j, s):
        return copy(buf.at[j, k, s], buf.at[j, k, s], xsend.at[j, s], xrecv.at[j, s], sib)

    def from_sib(j, s):
        return copy(buf.at[j, 1 - k, s], buf.at[j, 1 - k, s], xsend.at[j, s], xrecv.at[j, s], sib)

    def own(s):
        @pl.when(has_right)
        def _():
            to_right(c, s).start()

        @pl.when(has_left)
        def _():
            to_left(c, s).start()

        to_sib(c, s).start()

    h = hidden[...].astype(jnp.float32)
    scale = lax.rsqrt(jnp.mean(h * h, axis=1, keepdims=True) + EPS)
    gain_line = flat(gain)
    for s in range(ns):
        part = slice(s * dc, (s + 1) * dc)
        normed = (hidden[:, part].astype(jnp.float32) * scale * gain_line[:, part]).astype(jnp.bfloat16)
        buf[c, k, s] = normed
        mytail[:, part] = normed[rows - 16 :]
        if s == 0:
            pl.semaphore_wait(barrier, peers - 1 + spans - 1)
        own(s)

    def w_far(m, core):
        return copy(
            wout.at[:, half_cols_at(core, seq)], wq.at[tp, seq],
            wsend.at[1 + m, core], wrecv.at[tp], {"tp": 2 * servers[m] + core},
        )

    other = tp + 1 - 2 * k
    w_near = [
        copy(wout.at[:, half_cols_at(1 - k, e)], wq.at[tp, e], wsend.at[1 + len(servers), e], wrecv.at[tp], sib)
        for e in range(spans)
    ]
    near_in = copy(wq.at[other], wq.at[other], wsend.at[0, 0], wrecv.at[other], sib)

    def w_send(m, core, close):
        @pl.when((c != servers[m]) & ((c // 2 == m) == close))
        def _():
            w_far(m, core).start()

    sends = [(m, core) for m in range(len(servers)) for core in range(2)]

    last = peers - 1
    has_tail = seq > 0
    tail_next = copy(mytail, tail, tsend.at[0], trecv.at[0], {"seq": lax.rem(seq + 1, spans)})
    tail_left = copy(tail, tail, tsend.at[1], trecv.at[0], {"tp": lax.rem(tp + peers - 2, peers)})
    tail_sib = copy(tail, tail, tsend.at[2], trecv.at[0], sib)

    @pl.when((tp == last) & (seq < spans - 1))
    def _():
        tail_next.start()

    group_out = copy(group, gbuf.at[k], gsend.at[0], grecv.at[0], sib)
    group_out.start()
    gtaps[k] = jnp.zeros((8, LANES), jnp.float32)
    gtaps[k, :count] = taps_group[...].astype(jnp.float32)
    taps_out = copy(gtaps.at[k], gtaps.at[k], gsend.at[1], grecv.at[1], sib)
    taps_out.start()

    @pl.when(serving)
    def _():
        for part in w_near:
            part.start()

    def far_block(m):
        beyond = lax.rem(4 * (c // 2) + 2 + m, peers)
        return jnp.where(m < 2, 2 * mate + m, beyond)

    def wq_part(j, span):
        return wq.at[j, span]

    def q_copy(j, origin, b):
        return copy(
            wq_part(j, origin), wq_part(j, origin), qsend.at[j, origin, b], qrecv.at[j, origin],
            {"seq": seq ^ (1 << b)},
        )

    def q_spread(m):
        j = far_block(m)
        copy(wq_part(j, seq), wq_part(j, seq), wsend.at[0, 0], wrecv.at[j], sib).wait_recv()
        for b in range(bits):
            q_copy(j, seq, b).start()

    def q_forwards(up):
        found = []
        for e in range(1, spans):
            top, low = e.bit_length() - 1, (e & -e).bit_length() - 1
            targets = [b for b in range(bits) if (b > top if up else b < low)]
            found.append((e, targets))
        return found

    def q_forward(m):
        j = far_block(m)
        for up in (True, False):
            @pl.when(j % 2 == (0 if up else 1))
            def _():
                for e, targets in q_forwards(up):
                    if targets:
                        origin = seq ^ e
                        part = wq_part(j, origin)
                        copy(part, part, wsend.at[0, 0], qrecv.at[j, origin], sib).wait_recv()
                        for b in targets:
                            q_copy(j, origin, b).start()

    def q_drain(m):
        j = far_block(m)
        for b in range(bits):
            q_copy(j, seq, b).wait_send()
        for up in (True, False):
            @pl.when(j % 2 == (0 if up else 1))
            def _():
                for e, targets in q_forwards(up):
                    for b in targets:
                        q_copy(j, seq ^ e, b).wait_send()

    inner_in.wait()
    lane_tiles = inner_dev // 2 // LANES
    size = 256
    depth = size // (2 * lane_tiles)
    row_at = lax.broadcasted_iota(jnp.int32, (size, size), 0)
    col_at = lax.broadcasted_iota(jnp.int32, (size, size), 1)
    kk, jj, tt = row_at % depth, row_at // (depth * lane_tiles), row_at // depth % lane_tiles
    perm = (col_at == kk * (2 * lane_tiles) + tt * 2 + jj).astype(jnp.float32).astype(jnp.bfloat16)
    gate_at = half_cols + 2 * LANES

    def sort(i, carry):
        block = raw[pl.ds(pl.multiple_of(i * size, size), size), :]
        out = jnp.dot(perm, block, preferred_element_type=jnp.float32).astype(jnp.bfloat16)
        at = pl.ds(pl.multiple_of(i * depth, depth), depth)
        for t in range(lane_tiles):
            w[at, gate_at + t * LANES : gate_at + (t + 1) * LANES] = out[t * depth : (t + 1) * depth]
            scan = out[(lane_tiles + t) * depth : (lane_tiles + t + 1) * depth]
            w[at, t * LANES : (t + 1) * LANES] = scan
        return carry

    lax.fori_loop(0, raw.shape[0] // size, sort, 0)
    pick_at = [lax.broadcasted_iota(jnp.int32, (heads, LANES), d) for d in range(2)]
    pick = (pick_at[0] == pick_at[1]).astype(jnp.float32)

    def turn(i, carry):
        at = pl.ds(pl.multiple_of(i * size, size), size)
        out = dot16(step[:, at], pick, ((0,), (0,)))
        w[at, gate_at + half_cols :] = out.astype(jnp.bfloat16)
        return carry

    lax.fori_loop(0, width // size, turn, 0)
    group_in.wait()
    copy(gbuf.at[1 - k], gbuf.at[1 - k], gsend.at[0], grecv.at[0], sib).wait_recv()
    copy(gtaps.at[1 - k], gtaps.at[1 - k], gsend.at[1], grecv.at[1], sib).wait_recv()
    taps[:count, :half_cols] = taps_inner[...].astype(jnp.float32)
    for m in range(2):
        w[:, half_cols + m * LANES : half_cols + (m + 1) * LANES] = gbuf[m]
        taps[:, half_cols + m * LANES : half_cols + (m + 1) * LANES] = gtaps[m]

    def arrivals(i):
        d, s = i // ns, i % ns

        @pl.when(c - d >= 0)
        def _():
            j = c - d
            copy(buf.at[j, k, s], buf.at[j, k, s], rsend.at[j, s], rrecv.at[j, s], sib).wait_recv()

            @pl.when(has_right)
            def _():
                to_right(j, s).start()

            to_sib(j, s).start()

        @pl.when(c + d < n)
        def _():
            j = c + d
            copy(buf.at[j, k, s], buf.at[j, k, s], lsend.at[j, s], lrecv.at[j, s], sib).wait_recv()

            @pl.when(has_left)
            def _():
                to_left(j, s).start()

            to_sib(j, s).start()

    def compute(i):
        d, s = i // ns, i % ns

        def side(which, carry):
            j = c - d + 2 * d * which

            @pl.when((j >= 0) & (j < n) & ((which == 0) | (d > 0)))
            def _():
                from_sib(j, s).wait_recv()
                x = buf[j, :, s].reshape(2 * rows, dc)
                at = pl.ds(pl.multiple_of(s * dc, dc), dc)
                out = jnp.dot(x, w[at, :], preferred_element_type=jnp.float32)
                place = pl.ds(pl.multiple_of(j * 2 * rows, 2 * rows), 2 * rows)

                @pl.when(s == 0)
                def _():
                    proj[place, :] = out

                @pl.when(s > 0)
                def _():
                    proj[place, :] += out

            return carry

        lax.fori_loop(0, 2, side, 0)

    far = peers - 2
    first_spread, first_forward = 2 * ns - 1, 2 * ns + 2
    near = min(2, far)

    conv = half_cols + 2 * LANES
    inner_own = half_cols
    head_dim = inner_own // heads
    length = peers * rows
    per_chip = 2 * rows // STRETCH
    bias_line = head_line(bias, heads, LANES, 1)
    rate_line = head_line(rate, heads, LANES, 1)
    skip_line = head_line(skip, heads, inner_own, head_dim)
    first = seq * (length // STRETCH)

    def take_tail():
        @pl.when(has_tail)
        def _():
            @pl.when(k == 0)
            def _():
                copy(tail, tail, tsend.at[1], trecv.at[0], sib).wait_recv()

            edge[...] = jnp.dot(tail[...], w[:, :conv], preferred_element_type=jnp.float32)[8:]

        @pl.when(jnp.logical_not(has_tail))
        def _():
            edge[...] = jnp.zeros_like(edge)

    def scan_slot(d, u):
        far_side = d > 0
        lowest = (c - d == 0) & far_side | (c == 0) & (d == 1)
        chip = jnp.where(u == 0, c - d, jnp.where(u == 1, c - d + 1, jnp.where(u < 4, c + d, 0)))
        part = jnp.where((u == 0) | (u == 3), 1, 0)
        ready = jnp.where(u == 0, c - d >= 0, jnp.where(u == 1, far_side & (c - d >= 0), jnp.where(u < 4, far_side & (c + d < n), lowest)))

        @pl.when(ready & (part < per_chip))
        def _():
            @pl.when(u == 4)
            def _():
                take_tail()

            i = chip * per_chip + part
            at = pl.ds(pl.multiple_of(i * STRETCH, STRETCH), STRETCH)
            scan_stretch(
                count, heads, head_dim, inner_own, LANES, at,
                proj, segments, first, i, taps, bias_line, rate_line, skip_line, y, c_maps, entries, edge, fresh, decays,
            )

    def scans(i):
        d, u = i // ns - 1, i % ns

        def one(slot, carry):
            scan_slot(d, slot)
            return carry

        @pl.when((d >= 0) & (u < 4))
        def _():
            lax.fori_loop(u, jnp.where(u == 3, 5, u + 1), one, 0)

    def item(i, carry):
        @pl.when((i >= ns) & (i < n * ns))
        def _():
            arrivals(i)

        @pl.when((i == ns + 1) & has_tail & (k == 1))
        def _():
            copy(tail, tail, tsend.at[1], trecv.at[0], sib).wait_recv()

            @pl.when(has_left)
            def _():
                tail_left.start()

            tail_sib.start()

        for close, when in ((True, ns), (False, 3 * ns - 1)):
            @pl.when(i == when)
            def _():
                for m, core in sends:
                    w_send(m, core, close)

        @pl.when(i <= n * ns)
        def _():
            compute(i - 1)

        scans(i)

        @pl.when(serving & (i >= first_spread) & (i < first_spread + near))
        def _():
            q_spread(i - first_spread)

        @pl.when(serving & (i >= first_forward) & (i < first_forward + near))
        def _():
            q_forward(i - first_forward)

        return carry

    lax.fori_loop(1, n * ns + 4, item, 0)

    packed_sum = jnp.zeros(state.shape, jnp.float32)
    whole = jnp.ones((8, inner_own), jnp.float32)
    for i in range(length // STRETCH):
        packed_sum = decays[i, 0:1] * packed_sum + fresh[i]
        whole = whole * decays[i]

    packed[...] = packed_sum.astype(jnp.bfloat16)
    decay[...] = whole

    def state_to(e):
        dev = {"seq": lax.rem(seq + e, spans)}
        return (
            copy(packed, came.at[e], ssend.at[0, e], srecv.at[0, e], dev),
            copy(decay, came_decay.at[e], ssend.at[1, e], srecv.at[1, e], dev),
        )

    for e in range(1, spans):
        @pl.when(seq + e < spans)
        def _():
            for part in state_to(e):
                part.start()

    def over(act):
        def one(m, carry):
            act(m)
            return carry
        return one

    @pl.when(serving)
    def _():
        lax.fori_loop(near, far, over(q_spread), 0)

    state[...] = jnp.zeros_like(state)
    for e in range(spans - 1, 0, -1):
        @pl.when(e <= seq)
        def _():
            for part in state_to(e):
                part.wait_recv()
            state[...] = came[e].astype(jnp.float32) + came_decay[e, 0:1] * state[...]

    def enter(i, carry):
        entering[i] = state[...].astype(jnp.bfloat16)
        state[...] = decays[i, 0:1] * state[...] + fresh[i]
        return carry

    lax.fori_loop(0, length // STRETCH, enter, 0)

    block = 2 * rows
    pairs = n // 2

    def chip_at(i):
        m = lax.rem(i, pairs)
        first = i < pairs
        return jnp.where(first, 2 * m + m % 2, 2 * m + 1 - m % 2)

    def rows_of(chip):
        return pl.ds(pl.multiple_of(chip * block, block), block)

    def sq_copy(chip):
        return copy(sq.at[0, chip], sq.at[1, chip], esend.at[chip], erecv.at[chip], sib)

    def gate_block(i, carry):
        chip = chip_at(i)
        at = rows_of(chip)
        maps = c_maps[at, :]
        carried = [
            dot16(maps[u * STRETCH : (u + 1) * STRETCH], entering[chip * per_chip + u])
            for u in range(per_chip)
        ]
        carried = jnp.concatenate(carried, axis=0) * widen(entries[at, :], heads, head_dim)
        gated = (y[at, :] + carried) * silu(proj[at, conv : conv + inner_own])
        y[at, :] = gated
        sums = jnp.sum(gated * gated, axis=1, keepdims=True)
        sq[0, chip] = jnp.broadcast_to(sums, (block, LANES))
        sq_copy(chip).start()
        return carry

    lax.fori_loop(0, n, gate_block, 0)

    def server_of(chip):
        m = chip // 2
        return 2 * m + 1 - m % 2

    def slot_of(chip):
        return jnp.where(chip == server_of(chip), 1, 0)

    def mixed_far(chip):
        return copy(
            mixed.at[chip], taken.at[slot_of(chip), tp], msend.at[chip], mrecv.at[slot_of(chip), c],
            {"tp": lax.rem(2 * server_of(chip) + k, peers)},
        )

    def mixed_near(slot, src):
        place = taken.at[slot, 2 * src + k]
        return copy(place, place, nsend.at[slot, src], nrecv.at[slot, src], sib)

    mix_line = flat(mixer_gain)

    def mix_block(i, carry):
        chip = chip_at(i)
        at = rows_of(chip)
        sq_copy(chip).wait_recv()
        mean = (sq[0, chip] + sq[1, chip]) / (2 * inner_own)
        factor = lax.rsqrt(mean + EPS)
        wide = jnp.concatenate([factor] * (inner_own // LANES), axis=1)
        done = (y[at, :] * wide * mix_line).astype(jnp.bfloat16)

        @pl.when(c != server_of(chip))
        def _():
            mixed[chip] = done

            @pl.when(i < pairs)
            def _():
                mixed_far(chip).start()

        @pl.when(c == server_of(chip))
        def _():
            taken[slot_of(chip), tp] = done
            mixed_near(slot_of(chip), c).start()

        return carry

    lax.fori_loop(0, n, mix_block, 0)

    def mates_left(i, carry):
        @pl.when(c != server_of(chip_at(i)))
        def _():
            mixed_far(chip_at(i)).wait_send()

        return carry

    lax.fori_loop(0, pairs, mates_left, 0)

    def servers_next(i, carry):
        @pl.when(c != chip_at(i))
        def _():
            mixed_far(chip_at(i)).start()

        return carry

    lax.fori_loop(pairs, n, servers_next, 0)

    def out_cols(core, q):
        return pl.ds(pl.multiple_of(core * half + q * quarter, LANES), quarter)

    def result_far(q, core):
        return copy(
            results.at[0, q, pl.ds(core * rows, rows)], out.at[:, out_cols(k, q)], osend.at[q, core], orecv.at[k, q],
            {"tp": 2 * mate + core},
        )

    def result_near(q):
        return copy(
            results.at[1, q, pl.ds(pl.multiple_of((1 - k) * rows, rows), rows)], out.at[:, out_cols(k, q)],
            osend.at[q, 2], orecv.at[k, q], sib,
        )

    @pl.when(serving)
    def _():
        for e in range(spans):
            own_half[e].wait()
        near_in.wait_recv()
        lax.fori_loop(near, max(near, far - 2), over(q_forward), 0)

        def collect(slot):
            def relay(m, carry):
                src = lax.rem(c + m, n)
                place = taken.at[slot, 2 * src + k]
                copy(place, place, nsend.at[slot, src], mrecv.at[slot, src], sib).wait_recv()
                mixed_near(slot, src).start()
                return carry

            lax.fori_loop(1, n, relay, 0)

            def from_near(src, carry):
                place = taken.at[slot, 2 * src + 1 - k]
                copy(place, place, nsend.at[slot, src], nrecv.at[slot, src], sib).wait_recv()
                return carry

            lax.fori_loop(0, n, from_near, 0)

        def multiply(slot, q):
            sums = jnp.zeros((block, wq.shape[3]), jnp.float32)
            for j in range(peers):
                sums += jnp.dot(taken[slot, j], wq[j, q], preferred_element_type=jnp.float32)
            return sums.astype(jnp.bfloat16)

        collect(0)

        def for_mate(e, carry):
            q = seq ^ e

            @pl.when(e == 1)
            def _():
                lax.fori_loop(max(near, far - 2), far, over(q_forward), 0)

            def part_in(m, carry):
                j = far_block(m)
                ends = jnp.where(j % 2 == 0, 2 * e >= spans, e % 2 == 1)

                @pl.when((e > 0) & ends)
                def _():
                    part = wq_part(j, q)
                    copy(part, part, wsend.at[0, 0], qrecv.at[j, q], sib).wait_recv()

                return carry

            lax.fori_loop(0, far, part_in, 0)
            results[0, q] = multiply(0, q)
            for core in range(2):
                result_far(q, core).start()
            return carry

        lax.fori_loop(0, spans, for_mate, 0)
        collect(1)

        def for_own(q, carry):
            results[1, q] = multiply(1, q)
            result_near(q).start()
            out[:, out_cols(k, q)] = results[1, q, pl.ds(pl.multiple_of(k * rows, rows), rows)]
            return carry

        lax.fori_loop(0, spans, for_own, 0)

    def finish(core, q):
        place = out.at[:, out_cols(core, q)]
        arrival = copy(place, place, osend.at[q, 0], orecv.at[core, q], sib)

        @pl.when(jnp.logical_not(serving) | (k != core))
        def _():
            arrival.wait_recv()

    for q in range(spans):
        for core in range(2):
            finish(core, q)

    def drain(i, carry):
        j, s = i // ns, i % ns
        to_sib(j, s).wait_send()

        @pl.when(has_right & (j <= c))
        def _():
            to_right(j, s).wait_send()

        @pl.when(has_left & (j >= c))
        def _():
            to_left(j, s).wait_send()

        return carry

    lax.fori_loop(0, n * ns, drain, 0)
    group_out.wait_send()
    taps_out.wait_send()

    @pl.when((tp == last) & (seq < spans - 1))
    def _():
        tail_next.wait_send()

    @pl.when(has_tail & (k == 1))
    def _():
        @pl.when(has_left)
        def _():
            tail_left.wait_send()

        tail_sib.wait_send()

    for m, core in sends:
        @pl.when(c != servers[m])
        def _():
            w_far(m, core).wait_send()

    for e in range(1, spans):
        @pl.when(seq + e < spans)
        def _():
            for part in state_to(e):
                part.wait_send()

    def sums_left(chip, carry):
        sq_copy(chip).wait_send()

        @pl.when((c != chip) & (chip == server_of(chip)))
        def _():
            mixed_far(chip).wait_send()

        return carry

    lax.fori_loop(0, n, sums_left, 0)

    @pl.when(serving)
    def _():
        for e in range(spans):
            w_near[e].wait_send()

        def far_left(m, carry):
            q_drain(m)
            return carry

        lax.fori_loop(0, far, far_left, 0)

        def near_left(src, carry):
            for slot in range(2):
                mixed_near(slot, src).wait_send()
            return carry

        lax.fori_loop(0, n, near_left, 0)

        def results_left(q, carry):
            for core in range(2):
                result_far(q, core).wait_send()
            result_near(q).wait_send()
            return carry

        lax.fori_loop(0, spans, results_left, 0)


def mixer(hidden, gain, inner, group, step, wout, segments, taps_inner, taps_group, bias, rate, skip, mixer_gain, heads, count, n, spans, ns):
    rows, width = hidden.shape
    inner_dev = inner.shape[0] * inner.shape[1] // width
    own = inner_dev // 2
    cols = inner_dev + 3 * LANES
    half = wout.shape[1] // 2
    length = 2 * n * rows
    vmem = pl.BlockSpec(memory_space=pltpu.VMEM)
    anywhere = pl.BlockSpec(memory_space=pl.ANY)
    scalars = pl.BlockSpec(memory_space=pltpu.SMEM)
    dma = pltpu.SemaphoreType.DMA
    bits = max(1, spans.bit_length() - 1)
    bf16, f32 = jnp.bfloat16, jnp.float32
    return pl.pallas_call(
        functools.partial(mixer_kernel, n, spans, ns, heads, count),
        out_shape=jax.ShapeDtypeStruct(hidden.shape, bf16),
        in_specs=[vmem, vmem, anywhere, anywhere, vmem, anywhere] + [vmem] * 3 + [scalars] * 3 + [vmem],
        out_specs=vmem,
        scratch_shapes=[
            pltpu.VMEM((n, 2, ns, rows, width // ns), bf16),
            pltpu.VMEM((16, width), bf16),
            pltpu.VMEM((16, width), bf16),
            pltpu.VMEM(inner.shape, bf16),
            pltpu.VMEM((2,) + group.shape, bf16),
            pltpu.VMEM((2, 8, LANES), f32),
            pltpu.VMEM((8, own + 2 * LANES), f32),
            pltpu.VMEM((width, cols), bf16),
            pltpu.VMEM((length, cols), f32),
            pltpu.VMEM((8, own + 2 * LANES), f32),
            pltpu.VMEM((2 * n, spans, wout.shape[0], half // spans), bf16),
            pltpu.VMEM((length, own), f32),
            pltpu.VMEM((length, LANES), bf16),
            pltpu.VMEM((length, LANES), f32),
            pltpu.VMEM((LANES, own), f32),
            pltpu.VMEM((length // STRETCH, LANES, own), f32),
            pltpu.VMEM((length // STRETCH, 8, own), f32),
            pltpu.VMEM((length // STRETCH, LANES, own), bf16),
            pltpu.VMEM((LANES, own), bf16),
            pltpu.VMEM((8, own), f32),
            pltpu.VMEM((spans, LANES, own), bf16),
            pltpu.VMEM((spans, 8, own), f32),
            pltpu.VMEM((2, n, 2 * rows, LANES), f32),
            pltpu.VMEM((n, 2 * rows, own), bf16),
            pltpu.VMEM((2, 2 * n, 2 * rows, own), bf16),
            pltpu.VMEM((2, spans, 2 * rows, half // spans), bf16),
            dma((n, ns)), dma((n, ns)), dma((n, ns)), dma((n, ns)), dma((n, ns)), dma((n, ns)),
            dma((3,)), dma((1,)), dma((2,)), dma((2,)),
            dma((2 + n // 2, max(2, spans))), dma((2 * n,)), dma((2 * n, spans, bits)), dma((2 * n, spans)), dma((3,)),
            dma((2, spans)), dma((2, spans)), dma((n,)), dma((n,)),
            dma((n,)), dma((2, n)), dma((2, n)), dma((2, n)), dma((spans, 3)), dma((2, spans)),
        ],
        compiler_params=pltpu.CompilerParams(
            collective_id=0, has_side_effects=True, vmem_limit_bytes=60 << 20
        ),
        cost_estimate=pl.CostEstimate(
            flops=24_000_000_000, bytes_accessed=12_000_000, transcendentals=4_000_000
        ),
        name="mixer",
    )(hidden, gain, inner, group, step, wout, segments, taps_inner, taps_group, bias, rate, skip, mixer_gain)


def by_row(weight):
    width, pair, cols = weight.shape
    tiles = cols // LANES
    return weight.reshape(width, pair, tiles, LANES).transpose(0, 2, 1, 3).reshape(-1, LANES)


def body(
    hidden,
    norm_gain,
    inner_weight,
    group_weight,
    step_weight,
    step_bias,
    decay_rate,
    filter_inner,
    filter_group,
    skip_gain,
    mixer_gain,
    output_weight,
    segment_ids,
):
    spans, chips = lax.axis_size("seq"), lax.axis_size("tp") // 2
    summed = mixer(
        hidden, norm_gain.reshape(-1, LANES), by_row(inner_weight), group_weight, step_weight.T, output_weight,
        segment_ids.reshape(-1, STRETCH), filter_inner, filter_group, step_bias, decay_rate, skip_gain,
        mixer_gain.reshape(-1, LANES), step_weight.shape[1], filter_inner.shape[0], chips, spans, 4,
    )
    return (hidden.astype(jnp.float32) + summed.astype(jnp.float32)).astype(jnp.bfloat16)


def solution(mesh):
    in_specs = (
        P(("seq", "tp"), None),
        P(),
        P(None, None, "tp"),
        P(None, "tp"),
        P(None, "tp"),
        P("tp"),
        P("tp"),
        P(None, "tp"),
        P(None, "tp"),
        P("tp"),
        P("tp"),
        P("tp", None),
        P(),
    )
    out_specs = P(("seq", "tp"), None)
    return jax.shard_map(body, mesh=mesh, in_specs=in_specs, out_specs=out_specs, check_vma=False)
```
